32 devices in a mesh: lat: 16 (over z, y, x), rep: 2 (over core).
Axes of the slice: x: 2, y: 2, z: 4, core: 2. Of those that a mesh axis runs over, the one named last changes fastest.
Arguments:
- near_field: bfloat16 [16, 2, 2048, 4096], P(None, None, 'lat'), may hold values from -6 to 6
- assign: int32 [32], replicated, may hold values from 0 to 31, as said below
- ana_v: bfloat16 [16, 2112, 2048], P('lat', 'rep'), may hold values from -0.125 to 0.125
- ana_w: bfloat16 [16, 2112, 2048], P('lat', 'rep'), may hold values from -0.125 to 0.125
- syn_v: bfloat16 [16, 2112, 32], P('lat', 'rep'), may hold values from -0.1875 to 0.1875
- syn_w: bfloat16 [16, 2112, 32], P('lat', 'rep'), may hold values from -0.1875 to 0.1875
Outputs:
- far_field: float32 [16, 2, 32, 8192], P(None, None, 'lat', 'rep')
The draws below stay inside these ranges and needn't reach their ends.
Inputs may be any that keep to these rules, and one draw needn't show every extreme that they name: assign is a permutation; for each pair p, assign at slots 2p and 2p + 1 sums to 31.
All inputs are finite; a program needn't handle non-finite values.
Results may differ from the reference program's by a relative error of at most 0.0062.
Values may be sent and summed in bfloat16 or wider, within the bound.
A program may use at most 128 MiB of HBM per device.

```python
import math
import jax
import jax.numpy as jnp
from jax import lax

NLAT = 2048
NLON = 4096
LMAX = 2048
NLON_OUT = 8192
FIELDS = 16
ORDERS = 32
PAIRS = 16
STRIDE = 64
PACK = 2112
OUTROWS = 32


def draw_assign(key, part):
    key_perm, key_flip = jax.random.split(key)
    pair_count = ORDERS // 2
    lower = jax.random.permutation(key_perm, pair_count).astype(jnp.int32)
    upper = ORDERS - 1 - lower
    flips = jax.random.randint(key_flip, (pair_count,), 0, 2)
    first = jnp.where(flips == 1, lower, upper)
    second = jnp.where(flips == 1, upper, lower)
    return jnp.stack([first, second], axis=1).reshape(ORDERS).astype(jnp.int32)


def shard_levels(own_key, extent, cuts, least, top_value):
    def one(axis_at, parts):
        draws = jax.random.uniform(jax.random.fold_in(jax.random.fold_in(own_key, 6), axis_at), (parts,), jnp.float32, least / len(cuts), top_value / len(cuts))
        return jnp.repeat(jnp.exp(draws), extent[axis_at] // parts).reshape((-1,) + (1,) * (len(extent) - axis_at - 1))

    loudness = one(*cuts[0])
    for cut in cuts[1:]:
        loudness = loudness * one(*cut)
    return loudness


def gaussian(stream_key, dims, scale, reach, pieces=(), kind=jnp.bfloat16):
    gain = shard_levels(stream_key, dims, pieces, -0.22, 0.18) if pieces else 1.0
    array = jax.random.normal(stream_key, dims, jnp.float32) * scale * gain
    return jnp.minimum(jnp.maximum(array, -reach), reach).astype(kind)


def setup_inputs(seed: int = 0) -> dict:
    splits = jax.random.split(jax.random.key(seed), 7)
    return {
        "near_field": gaussian(splits[0], (FIELDS, 2, NLAT, NLON), 1.0, 6.0, ((2, 16),)),
        "assign": draw_assign(jax.random.fold_in(splits[6], 71), 0),
        "ana_v": gaussian(splits[2], (PAIRS, PACK, NLAT), NLAT ** -0.5, 0.125, ((0, 16), (1, 2))),
        "ana_w": gaussian(splits[3], (PAIRS, PACK, NLAT), NLAT ** -0.5, 0.125, ((0, 16), (1, 2))),
        "syn_v": gaussian(splits[4], (PAIRS, PACK, OUTROWS), (LMAX // 2) ** -0.5, 0.1875, ((0, 16), (1, 2))),
        "syn_w": gaussian(splits[5], (PAIRS, PACK, OUTROWS), (LMAX // 2) ** -0.5, 0.1875, ((0, 16), (1, 2))),
    }


def forward_table(orders, length):
    column = jnp.arange(length, dtype=jnp.int32)
    phase_index = orders[:, None] * column[None, :] % length
    angles = phase_index.astype(jnp.float32) * (2.0 * math.pi / length)
    factor = 1.0 / math.sqrt(length)
    stacked = jnp.stack([jnp.cos(angles) * factor, -jnp.sin(angles) * factor], axis=1)
    return stacked.reshape(2 * orders.shape[0], length).astype(jnp.bfloat16)

def inverse_table(orders, begin, count, length):
    column = begin + jnp.arange(count, dtype=jnp.int32)
    phase_index = orders[:, None] * column[None, :] % length
    angles = phase_index.astype(jnp.float32) * (2.0 * math.pi / length)
    weight = jnp.where(orders == 0, 1.0, 2.0).astype(jnp.float32)[:, None] / math.sqrt(orders.shape[0])
    stacked = jnp.stack([weight * jnp.cos(angles), -weight * jnp.sin(angles)], axis=1)
    return stacked.reshape(2 * orders.shape[0], count).astype(jnp.bfloat16)

def legendre(spectra, mat_av, mat_aw, mat_sv, mat_sw, packed, first_order, second_order):
    count = spectra.shape[1]
    flat = spectra.reshape(8 * count, spectra.shape[3])
    along_v = jnp.dot(mat_av, flat.T, preferred_element_type=jnp.float32).reshape(-1, 2, 2, count, 2)
    along_w = jnp.dot(mat_aw, flat.T, preferred_element_type=jnp.float32).reshape(-1, 2, 2, count, 2)
    border = LMAX - first_order
    second = packed >= border
    degree = jnp.where(second, second_order + packed - border, first_order + packed)
    chosen_v = jnp.where(second[:, None, None, None], along_v[:, 1], along_v[:, 0])
    chosen_w = jnp.where(second[:, None, None, None], along_w[:, 1], along_w[:, 0])
    sph_re = chosen_v[:, 0, :, 0] + chosen_w[:, 1, :, 1]
    sph_im = chosen_v[:, 1, :, 0] - chosen_w[:, 0, :, 1]
    tor_re = chosen_w[:, 1, :, 0] - chosen_v[:, 0, :, 1]
    tor_im = -chosen_w[:, 0, :, 0] - chosen_v[:, 1, :, 1]
    quarter = (degree + 1) % 4
    cosine = jnp.where(quarter == 0, 1.0, jnp.where(quarter == 2, -1.0, 0.0)).astype(jnp.float32)[:, None]
    sine = jnp.where(quarter == 1, -1.0, jnp.where(quarter == 3, 1.0, 0.0)).astype(jnp.float32)[:, None]
    coeffs = jnp.stack([cosine * sph_re - sine * sph_im, cosine * sph_im + sine * sph_re, cosine * tor_re - sine * tor_im, cosine * tor_im + sine * tor_re], axis=1).astype(jnp.bfloat16)
    in_second = second.astype(jnp.bfloat16)[:, None, None]
    masked = jnp.stack([coeffs * (1 - in_second), coeffs * in_second], axis=1).reshape(coeffs.shape[0], 8 * count)
    synth_v = jnp.dot(masked.T, mat_sv, preferred_element_type=jnp.float32).reshape(2, 4, count, -1)
    synth_w = jnp.dot(masked.T, mat_sw, preferred_element_type=jnp.float32).reshape(2, 4, count, -1)
    theta_re = synth_v[:, 0] - synth_w[:, 3]
    theta_im = synth_v[:, 1] + synth_w[:, 2]
    phi_re = -synth_w[:, 1] - synth_v[:, 2]
    phi_im = synth_w[:, 0] - synth_v[:, 3]
    real_part = jnp.stack([theta_re, phi_re], axis=2)
    imag_part = jnp.stack([theta_im, phi_im], axis=2)
    return jnp.stack([real_part, imag_part], axis=1).reshape(4, count, 2, -1)

def reference(near_field, assign, ana_v, ana_w, syn_v, syn_w):
    orders = STRIDE * assign
    table = forward_table(orders, NLON)
    flat_field = near_field.reshape(FIELDS * 2 * NLAT, NLON)
    spectrum = jnp.dot(flat_field, table.T, preferred_element_type=jnp.float32).astype(jnp.bfloat16)
    spectrum = spectrum.reshape(FIELDS, 2, NLAT, 2 * ORDERS).transpose(3, 0, 1, 2)
    slots = spectrum.reshape(PAIRS, 4, FIELDS, 2, NLAT)
    packed = jnp.arange(PACK, dtype=jnp.int32)
    pair_orders = orders.reshape(PAIRS, 2)

    def per_pair(inputs_now):
        spectra, mat_av, mat_aw, mat_sv, mat_sw, first_order, second_order = inputs_now
        return legendre(spectra, mat_av, mat_aw, mat_sv, mat_sw, packed, first_order, second_order)
    order_rows = lax.map(per_pair, (slots, ana_v, ana_w, syn_v, syn_w, pair_orders[:, 0], pair_orders[:, 1]))
    order_rows = order_rows.reshape(2 * ORDERS, FIELDS * 2 * OUTROWS).astype(jnp.bfloat16)
    inverse = inverse_table(orders, 0, NLON_OUT, NLON_OUT)
    far_field = jnp.dot(order_rows.T, inverse, preferred_element_type=jnp.float32)
    return far_field.reshape(FIELDS, 2, OUTROWS, NLON_OUT)
```

```python
import functools
import math

import jax
import jax.numpy as jnp
from jax import lax
from jax.experimental import pallas as pl
from jax.experimental.pallas import tpu as pltpu
from jax.sharding import PartitionSpec as P

LMAX = 2048
NLON_OUT = 8192


def forward_table(orders, length):
    column = jnp.arange(length, dtype=jnp.int32)
    phase_index = orders[:, None] * column[None, :] % length
    angles = phase_index.astype(jnp.float32) * (2.0 * math.pi / length)
    factor = 1.0 / math.sqrt(length)
    stacked = jnp.stack([jnp.cos(angles) * factor, -jnp.sin(angles) * factor], axis=1)
    return stacked.reshape(2 * orders.shape[0], length).astype(jnp.bfloat16)


def inverse_table(orders, begin, count, length):
    column = begin + jnp.arange(count, dtype=jnp.int32)
    phase_index = orders[:, None] * column[None, :] % length
    angles = phase_index.astype(jnp.float32) * (2.0 * math.pi / length)
    weight = jnp.where(orders == 0, 1.0, 2.0).astype(jnp.float32)[:, None] / math.sqrt(
        orders.shape[0]
    )
    stacked = jnp.stack([weight * jnp.cos(angles), -weight * jnp.sin(angles)], axis=1)
    return stacked.reshape(2 * orders.shape[0], count).astype(jnp.bfloat16)


def pad_rows(matrix, tile_count, tile_rows):
    missing = tile_count * tile_rows - matrix.shape[0]
    return jnp.pad(matrix, ((0, missing), (0, 0))).reshape(tile_count, tile_rows, matrix.shape[1])


def legendre(spectra, mat_av, mat_aw, mat_sv, mat_sw, packed_start, first_order, second_order):
    count = spectra.shape[1]
    flat = spectra.reshape(2, 4 * count, spectra.shape[3])
    tile_rows = 128
    tile_count = -(-mat_av.shape[0] // tile_rows)
    out_rows = mat_sv.shape[1]
    border = LMAX - first_order

    def step(carry, inputs_now):
        total_v, total_w = carry
        number, tile_av, tile_aw, tile_sv, tile_sw = inputs_now
        first_row = packed_start + number * tile_rows
        packed = first_row + jnp.arange(tile_rows, dtype=jnp.int32)
        second = packed >= border
        branch_kind = jnp.where(
            first_row >= border, 1, jnp.where(first_row + tile_rows - 1 < border, 0, 2)
        )

        def single_slot(slot):

            def compute():
                slot_flat = flat[slot]
                part_v = jnp.dot(tile_av, slot_flat.T, preferred_element_type=jnp.float32).reshape(
                    tile_rows, 2, count, 2
                )
                part_w = jnp.dot(tile_aw, slot_flat.T, preferred_element_type=jnp.float32).reshape(
                    tile_rows, 2, count, 2
                )
                return (part_v, part_w)

            return compute

        def both_slots():
            first_v, first_w = single_slot(0)()
            second_v, second_w = single_slot(1)()
            choose_second = second[:, None, None, None]
            return (
                jnp.where(choose_second, second_v, first_v),
                jnp.where(choose_second, second_w, first_w),
            )

        chosen_v, chosen_w = lax.switch(branch_kind, [single_slot(0), single_slot(1), both_slots])
        degree = jnp.where(second, second_order + packed - border, first_order + packed)
        sph_re = chosen_v[:, 0, :, 0] + chosen_w[:, 1, :, 1]
        sph_im = chosen_v[:, 1, :, 0] - chosen_w[:, 0, :, 1]
        tor_re = chosen_w[:, 1, :, 0] - chosen_v[:, 0, :, 1]
        tor_im = -chosen_w[:, 0, :, 0] - chosen_v[:, 1, :, 1]
        quarter = (degree + 1) % 4
        cosine = jnp.where(quarter == 0, 1.0, jnp.where(quarter == 2, -1.0, 0.0)).astype(
            jnp.float32
        )[:, None]
        sine = jnp.where(quarter == 1, -1.0, jnp.where(quarter == 3, 1.0, 0.0)).astype(jnp.float32)[
            :, None
        ]
        coeffs = jnp.stack(
            [
                cosine * sph_re - sine * sph_im,
                cosine * sph_im + sine * sph_re,
                cosine * tor_re - sine * tor_im,
                cosine * tor_im + sine * tor_re,
            ],
            axis=1,
        ).astype(jnp.bfloat16)
        flat_coeffs = coeffs.reshape(tile_rows, 4 * count)
        second_mask = second.astype(jnp.bfloat16)[:, None]

        def mixed_rows():
            lower_c = flat_coeffs * (1 - second_mask)
            upper_c = flat_coeffs * second_mask
            add_v = jnp.stack(
                [
                    jnp.dot(lower_c.T, tile_sv, preferred_element_type=jnp.float32),
                    jnp.dot(upper_c.T, tile_sv, preferred_element_type=jnp.float32),
                ]
            )
            add_w = jnp.stack(
                [
                    jnp.dot(lower_c.T, tile_sw, preferred_element_type=jnp.float32),
                    jnp.dot(upper_c.T, tile_sw, preferred_element_type=jnp.float32),
                ]
            )
            return (add_v, add_w)

        def single_rows():
            part_v = jnp.dot(flat_coeffs.T, tile_sv, preferred_element_type=jnp.float32)
            part_w = jnp.dot(flat_coeffs.T, tile_sw, preferred_element_type=jnp.float32)
            upper_pick = (branch_kind == 1).astype(jnp.float32)
            return (
                jnp.stack([part_v * (1.0 - upper_pick), part_v * upper_pick]),
                jnp.stack([part_w * (1.0 - upper_pick), part_w * upper_pick]),
            )

        add_v, add_w = lax.cond(branch_kind == 2, mixed_rows, single_rows)
        return ((total_v + add_v, total_w + add_w), None)

    start_v = jnp.zeros((2, 4 * count, out_rows), jnp.float32)
    start_w = jnp.zeros((2, 4 * count, out_rows), jnp.float32)
    numbers = jnp.arange(tile_count, dtype=jnp.int32)
    (total_v, total_w), unused = lax.scan(
        step,
        (start_v, start_w),
        (
            numbers,
            pad_rows(mat_av, tile_count, tile_rows),
            pad_rows(mat_aw, tile_count, tile_rows),
            pad_rows(mat_sv, tile_count, tile_rows),
            pad_rows(mat_sw, tile_count, tile_rows),
        ),
    )
    synth_v = total_v.reshape(2, 4, count, -1)
    synth_w = total_w.reshape(2, 4, count, -1)
    theta_re = synth_v[:, 0] - synth_w[:, 3]
    theta_im = synth_v[:, 1] + synth_w[:, 2]
    phi_re = -synth_w[:, 1] - synth_v[:, 2]
    phi_im = synth_w[:, 0] - synth_v[:, 3]
    real_part = jnp.stack([theta_re, phi_re], axis=2)
    imag_part = jnp.stack([theta_im, phi_im], axis=2)
    return jnp.stack([real_part, imag_part], axis=1).reshape(4, count, 2, -1)


def plain_body(near_field, assign, ana_v, ana_w, syn_v, syn_w):
    order_count = assign.shape[0]
    spacing = LMAX // order_count
    orders = spacing * assign
    pair_orders = lax.dynamic_slice_in_dim(orders, 2 * lax.axis_index("lat"), 2, 0)
    half_pack = ana_v.shape[1]
    packed_start = lax.axis_index("rep") * half_pack
    table = forward_table(orders, near_field.shape[3])
    spectrum = jnp.einsum(
        "jk,fctk->jfct", table, near_field, preferred_element_type=jnp.float32
    ).astype(jnp.bfloat16)
    partial_value = legendre(
        lax.all_to_all(spectrum, "lat", split_axis=0, concat_axis=3, tiled=True),
        ana_v[0],
        ana_w[0],
        syn_v[0],
        syn_w[0],
        packed_start,
        pair_orders[0],
        pair_orders[1],
    )
    summed = lax.psum(partial_value, "rep").astype(jnp.bfloat16)
    regrouped = lax.all_to_all(summed, "lat", split_axis=3, concat_axis=0, tiled=True)
    longitudes = NLON_OUT // lax.axis_size("rep")
    inverse = inverse_table(orders, lax.axis_index("rep") * longitudes, longitudes, NLON_OUT)
    return jnp.einsum("jfcr,jp->fcrp", regrouped, inverse, preferred_element_type=jnp.float32)

MESH = pl.DeviceIdType.MESH
GROUP = 4
NT = (((1,), (1,)), ((), ()))
TN = (((0,), (0,)), ((), ()))


def kernel(
    lats,
    spacing,
    assign_hbm,
    field_hbm,
    av_hbm,
    aw_hbm,
    sv_hbm,
    sw_hbm,
    out_ref,
    assign_ref,
    table_ref,
    inverse_ref,
    ring,
    ana,
    syn,
    mix,
    staged,
    packet,
    spec,
    total,
    coeffs,
    rows_out,
    rows_in,
    rows_sum,
    field_sem,
    load_sem,
    send_sem,
    recv_sem,
    pass_send,
    pass_recv,
    row_send,
    row_recv,
):
    lat = lax.axis_index("lat")
    rep = lax.axis_index("rep")
    other = 1 - rep
    fields = field_hbm.shape[0]
    groups = fields // GROUP
    half_pack = ana.shape[1]
    span = 4 * GROUP
    near = lats // 2
    side = lat // near
    spot = lax.rem(lat, near)
    width = near * 128

    def fetch(f):
        return pltpu.make_async_copy(field_hbm.at[f, rep], ring.at[f], field_sem.at[f])

    loads = [
        pltpu.make_async_copy(assign_hbm, assign_ref, load_sem.at[0]),
        pltpu.make_async_copy(sv_hbm.at[0], syn.at[0], load_sem.at[1]),
        pltpu.make_async_copy(sw_hbm.at[0], syn.at[1], load_sem.at[2]),
        pltpu.make_async_copy(av_hbm.at[0], ana.at[0], load_sem.at[3]),
        pltpu.make_async_copy(aw_hbm.at[0], ana.at[1], load_sem.at[4]),
    ]
    loads[0].start()
    for f in range(fields):
        fetch(f).start()
    for load in loads[1:]:
        load.start()

    barrier = pltpu.get_barrier_semaphore()

    def greet(i, carry):
        peer = lax.rem(lat + i, lats)
        pl.semaphore_signal(barrier, inc=1, device_id=(peer, rep), device_id_type=MESH)
        pl.semaphore_signal(barrier, inc=1, device_id=(peer, other), device_id_type=MESH)
        return carry

    pl.semaphore_signal(barrier, inc=1, device_id=(lat, other), device_id_type=MESH)
    lax.fori_loop(1, lats, greet, 0)

    loads[0].wait()
    length = field_hbm.shape[3]

    def orders_of(index):
        order = jnp.zeros(index.shape, jnp.int32)
        for k in range(2 * lats):
            order = jnp.where(index == k, spacing * assign_ref[k], order)
        return order

    shape = (4 * lats, 128)
    row = lax.broadcasted_iota(jnp.int32, shape, 0)
    phase = orders_of((row // 4) * 2 + (row & 1)) * lax.broadcasted_iota(jnp.int32, shape, 1)
    phase = lax.rem(phase + ((row // 2) & 1) * (length // 4), length)
    wave = jnp.cos(phase.astype(jnp.float32) * (2.0 * math.pi / length)) * (1.0 / math.sqrt(length))
    wave = wave.astype(jnp.bfloat16)
    table_ref[:, 0:128] = wave
    table_ref[:, 128:256] = wave

    def send(group, peer, far):
        return pltpu.make_async_remote_copy(
            src_ref=packet.at[pl.ds(pl.multiple_of((group * lats + peer) * span, span), span)],
            dst_ref=spec.at[
                far,
                pl.ds(pl.multiple_of((rep * groups + group) * span, span), span),
                pl.ds(pl.multiple_of(spot * 128, 128), 128),
            ],
            send_sem=send_sem,
            recv_sem=recv_sem.at[1 if group == groups - 1 else 0, far],
            device_id=(peer, rep),
            device_id_type=MESH,
        )

    def bulk(rows, send_at, recv_at):
        return pltpu.make_async_remote_copy(
            src_ref=packet.at[pl.ds(0, rows)],
            dst_ref=packet.at[pl.ds(0, rows)],
            send_sem=send_at,
            recv_sem=recv_at,
            device_id=(lat, other),
            device_id_type=MESH,
        )

    def arrived(last, far):
        blocks = (1 if last else groups - 1) * (near if far else near - 1)
        bulk(blocks * span, send_sem, recv_sem.at[last, far]).wait_recv()

    def hand(core, last, far):
        begin, count = (groups - 1, 1) if last else (0, groups - 1)
        block = spec.at[far, pl.ds(pl.multiple_of((core * groups + begin) * span, span), count * span)]
        return pltpu.make_async_remote_copy(
            src_ref=block,
            dst_ref=block,
            send_sem=pass_send.at[last, far],
            recv_sem=pass_recv.at[last, far],
            device_id=(lat, other),
            device_id_type=MESH,
        )

    def fold(f, carry):
        fetch(f).wait()
        total_f = ring[f, :, 0:128].astype(jnp.float32)
        for piece in range(1, ring.shape[2] // 128):
            total_f = total_f + ring[f, :, piece * 128 : (piece + 1) * 128].astype(jnp.float32)
        high = total_f.astype(jnp.bfloat16)
        low = (total_f - high.astype(jnp.float32)).astype(jnp.bfloat16)
        both = jnp.concatenate([high, low], axis=1)
        value = lax.dot_general(table_ref[...], both, NT, preferred_element_type=jnp.float32)
        staged[pl.ds(lax.rem(f, GROUP), 4 * lats, stride=GROUP), :] = value
        return carry

    for group in range(groups):
        lax.fori_loop(group * GROUP, (group + 1) * GROUP, fold, 0)
        packet[group * lats * span : (group + 1) * lats * span, :] = staged[...].astype(jnp.bfloat16)
        if group == 0:
            pl.semaphore_wait(barrier, 2 * lats - 1)

        def send_far(i, carry, group=group):
            send(group, (1 - side) * near + lax.rem(spot + i, near), 1).start()
            return carry

        def send_near(i, carry, group=group):
            send(group, side * near + lax.rem(spot + i, near), 0).start()
            return carry

        lax.fori_loop(0, near, send_far, 0)
        lax.fori_loop(1, near, send_near, 0)
        spec[
            0,
            pl.ds(pl.multiple_of((rep * groups + group) * span, span), span),
            pl.ds(pl.multiple_of(spot * 128, 128), 128),
        ] = packet[pl.ds(pl.multiple_of((group * lats + lat) * span, span), span), :]

    first_order = spacing * assign_ref[2 * lat]
    second_order = spacing * assign_ref[2 * lat + 1]
    border = LMAX - first_order
    loads[1].wait()
    loads[2].wait()
    out_rows = syn.shape[1]
    kinds = 4 * out_rows
    row_at = lax.broadcasted_iota(jnp.int32, (kinds, out_rows), 0)
    col_at = lax.broadcasted_iota(jnp.int32, (kinds, out_rows), 1)
    pick_v = ((row_at == col_at) | (row_at == col_at + out_rows)).astype(jnp.float32).astype(jnp.bfloat16)
    pick_w = (
        ((row_at == col_at + 2 * out_rows) | (row_at == col_at + 3 * out_rows)).astype(jnp.float32).astype(jnp.bfloat16)
    )
    spread = jnp.dot(pick_v, syn[0], preferred_element_type=jnp.float32)
    spread = spread + jnp.dot(pick_w, syn[1], preferred_element_type=jnp.float32)
    packed = rep * half_pack + lax.broadcasted_iota(jnp.int32, (1, half_pack), 1)
    degree = jnp.where(packed >= border, second_order + packed - border, first_order + packed)
    quarter = (degree + 1) & 3
    cosine = jnp.where(quarter == 0, 1.0, jnp.where(quarter == 2, -1.0, 0.0))
    sine = jnp.where(quarter == 1, -1.0, jnp.where(quarter == 3, 1.0, 0.0))
    kind = lax.broadcasted_iota(jnp.int32, (kinds, 1), 0) // out_rows
    factor = jnp.where((kind & 1) == 0, cosine, sine)
    mix[...] = (spread * factor).astype(jnp.bfloat16)

    own_rows = out_rows // lats
    shape = (out_rows, 128)
    row = lax.broadcasted_iota(jnp.int32, shape, 0)
    n = lax.broadcasted_iota(jnp.int32, shape, 1)
    for slot_at in range(2):
        order = orders_of((row // own_rows) * 2 + slot_at)
        weight = jnp.where(order == 0, 1.0, 2.0) * (1.0 / math.sqrt(2 * lats))
        for part_at in range(2):
            phase = lax.rem(order * n + part_at * (NLON_OUT // 4), NLON_OUT)
            wave = weight * jnp.cos(phase.astype(jnp.float32) * (2.0 * math.pi / NLON_OUT))
            begin = (part_at * 2 + slot_at) * out_rows
            for o in range(own_rows):
                inverse_ref[begin : begin + out_rows, o * 128 : (o + 1) * 128] = jnp.where(
                    lax.rem(row, own_rows) == o, wave, 0.0
                ).astype(jnp.bfloat16)

    loads[3].wait()
    loads[4].wait()
    arrived(0, 0)
    hand(rep, 0, 0).start()
    arrived(0, 1)
    hand(rep, 0, 1).start()
    arrived(1, 0)
    hand(rep, 1, 0).start()
    hand(other, 0, 0).wait_recv()
    hand(other, 1, 0).wait_recv()
    columns = pl.ds(pl.multiple_of(side * width, 128), width)
    for k in range(2):
        total[k] = lax.dot_general(ana[k, :, columns], spec[0], NT, preferred_element_type=jnp.float32)
    arrived(1, 1)
    hand(rep, 1, 1).start()
    hand(other, 0, 1).wait_recv()
    hand(other, 1, 1).wait_recv()

    columns = pl.ds(pl.multiple_of((1 - side) * width, 128), width)
    lane = lax.broadcasted_iota(jnp.int32, (1, 128), 1)
    lane_slot = (lane // GROUP) & 1
    at = rep * half_pack + lax.broadcasted_iota(jnp.int32, (half_pack, 1), 0)
    row_slot = jnp.where(at >= border, 1, 0)
    for k in range(2):
        value = total[k] + lax.dot_general(ana[k, :, columns], spec[1], NT, preferred_element_type=jnp.float32)
        coeffs[:, k * 128 : (k + 1) * 128] = jnp.where(row_slot == lane_slot, value, 0.0).astype(jnp.bfloat16)

    part = (lane // (2 * GROUP)) & 1
    comp = lane // 64

    def swap_part(x):
        return jnp.where(part == 0, pltpu.roll(x, 128 - 2 * GROUP, 1), pltpu.roll(x, 2 * GROUP, 1))

    def swap_comp(x):
        return pltpu.roll(x, 64, 1)

    part_sign = jnp.where(part == 0, -1.0, 1.0)
    comp_sign = jnp.where(comp == 0, 1.0, -1.0)
    synth = jnp.dot(mix[...], coeffs[...], preferred_element_type=jnp.float32)
    synth = synth[:, 0:128] - comp_sign * part_sign * swap_comp(swap_part(synth[:, 128:256]))
    cos_v, sin_v, cos_w, sin_w = (synth[k * out_rows : (k + 1) * out_rows] for k in range(4))
    rows = cos_v + part_sign * swap_part(sin_v)
    rows = rows + comp_sign * swap_comp(sin_w) - comp_sign * part_sign * swap_comp(swap_part(cos_w))
    for k in range(lats):
        rows_out[k] = rows[k * own_rows : (k + 1) * own_rows]

    def row_copy(target_lat, target_rep):
        return pltpu.make_async_remote_copy(
            src_ref=rows_out.at[target_lat],
            dst_ref=rows_in.at[rep * lats + lat],
            send_sem=row_send,
            recv_sem=row_recv,
            device_id=(target_lat, target_rep),
            device_id_type=MESH,
        )

    def send_rows(i, carry):
        peer = lax.rem(lat + i, lats)
        row_copy(peer, rep).start()
        row_copy(peer, other).start()
        return carry

    lax.fori_loop(1, lats, send_rows, 0)
    row_copy(lat, other).start()
    rows_in[rep * lats + lat] = rows_out[lat]

    bulk(groups * (lats - 1) * span, send_sem, recv_sem.at[0, 0]).wait_send()
    for last in range(2):
        for far in range(2):
            hand(rep, last, far).wait_send()

    all_rows = pltpu.make_async_remote_copy(
        src_ref=rows_in.at[pl.ds(0, 2 * lats - 1)],
        dst_ref=rows_in.at[pl.ds(0, 2 * lats - 1)],
        send_sem=row_send,
        recv_sem=row_recv,
        device_id=(lat, other),
        device_id_type=MESH,
    )
    all_rows.wait_recv()

    for k in range(lats):
        rows_sum[k * own_rows : (k + 1) * own_rows, :] = rows_in[k] + rows_in[lats + k]
    summed = rows_sum[...]
    gathered = [summed] + [pltpu.roll(summed, 128 - k * GROUP, 1) for k in range(1, 4)]
    gathered = jnp.concatenate(gathered, axis=0).astype(jnp.bfloat16)
    value = lax.dot_general(gathered, inverse_ref[...], TN, preferred_element_type=jnp.float32)
    for block in range(2 * groups):
        comp_at, group = block // groups, block % groups
        for o in range(own_rows):
            begin = (group * GROUP * 2 + comp_at) * own_rows + o
            out_ref[pl.ds(begin, GROUP, stride=2 * own_rows), :] = value[
                block * span : block * span + GROUP, o * 128 : (o + 1) * 128
            ]
    all_rows.wait_send()


def repeat_kernel(small_ref, out_hbm, wide, sem):
    value = small_ref[...]
    width = wide.shape[3]
    for k in range(width // 128):
        wide[:, :, :, k * 128 : (k + 1) * 128] = value
    copies = [
        pltpu.make_async_copy(wide, out_hbm.at[:, :, :, k * width : (k + 1) * width], sem.at[k])
        for k in range(out_hbm.shape[3] // width)
    ]
    for copy in copies:
        copy.start()
    for copy in copies:
        copy.wait()


def fast_body(near_field, assign, ana_v, ana_w, syn_v, syn_w):
    lats = lax.axis_size("lat")
    fields, comps, own_lat, length = near_field.shape
    order_count = assign.shape[0]
    half_pack = ana_v.shape[1]
    out_rows = syn_v.shape[2]
    own_rows = out_rows // lats
    hbm_spec = pl.BlockSpec(memory_space=pltpu.HBM)
    vmem_spec = pl.BlockSpec(memory_space=pltpu.VMEM)
    small = pl.pallas_call(
        functools.partial(kernel, lats, LMAX // order_count),
        out_shape=jax.ShapeDtypeStruct((fields * 2 * own_rows, 128), jnp.float32),
        in_specs=[hbm_spec] * 6,
        out_specs=vmem_spec,
        scratch_shapes=[
            pltpu.SMEM((order_count,), jnp.int32),
            pltpu.VMEM((4 * lats, 256), jnp.bfloat16),
            pltpu.VMEM((4 * out_rows, own_rows * 128), jnp.bfloat16),
            pltpu.VMEM((fields, own_lat, length), jnp.bfloat16),
            pltpu.VMEM((2, half_pack, ana_v.shape[2]), jnp.bfloat16),
            pltpu.VMEM((2, out_rows, half_pack), jnp.bfloat16),
            pltpu.VMEM((4 * out_rows, half_pack), jnp.bfloat16),
            pltpu.VMEM((4 * lats * GROUP, 128), jnp.float32),
            pltpu.VMEM((4 * lats * fields, 128), jnp.bfloat16),
            pltpu.VMEM((2, 8 * fields, lats // 2 * own_lat), jnp.bfloat16),
            pltpu.VMEM((2, half_pack, 128), jnp.float32),
            pltpu.VMEM((half_pack, 256), jnp.bfloat16),
            pltpu.VMEM((lats, own_rows, 128), jnp.float32),
            pltpu.VMEM((2 * lats, own_rows, 128), jnp.float32),
            pltpu.VMEM((lats * own_rows, 128), jnp.float32),
            pltpu.SemaphoreType.DMA((fields,)),
            pltpu.SemaphoreType.DMA((5,)),
            pltpu.SemaphoreType.DMA,
            pltpu.SemaphoreType.DMA((2, 2)),
            pltpu.SemaphoreType.DMA((2, 2)),
            pltpu.SemaphoreType.DMA((2, 2)),
            pltpu.SemaphoreType.DMA,
            pltpu.SemaphoreType.DMA,
        ],
        compiler_params=pltpu.CompilerParams(
            collective_id=0, has_side_effects=True, vmem_limit_bytes=66_000_000
        ),
    )(assign, near_field, ana_v, ana_w, syn_v.swapaxes(1, 2), syn_w.swapaxes(1, 2))
    repeats = NLON_OUT // lax.axis_size("rep") // 128
    spread = 4
    return pl.pallas_call(
        repeat_kernel,
        out_shape=jax.ShapeDtypeStruct((fields, 2, own_rows, repeats * 128), jnp.float32),
        in_specs=[pl.BlockSpec(memory_space=pltpu.VMEM)],
        out_specs=hbm_spec,
        scratch_shapes=[
            pltpu.VMEM((fields, 2, own_rows, repeats // spread * 128), jnp.float32),
            pltpu.SemaphoreType.DMA((spread,)),
        ],
    )(small.reshape(fields, 2, own_rows, 128))


def fits(mesh, near_field, assign, ana_v, syn_v):
    lats = mesh.shape["lat"]
    fields, comps, rows, length = near_field.shape
    spacing = LMAX // assign.shape[0]
    return (
        mesh.shape["rep"] == 2
        and fields == 4 * GROUP
        and lats >= 4
        and comps == 2
        and lats & (lats - 1) == 0
        and rows == 128 * lats
        and assign.shape[0] == 2 * lats
        and 128 * spacing % length == 0
        and 128 * spacing % NLON_OUT == 0
        and syn_v.shape[2] == 32
        and ana_v.shape[1] % 64 == 0
    )


def solution(mesh):
    in_specs = (
        P(None, None, "lat", None),
        P(),
        P("lat", "rep", None),
        P("lat", "rep", None),
        P("lat", "rep", None),
        P("lat", "rep", None),
    )
    out_specs = P(None, None, "lat", "rep")

    def run(near_field, assign, ana_v, ana_w, syn_v, syn_w):
        chosen = fast_body if fits(mesh, near_field, assign, ana_v, syn_v) else plain_body
        mapped = jax.shard_map(chosen, mesh=mesh, in_specs=in_specs, out_specs=out_specs, check_vma=False)
        return mapped(near_field, assign, ana_v, ana_w, syn_v, syn_w)

    return run
```

```python
import functools
import math

import jax
import jax.numpy as jnp
from jax import lax
from jax.experimental import pallas as pl
from jax.experimental.pallas import tpu as pltpu
from jax.sharding import PartitionSpec as P

LMAX = 2048
NLON_OUT = 8192


def forward_table(orders, length):
    column = jnp.arange(length, dtype=jnp.int32)
    phase_index = orders[:, None] * column[None, :] % length
    angles = phase_index.astype(jnp.float32) * (2.0 * math.pi / length)
    factor = 1.0 / math.sqrt(length)
    stacked = jnp.stack([jnp.cos(angles) * factor, -jnp.sin(angles) * factor], axis=1)
    return stacked.reshape(2 * orders.shape[0], length).astype(jnp.bfloat16)


def inverse_table(orders, begin, count, length):
    column = begin + jnp.arange(count, dtype=jnp.int32)
    phase_index = orders[:, None] * column[None, :] % length
    angles = phase_index.astype(jnp.float32) * (2.0 * math.pi / length)
    weight = jnp.where(orders == 0, 1.0, 2.0).astype(jnp.float32)[:, None] / math.sqrt(
        orders.shape[0]
    )
    stacked = jnp.stack([weight * jnp.cos(angles), -weight * jnp.sin(angles)], axis=1)
    return stacked.reshape(2 * orders.shape[0], count).astype(jnp.bfloat16)


def pad_rows(matrix, tile_count, tile_rows):
    missing = tile_count * tile_rows - matrix.shape[0]
    return jnp.pad(matrix, ((0, missing), (0, 0))).reshape(tile_count, tile_rows, matrix.shape[1])


def legendre(spectra, mat_av, mat_aw, mat_sv, mat_sw, packed_start, first_order, second_order):
    count = spectra.shape[1]
    flat = spectra.reshape(2, 4 * count, spectra.shape[3])
    tile_rows = 128
    tile_count = -(-mat_av.shape[0] // tile_rows)
    out_rows = mat_sv.shape[1]
    border = LMAX - first_order

    def step(carry, inputs_now):
        total_v, total_w = carry
        number, tile_av, tile_aw, tile_sv, tile_sw = inputs_now
        first_row = packed_start + number * tile_rows
        packed = first_row + jnp.arange(tile_rows, dtype=jnp.int32)
        second = packed >= border
        branch_kind = jnp.where(
            first_row >= border, 1, jnp.where(first_row + tile_rows - 1 < border, 0, 2)
        )

        def single_slot(slot):

            def compute():
                slot_flat = flat[slot]
                part_v = jnp.dot(tile_av, slot_flat.T, preferred_element_type=jnp.float32).reshape(
                    tile_rows, 2, count, 2
                )
                part_w = jnp.dot(tile_aw, slot_flat.T, preferred_element_type=jnp.float32).reshape(
                    tile_rows, 2, count, 2
                )
                return (part_v, part_w)

            return compute

        def both_slots():
            first_v, first_w = single_slot(0)()
            second_v, second_w = single_slot(1)()
            choose_second = second[:, None, None, None]
            return (
                jnp.where(choose_second, second_v, first_v),
                jnp.where(choose_second, second_w, first_w),
            )

        chosen_v, chosen_w = lax.switch(branch_kind, [single_slot(0), single_slot(1), both_slots])
        degree = jnp.where(second, second_order + packed - border, first_order + packed)
        sph_re = chosen_v[:, 0, :, 0] + chosen_w[:, 1, :, 1]
        sph_im = chosen_v[:, 1, :, 0] - chosen_w[:, 0, :, 1]
        tor_re = chosen_w[:, 1, :, 0] - chosen_v[:, 0, :, 1]
        tor_im = -chosen_w[:, 0, :, 0] - chosen_v[:, 1, :, 1]
        quarter = (degree + 1) % 4
        cosine = jnp.where(quarter == 0, 1.0, jnp.where(quarter == 2, -1.0, 0.0)).astype(
            jnp.float32
        )[:, None]
        sine = jnp.where(quarter == 1, -1.0, jnp.where(quarter == 3, 1.0, 0.0)).astype(jnp.float32)[
            :, None
        ]
        coeffs = jnp.stack(
            [
                cosine * sph_re - sine * sph_im,
                cosine * sph_im + sine * sph_re,
                cosine * tor_re - sine * tor_im,
                cosine * tor_im + sine * tor_re,
            ],
            axis=1,
        ).astype(jnp.bfloat16)
        flat_coeffs = coeffs.reshape(tile_rows, 4 * count)
        second_mask = second.astype(jnp.bfloat16)[:, None]

        def mixed_rows():
            lower_c = flat_coeffs * (1 - second_mask)
            upper_c = flat_coeffs * second_mask
            add_v = jnp.stack(
                [
                    jnp.dot(lower_c.T, tile_sv, preferred_element_type=jnp.float32),
                    jnp.dot(upper_c.T, tile_sv, preferred_element_type=jnp.float32),
                ]
            )
            add_w = jnp.stack(
                [
                    jnp.dot(lower_c.T, tile_sw, preferred_element_type=jnp.float32),
                    jnp.dot(upper_c.T, tile_sw, preferred_element_type=jnp.float32),
                ]
            )
            return (add_v, add_w)

        def single_rows():
            part_v = jnp.dot(flat_coeffs.T, tile_sv, preferred_element_type=jnp.float32)
            part_w = jnp.dot(flat_coeffs.T, tile_sw, preferred_element_type=jnp.float32)
            upper_pick = (branch_kind == 1).astype(jnp.float32)
            return (
                jnp.stack([part_v * (1.0 - upper_pick), part_v * upper_pick]),
                jnp.stack([part_w * (1.0 - upper_pick), part_w * upper_pick]),
            )

        add_v, add_w = lax.cond(branch_kind == 2, mixed_rows, single_rows)
        return ((total_v + add_v, total_w + add_w), None)

    start_v = jnp.zeros((2, 4 * count, out_rows), jnp.float32)
    start_w = jnp.zeros((2, 4 * count, out_rows), jnp.float32)
    numbers = jnp.arange(tile_count, dtype=jnp.int32)
    (total_v, total_w), unused = lax.scan(
        step,
        (start_v, start_w),
        (
            numbers,
            pad_rows(mat_av, tile_count, tile_rows),
            pad_rows(mat_aw, tile_count, tile_rows),
            pad_rows(mat_sv, tile_count, tile_rows),
            pad_rows(mat_sw, tile_count, tile_rows),
        ),
    )
    synth_v = total_v.reshape(2, 4, count, -1)
    synth_w = total_w.reshape(2, 4, count, -1)
    theta_re = synth_v[:, 0] - synth_w[:, 3]
    theta_im = synth_v[:, 1] + synth_w[:, 2]
    phi_re = -synth_w[:, 1] - synth_v[:, 2]
    phi_im = synth_w[:, 0] - synth_v[:, 3]
    real_part = jnp.stack([theta_re, phi_re], axis=2)
    imag_part = jnp.stack([theta_im, phi_im], axis=2)
    return jnp.stack([real_part, imag_part], axis=1).reshape(4, count, 2, -1)


def plain_body(near_field, assign, ana_v, ana_w, syn_v, syn_w):
    order_count = assign.shape[0]
    spacing = LMAX // order_count
    orders = spacing * assign
    pair_orders = lax.dynamic_slice_in_dim(orders, 2 * lax.axis_index("lat"), 2, 0)
    half_pack = ana_v.shape[1]
    packed_start = lax.axis_index("rep") * half_pack
    table = forward_table(orders, near_field.shape[3])
    spectrum = jnp.einsum(
        "jk,fctk->jfct", table, near_field, preferred_element_type=jnp.float32
    ).astype(jnp.bfloat16)
    partial_value = legendre(
        lax.all_to_all(spectrum, "lat", split_axis=0, concat_axis=3, tiled=True),
        ana_v[0],
        ana_w[0],
        syn_v[0],
        syn_w[0],
        packed_start,
        pair_orders[0],
        pair_orders[1],
    )
    summed = lax.psum(partial_value, "rep").astype(jnp.bfloat16)
    regrouped = lax.all_to_all(summed, "lat", split_axis=3, concat_axis=0, tiled=True)
    longitudes = NLON_OUT // lax.axis_size("rep")
    inverse = inverse_table(orders, lax.axis_index("rep") * longitudes, longitudes, NLON_OUT)
    return jnp.einsum("jfcr,jp->fcrp", regrouped, inverse, preferred_element_type=jnp.float32)

MESH = pl.DeviceIdType.MESH
GROUP = 4
NT = (((1,), (1,)), ((), ()))
TN = (((0,), (0,)), ((), ()))


def kernel(
    lats,
    spacing,
    assign_hbm,
    field_hbm,
    av_hbm,
    aw_hbm,
    sv_hbm,
    sw_hbm,
    out_ref,
    assign_ref,
    table_ref,
    inverse_ref,
    ring,
    ana,
    syn,
    mix,
    staged,
    packet,
    spec,
    total,
    coeffs,
    rows_out,
    rows_in,
    rows_sum,
    field_sem,
    load_sem,
    send_sem,
    recv_sem,
    pass_send,
    pass_recv,
    row_send,
    row_recv,
):
    lat = lax.axis_index("lat")
    rep = lax.axis_index("rep")
    other = 1 - rep
    fields = field_hbm.shape[0]
    groups = fields // GROUP
    half_pack = ana.shape[1]
    span = 4 * GROUP
    near = lats // 2
    side = lat // near
    spot = lax.rem(lat, near)
    width = near * 128

    def fetch(f):
        return pltpu.make_async_copy(field_hbm.at[f, rep], ring.at[f], field_sem.at[f])

    loads = [
        pltpu.make_async_copy(assign_hbm, assign_ref, load_sem.at[0]),
        pltpu.make_async_copy(sv_hbm.at[0], syn.at[0], load_sem.at[1]),
        pltpu.make_async_copy(sw_hbm.at[0], syn.at[1], load_sem.at[2]),
        pltpu.make_async_copy(av_hbm.at[0], ana.at[0], load_sem.at[3]),
        pltpu.make_async_copy(aw_hbm.at[0], ana.at[1], load_sem.at[4]),
    ]
    loads[0].start()
    for f in range(fields):
        fetch(f).start()
    for load in loads[1:]:
        load.start()

    barrier = pltpu.get_barrier_semaphore()

    def greet(i, carry):
        peer = lax.rem(lat + i, lats)
        pl.semaphore_signal(barrier, inc=1, device_id=(peer, rep), device_id_type=MESH)
        pl.semaphore_signal(barrier, inc=1, device_id=(peer, other), device_id_type=MESH)
        return carry

    pl.semaphore_signal(barrier, inc=1, device_id=(lat, other), device_id_type=MESH)
    lax.fori_loop(1, lats, greet, 0)

    loads[0].wait()
    length = field_hbm.shape[3]

    def orders_of(index):
        order = jnp.zeros(index.shape, jnp.int32)
        for k in range(2 * lats):
            order = jnp.where(index == k, spacing * assign_ref[k], order)
        return order

    shape = (4 * lats, 128)
    row = lax.broadcasted_iota(jnp.int32, shape, 0)
    phase = orders_of((row // 4) * 2 + (row & 1)) * lax.broadcasted_iota(jnp.int32, shape, 1)
    phase = lax.rem(phase + ((row // 2) & 1) * (length // 4), length)
    wave = jnp.cos(phase.astype(jnp.float32) * (2.0 * math.pi / length)) * (1.0 / math.sqrt(length))
    wave = wave.astype(jnp.bfloat16)
    table_ref[:, 0:128] = wave
    table_ref[:, 128:256] = wave

    def send(group, peer, far):
        return pltpu.make_async_remote_copy(
            src_ref=packet.at[pl.ds(pl.multiple_of((group * lats + peer) * span, span), span)],
            dst_ref=spec.at[
                far,
                pl.ds(pl.multiple_of((rep * groups + group) * span, span), span),
                pl.ds(pl.multiple_of(spot * 128, 128), 128),
            ],
            send_sem=send_sem,
            recv_sem=recv_sem.at[1 if group == groups - 1 else 0, far],
            device_id=(peer, rep),
            device_id_type=MESH,
        )

    def bulk(rows, send_at, recv_at):
        return pltpu.make_async_remote_copy(
            src_ref=packet.at[pl.ds(0, rows)],
            dst_ref=packet.at[pl.ds(0, rows)],
            send_sem=send_at,
            recv_sem=recv_at,
            device_id=(lat, other),
            device_id_type=MESH,
        )

    def arrived(last, far):
        blocks = (1 if last else groups - 1) * (near if far else near - 1)
        bulk(blocks * span, send_sem, recv_sem.at[last, far]).wait_recv()

    def hand(core, last, far):
        begin, count = (groups - 1, 1) if last else (0, groups - 1)
        block = spec.at[far, pl.ds(pl.multiple_of((core * groups + begin) * span, span), count * span)]
        return pltpu.make_async_remote_copy(
            src_ref=block,
            dst_ref=block,
            send_sem=pass_send.at[last, far],
            recv_sem=pass_recv.at[last, far],
            device_id=(lat, other),
            device_id_type=MESH,
        )

    def fold(f, carry):
        fetch(f).wait()
        total_f = ring[f, :, 0:128].astype(jnp.float32)
        for piece in range(1, ring.shape[2] // 128):
            total_f = total_f + ring[f, :, piece * 128 : (piece + 1) * 128].astype(jnp.float32)
        high = total_f.astype(jnp.bfloat16)
        low = (total_f - high.astype(jnp.float32)).astype(jnp.bfloat16)
        both = jnp.concatenate([high, low], axis=1)
        value = lax.dot_general(table_ref[...], both, NT, preferred_element_type=jnp.float32)
        staged[pl.ds(lax.rem(f, GROUP), 4 * lats, stride=GROUP), :] = value
        return carry

    for group in range(groups):
        lax.fori_loop(group * GROUP, (group + 1) * GROUP, fold, 0)
        packet[group * lats * span : (group + 1) * lats * span, :] = staged[...].astype(jnp.bfloat16)
        if group == 0:
            pl.semaphore_wait(barrier, 2 * lats - 1)

        def send_far(i, carry, group=group):
            send(group, (1 - side) * near + lax.rem(spot + i, near), 1).start()
            return carry

        def send_near(i, carry, group=group):
            send(group, side * near + lax.rem(spot + i, near), 0).start()
            return carry

        lax.fori_loop(0, near, send_far, 0)
        lax.fori_loop(1, near, send_near, 0)
        spec[
            0,
            pl.ds(pl.multiple_of((rep * groups + group) * span, span), span),
            pl.ds(pl.multiple_of(spot * 128, 128), 128),
        ] = packet[pl.ds(pl.multiple_of((group * lats + lat) * span, span), span), :]

    first_order = spacing * assign_ref[2 * lat]
    second_order = spacing * assign_ref[2 * lat + 1]
    border = LMAX - first_order
    loads[1].wait()
    loads[2].wait()
    out_rows = syn.shape[1]
    kinds = 4 * out_rows
    row_at = lax.broadcasted_iota(jnp.int32, (kinds, out_rows), 0)
    col_at = lax.broadcasted_iota(jnp.int32, (kinds, out_rows), 1)
    pick_v = ((row_at == col_at) | (row_at == col_at + out_rows)).astype(jnp.float32).astype(jnp.bfloat16)
    pick_w = (
        ((row_at == col_at + 2 * out_rows) | (row_at == col_at + 3 * out_rows)).astype(jnp.float32).astype(jnp.bfloat16)
    )
    spread = jnp.dot(pick_v, syn[0], preferred_element_type=jnp.float32)
    spread = spread + jnp.dot(pick_w, syn[1], preferred_element_type=jnp.float32)
    packed = rep * half_pack + lax.broadcasted_iota(jnp.int32, (1, half_pack), 1)
    degree = jnp.where(packed >= border, second_order + packed - border, first_order + packed)
    quarter = (degree + 1) & 3
    cosine = jnp.where(quarter == 0, 1.0, jnp.where(quarter == 2, -1.0, 0.0))
    sine = jnp.where(quarter == 1, -1.0, jnp.where(quarter == 3, 1.0, 0.0))
    kind = lax.broadcasted_iota(jnp.int32, (kinds, 1), 0) // out_rows
    factor = jnp.where((kind & 1) == 0, cosine, sine)
    mix[...] = (spread * factor).astype(jnp.bfloat16)

    own_rows = out_rows // lats
    shape = (out_rows, 128)
    row = lax.broadcasted_iota(jnp.int32, shape, 0)
    n = lax.broadcasted_iota(jnp.int32, shape, 1)
    for slot_at in range(2):
        order = orders_of((row // own_rows) * 2 + slot_at)
        weight = jnp.where(order == 0, 1.0, 2.0) * (1.0 / math.sqrt(2 * lats))
        for part_at in range(2):
            phase = lax.rem(order * n + part_at * (NLON_OUT // 4), NLON_OUT)
            wave = weight * jnp.cos(phase.astype(jnp.float32) * (2.0 * math.pi / NLON_OUT))
            begin = (part_at * 2 + slot_at) * out_rows
            for o in range(own_rows):
                inverse_ref[begin : begin + out_rows, o * 128 : (o + 1) * 128] = jnp.where(
                    lax.rem(row, own_rows) == o, wave, 0.0
                ).astype(jnp.bfloat16)

    loads[3].wait()
    loads[4].wait()
    arrived(0, 0)
    hand(rep, 0, 0).start()
    arrived(0, 1)
    hand(rep, 0, 1).start()
    arrived(1, 0)
    hand(rep, 1, 0).start()
    arrived(1, 1)
    hand(rep, 1, 1).start()
    hand(other, 0, 0).wait_recv()
    hand(other, 1, 0).wait_recv()
    columns = pl.ds(pl.multiple_of(side * width, 128), width)
    for k in range(2):
        total[k] = lax.dot_general(ana[k, :, columns], spec[0], NT, preferred_element_type=jnp.float32)
    hand(other, 0, 1).wait_recv()
    hand(other, 1, 1).wait_recv()

    columns = pl.ds(pl.multiple_of((1 - side) * width, 128), width)
    lane = lax.broadcasted_iota(jnp.int32, (1, 128), 1)
    lane_slot = (lane // GROUP) & 1
    at = rep * half_pack + lax.broadcasted_iota(jnp.int32, (half_pack, 1), 0)
    row_slot = jnp.where(at >= border, 1, 0)
    for k in range(2):
        value = total[k] + lax.dot_general(ana[k, :, columns], spec[1], NT, preferred_element_type=jnp.float32)
        coeffs[:, k * 128 : (k + 1) * 128] = jnp.where(row_slot == lane_slot, value, 0.0).astype(jnp.bfloat16)

    part = (lane // (2 * GROUP)) & 1
    comp = lane // 64

    def swap_part(x):
        return jnp.where(part == 0, pltpu.roll(x, 128 - 2 * GROUP, 1), pltpu.roll(x, 2 * GROUP, 1))

    def swap_comp(x):
        return pltpu.roll(x, 64, 1)

    part_sign = jnp.where(part == 0, -1.0, 1.0)
    comp_sign = jnp.where(comp == 0, 1.0, -1.0)
    synth = jnp.dot(mix[...], coeffs[...], preferred_element_type=jnp.float32)
    synth = synth[:, 0:128] - comp_sign * part_sign * swap_comp(swap_part(synth[:, 128:256]))
    cos_v, sin_v, cos_w, sin_w = (synth[k * out_rows : (k + 1) * out_rows] for k in range(4))
    rows = cos_v + part_sign * swap_part(sin_v)
    rows = rows + comp_sign * swap_comp(sin_w) - comp_sign * part_sign * swap_comp(swap_part(cos_w))
    for k in range(lats):
        rows_out[k] = rows[k * own_rows : (k + 1) * own_rows]

    def row_copy(target_lat, target_rep):
        return pltpu.make_async_remote_copy(
            src_ref=rows_out.at[target_lat],
            dst_ref=rows_in.at[rep * lats + lat],
            send_sem=row_send,
            recv_sem=row_recv,
            device_id=(target_lat, target_rep),
            device_id_type=MESH,
        )

    def send_rows(i, carry):
        peer = lax.rem(lat + i, lats)
        row_copy(peer, rep).start()
        row_copy(peer, other).start()
        return carry

    lax.fori_loop(1, lats, send_rows, 0)
    row_copy(lat, other).start()
    rows_in[rep * lats + lat] = rows_out[lat]

    bulk(groups * (lats - 1) * span, send_sem, recv_sem.at[0, 0]).wait_send()
    for last in range(2):
        for far in range(2):
            hand(rep, last, far).wait_send()

    all_rows = pltpu.make_async_remote_copy(
        src_ref=rows_in.at[pl.ds(0, 2 * lats - 1)],
        dst_ref=rows_in.at[pl.ds(0, 2 * lats - 1)],
        send_sem=row_send,
        recv_sem=row_recv,
        device_id=(lat, other),
        device_id_type=MESH,
    )
    all_rows.wait_recv()

    for k in range(lats):
        rows_sum[k * own_rows : (k + 1) * own_rows, :] = rows_in[k] + rows_in[lats + k]
    summed = rows_sum[...]
    gathered = [summed] + [pltpu.roll(summed, 128 - k * GROUP, 1) for k in range(1, 4)]
    gathered = jnp.concatenate(gathered, axis=0).astype(jnp.bfloat16)
    value = lax.dot_general(gathered, inverse_ref[...], TN, preferred_element_type=jnp.float32)
    for block in range(2 * groups):
        comp_at, group = block // groups, block % groups
        for o in range(own_rows):
            begin = (group * GROUP * 2 + comp_at) * own_rows + o
            out_ref[pl.ds(begin, GROUP, stride=2 * own_rows), :] = value[
                block * span : block * span + GROUP, o * 128 : (o + 1) * 128
            ]
    all_rows.wait_send()


def repeat_kernel(small_ref, out_hbm, wide, sem):
    value = small_ref[...]
    width = wide.shape[3]
    for k in range(width // 128):
        wide[:, :, :, k * 128 : (k + 1) * 128] = value
    copies = [
        pltpu.make_async_copy(wide, out_hbm.at[:, :, :, k * width : (k + 1) * width], sem.at[k])
        for k in range(out_hbm.shape[3] // width)
    ]
    for copy in copies:
        copy.start()
    for copy in copies:
        copy.wait()


def fast_body(near_field, assign, ana_v, ana_w, syn_v, syn_w):
    lats = lax.axis_size("lat")
    fields, comps, own_lat, length = near_field.shape
    order_count = assign.shape[0]
    half_pack = ana_v.shape[1]
    out_rows = syn_v.shape[2]
    own_rows = out_rows // lats
    hbm_spec = pl.BlockSpec(memory_space=pltpu.HBM)
    vmem_spec = pl.BlockSpec(memory_space=pltpu.VMEM)
    inputs = (assign, near_field, ana_v, ana_w, syn_v.swapaxes(1, 2), syn_w.swapaxes(1, 2))
    small = pl.pallas_call(
        functools.partial(kernel, lats, LMAX // order_count),
        out_shape=pltpu.VMEM((fields * 2 * own_rows, 128), jnp.float32),
        in_specs=[hbm_spec] * 6,
        out_specs=vmem_spec,
        scratch_shapes=[
            pltpu.SMEM((order_count,), jnp.int32),
            pltpu.VMEM((4 * lats, 256), jnp.bfloat16),
            pltpu.VMEM((4 * out_rows, own_rows * 128), jnp.bfloat16),
            pltpu.VMEM((fields, own_lat, length), jnp.bfloat16),
            pltpu.VMEM((2, half_pack, ana_v.shape[2]), jnp.bfloat16),
            pltpu.VMEM((2, out_rows, half_pack), jnp.bfloat16),
            pltpu.VMEM((4 * out_rows, half_pack), jnp.bfloat16),
            pltpu.VMEM((4 * lats * GROUP, 128), jnp.float32),
            pltpu.VMEM((4 * lats * fields, 128), jnp.bfloat16),
            pltpu.VMEM((2, 8 * fields, lats // 2 * own_lat), jnp.bfloat16),
            pltpu.VMEM((2, half_pack, 128), jnp.float32),
            pltpu.VMEM((half_pack, 256), jnp.bfloat16),
            pltpu.VMEM((lats, own_rows, 128), jnp.float32),
            pltpu.VMEM((2 * lats, own_rows, 128), jnp.float32),
            pltpu.VMEM((lats * own_rows, 128), jnp.float32),
            pltpu.SemaphoreType.DMA((fields,)),
            pltpu.SemaphoreType.DMA((5,)),
            pltpu.SemaphoreType.DMA,
            pltpu.SemaphoreType.DMA((2, 2)),
            pltpu.SemaphoreType.DMA((2, 2)),
            pltpu.SemaphoreType.DMA((2, 2)),
            pltpu.SemaphoreType.DMA,
            pltpu.SemaphoreType.DMA,
        ],
        compiler_params=pltpu.CompilerParams(
            collective_id=0, has_side_effects=True, vmem_limit_bytes=40_000_000
        ),
    )(*(pltpu.with_memory_space_constraint(x, pltpu.HBM) for x in inputs))
    repeats = NLON_OUT // lax.axis_size("rep") // 128
    spread = 4
    return pl.pallas_call(
        repeat_kernel,
        out_shape=jax.ShapeDtypeStruct((fields, 2, own_rows, repeats * 128), jnp.float32),
        in_specs=[pl.BlockSpec(memory_space=pltpu.VMEM)],
        out_specs=hbm_spec,
        scratch_shapes=[
            pltpu.VMEM((fields, 2, own_rows, repeats // spread * 128), jnp.float32),
            pltpu.SemaphoreType.DMA((spread,)),
        ],
    )(pltpu.with_memory_space_constraint(small.reshape(fields, 2, own_rows, 128), pltpu.VMEM))


def fits(mesh, near_field, assign, ana_v, syn_v):
    lats = mesh.shape["lat"]
    fields, comps, rows, length = near_field.shape
    spacing = LMAX // assign.shape[0]
    return (
        mesh.shape["rep"] == 2
        and fields == 4 * GROUP
        and lats >= 4
        and comps == 2
        and lats & (lats - 1) == 0
        and rows == 128 * lats
        and assign.shape[0] == 2 * lats
        and 128 * spacing % length == 0
        and 128 * spacing % NLON_OUT == 0
        and syn_v.shape[2] == 32
        and ana_v.shape[1] % 64 == 0
    )


def solution(mesh):
    in_specs = (
        P(None, None, "lat", None),
        P(),
        P("lat", "rep", None),
        P("lat", "rep", None),
        P("lat", "rep", None),
        P("lat", "rep", None),
    )
    out_specs = P(None, None, "lat", "rep")

    def run(near_field, assign, ana_v, ana_w, syn_v, syn_w):
        chosen = fast_body if fits(mesh, near_field, assign, ana_v, syn_v) else plain_body
        mapped = jax.shard_map(chosen, mesh=mesh, in_specs=in_specs, out_specs=out_specs, check_vma=False)
        return mapped(near_field, assign, ana_v, ana_w, syn_v, syn_w)

    return run
```

```python
import functools
import math

import jax
import jax.numpy as jnp
from jax import lax
from jax.experimental import pallas as pl
from jax.experimental.pallas import tpu as pltpu
from jax.sharding import PartitionSpec as P

LMAX = 2048
NLON_OUT = 8192


def forward_table(orders, length):
    column = jnp.arange(length, dtype=jnp.int32)
    phase_index = orders[:, None] * column[None, :] % length
    angles = phase_index.astype(jnp.float32) * (2.0 * math.pi / length)
    factor = 1.0 / math.sqrt(length)
    stacked = jnp.stack([jnp.cos(angles) * factor, -jnp.sin(angles) * factor], axis=1)
    return stacked.reshape(2 * orders.shape[0], length).astype(jnp.bfloat16)


def inverse_table(orders, begin, count, length):
    column = begin + jnp.arange(count, dtype=jnp.int32)
    phase_index = orders[:, None] * column[None, :] % length
    angles = phase_index.astype(jnp.float32) * (2.0 * math.pi / length)
    weight = jnp.where(orders == 0, 1.0, 2.0).astype(jnp.float32)[:, None] / math.sqrt(
        orders.shape[0]
    )
    stacked = jnp.stack([weight * jnp.cos(angles), -weight * jnp.sin(angles)], axis=1)
    return stacked.reshape(2 * orders.shape[0], count).astype(jnp.bfloat16)


def pad_rows(matrix, tile_count, tile_rows):
    missing = tile_count * tile_rows - matrix.shape[0]
    return jnp.pad(matrix, ((0, missing), (0, 0))).reshape(tile_count, tile_rows, matrix.shape[1])


def legendre(spectra, mat_av, mat_aw, mat_sv, mat_sw, packed_start, first_order, second_order):
    count = spectra.shape[1]
    flat = spectra.reshape(2, 4 * count, spectra.shape[3])
    tile_rows = 128
    tile_count = -(-mat_av.shape[0] // tile_rows)
    out_rows = mat_sv.shape[1]
    border = LMAX - first_order

    def step(carry, inputs_now):
        total_v, total_w = carry
        number, tile_av, tile_aw, tile_sv, tile_sw = inputs_now
        first_row = packed_start + number * tile_rows
        packed = first_row + jnp.arange(tile_rows, dtype=jnp.int32)
        second = packed >= border
        branch_kind = jnp.where(
            first_row >= border, 1, jnp.where(first_row + tile_rows - 1 < border, 0, 2)
        )

        def single_slot(slot):

            def compute():
                slot_flat = flat[slot]
                part_v = jnp.dot(tile_av, slot_flat.T, preferred_element_type=jnp.float32).reshape(
                    tile_rows, 2, count, 2
                )
                part_w = jnp.dot(tile_aw, slot_flat.T, preferred_element_type=jnp.float32).reshape(
                    tile_rows, 2, count, 2
                )
                return (part_v, part_w)

            return compute

        def both_slots():
            first_v, first_w = single_slot(0)()
            second_v, second_w = single_slot(1)()
            choose_second = second[:, None, None, None]
            return (
                jnp.where(choose_second, second_v, first_v),
                jnp.where(choose_second, second_w, first_w),
            )

        chosen_v, chosen_w = lax.switch(branch_kind, [single_slot(0), single_slot(1), both_slots])
        degree = jnp.where(second, second_order + packed - border, first_order + packed)
        sph_re = chosen_v[:, 0, :, 0] + chosen_w[:, 1, :, 1]
        sph_im = chosen_v[:, 1, :, 0] - chosen_w[:, 0, :, 1]
        tor_re = chosen_w[:, 1, :, 0] - chosen_v[:, 0, :, 1]
        tor_im = -chosen_w[:, 0, :, 0] - chosen_v[:, 1, :, 1]
        quarter = (degree + 1) % 4
        cosine = jnp.where(quarter == 0, 1.0, jnp.where(quarter == 2, -1.0, 0.0)).astype(
            jnp.float32
        )[:, None]
        sine = jnp.where(quarter == 1, -1.0, jnp.where(quarter == 3, 1.0, 0.0)).astype(jnp.float32)[
            :, None
        ]
        coeffs = jnp.stack(
            [
                cosine * sph_re - sine * sph_im,
                cosine * sph_im + sine * sph_re,
                cosine * tor_re - sine * tor_im,
                cosine * tor_im + sine * tor_re,
            ],
            axis=1,
        ).astype(jnp.bfloat16)
        flat_coeffs = coeffs.reshape(tile_rows, 4 * count)
        second_mask = second.astype(jnp.bfloat16)[:, None]

        def mixed_rows():
            lower_c = flat_coeffs * (1 - second_mask)
            upper_c = flat_coeffs * second_mask
            add_v = jnp.stack(
                [
                    jnp.dot(lower_c.T, tile_sv, preferred_element_type=jnp.float32),
                    jnp.dot(upper_c.T, tile_sv, preferred_element_type=jnp.float32),
                ]
            )
            add_w = jnp.stack(
                [
                    jnp.dot(lower_c.T, tile_sw, preferred_element_type=jnp.float32),
                    jnp.dot(upper_c.T, tile_sw, preferred_element_type=jnp.float32),
                ]
            )
            return (add_v, add_w)

        def single_rows():
            part_v = jnp.dot(flat_coeffs.T, tile_sv, preferred_element_type=jnp.float32)
            part_w = jnp.dot(flat_coeffs.T, tile_sw, preferred_element_type=jnp.float32)
            upper_pick = (branch_kind == 1).astype(jnp.float32)
            return (
                jnp.stack([part_v * (1.0 - upper_pick), part_v * upper_pick]),
                jnp.stack([part_w * (1.0 - upper_pick), part_w * upper_pick]),
            )

        add_v, add_w = lax.cond(branch_kind == 2, mixed_rows, single_rows)
        return ((total_v + add_v, total_w + add_w), None)

    start_v = jnp.zeros((2, 4 * count, out_rows), jnp.float32)
    start_w = jnp.zeros((2, 4 * count, out_rows), jnp.float32)
    numbers = jnp.arange(tile_count, dtype=jnp.int32)
    (total_v, total_w), unused = lax.scan(
        step,
        (start_v, start_w),
        (
            numbers,
            pad_rows(mat_av, tile_count, tile_rows),
            pad_rows(mat_aw, tile_count, tile_rows),
            pad_rows(mat_sv, tile_count, tile_rows),
            pad_rows(mat_sw, tile_count, tile_rows),
        ),
    )
    synth_v = total_v.reshape(2, 4, count, -1)
    synth_w = total_w.reshape(2, 4, count, -1)
    theta_re = synth_v[:, 0] - synth_w[:, 3]
    theta_im = synth_v[:, 1] + synth_w[:, 2]
    phi_re = -synth_w[:, 1] - synth_v[:, 2]
    phi_im = synth_w[:, 0] - synth_v[:, 3]
    real_part = jnp.stack([theta_re, phi_re], axis=2)
    imag_part = jnp.stack([theta_im, phi_im], axis=2)
    return jnp.stack([real_part, imag_part], axis=1).reshape(4, count, 2, -1)


def plain_body(near_field, assign, ana_v, ana_w, syn_v, syn_w):
    order_count = assign.shape[0]
    spacing = LMAX // order_count
    orders = spacing * assign
    pair_orders = lax.dynamic_slice_in_dim(orders, 2 * lax.axis_index("lat"), 2, 0)
    half_pack = ana_v.shape[1]
    packed_start = lax.axis_index("rep") * half_pack
    table = forward_table(orders, near_field.shape[3])
    spectrum = jnp.einsum(
        "jk,fctk->jfct", table, near_field, preferred_element_type=jnp.float32
    ).astype(jnp.bfloat16)
    partial_value = legendre(
        lax.all_to_all(spectrum, "lat", split_axis=0, concat_axis=3, tiled=True),
        ana_v[0],
        ana_w[0],
        syn_v[0],
        syn_w[0],
        packed_start,
        pair_orders[0],
        pair_orders[1],
    )
    summed = lax.psum(partial_value, "rep").astype(jnp.bfloat16)
    regrouped = lax.all_to_all(summed, "lat", split_axis=3, concat_axis=0, tiled=True)
    longitudes = NLON_OUT // lax.axis_size("rep")
    inverse = inverse_table(orders, lax.axis_index("rep") * longitudes, longitudes, NLON_OUT)
    return jnp.einsum("jfcr,jp->fcrp", regrouped, inverse, preferred_element_type=jnp.float32)

MESH = pl.DeviceIdType.MESH
GROUP = 4
NT = (((1,), (1,)), ((), ()))
TN = (((0,), (0,)), ((), ()))


def kernel(
    lats,
    spacing,
    assign_hbm,
    field_hbm,
    av_hbm,
    aw_hbm,
    sv_hbm,
    sw_hbm,
    out_ref,
    assign_ref,
    table_ref,
    inverse_ref,
    ring,
    ana,
    syn,
    mix,
    folded,
    staged,
    packet,
    spec,
    total,
    coeffs,
    rows_out,
    rows_in,
    rows_sum,
    field_sem,
    load_sem,
    send_sem,
    recv_sem,
    pass_send,
    pass_recv,
    row_send,
    row_recv,
):
    lat = lax.axis_index("lat")
    rep = lax.axis_index("rep")
    other = 1 - rep
    fields = field_hbm.shape[0]
    groups = fields // GROUP
    half_pack = ana.shape[1]
    span = 4 * GROUP
    near = lats // 2
    side = lat // near
    spot = lax.rem(lat, near)
    width = near * 128

    def fetch(f):
        return pltpu.make_async_copy(field_hbm.at[f, rep], ring.at[f], field_sem.at[f])

    loads = [
        pltpu.make_async_copy(assign_hbm, assign_ref, load_sem.at[0]),
        pltpu.make_async_copy(sv_hbm.at[0], syn.at[0], load_sem.at[1]),
        pltpu.make_async_copy(sw_hbm.at[0], syn.at[1], load_sem.at[2]),
        pltpu.make_async_copy(av_hbm.at[0], ana.at[0], load_sem.at[3]),
        pltpu.make_async_copy(aw_hbm.at[0], ana.at[1], load_sem.at[4]),
    ]
    barrier = pltpu.get_barrier_semaphore()

    def greet(i, carry):
        peer = lax.rem(lat + i, lats)
        pl.semaphore_signal(barrier, inc=1, device_id=(peer, rep), device_id_type=MESH)
        return carry

    lax.fori_loop(1, lats, greet, 0)
    pl.semaphore_signal(barrier, inc=1, device_id=(lat, other), device_id_type=MESH)

    loads[0].start()
    for f in range(GROUP):
        fetch(f).start()

    for f in range(GROUP, fields):
        fetch(f).start()
    for load in loads[1:]:
        load.start()

    loads[0].wait()
    length = field_hbm.shape[3]

    def orders_of(index):
        order = jnp.zeros(index.shape, jnp.int32)
        for k in range(2 * lats):
            order = jnp.where(index == k, spacing * assign_ref[k], order)
        return order

    shape = (4 * lats, 128)
    row = lax.broadcasted_iota(jnp.int32, shape, 0)
    phase = orders_of((row // 4) * 2 + (row & 1)) * lax.broadcasted_iota(jnp.int32, shape, 1)
    phase = lax.rem(phase + ((row // 2) & 1) * (length // 4), length)
    wave = jnp.cos(phase.astype(jnp.float32) * (2.0 * math.pi / length)) * (1.0 / math.sqrt(length))
    wave = wave.astype(jnp.bfloat16)
    table_ref[:, 0:128] = wave
    table_ref[:, 128:256] = wave

    def send(group, peer, far):
        return pltpu.make_async_remote_copy(
            src_ref=packet.at[pl.ds(pl.multiple_of((group * lats + peer) * span, span), span)],
            dst_ref=spec.at[
                far,
                pl.ds(pl.multiple_of((rep * groups + group) * span, span), span),
                pl.ds(pl.multiple_of(spot * 128, 128), 128),
            ],
            send_sem=send_sem,
            recv_sem=recv_sem.at[1 if group == groups - 1 else 0, far],
            device_id=(peer, rep),
            device_id_type=MESH,
        )

    def bulk(rows, send_at, recv_at):
        return pltpu.make_async_remote_copy(
            src_ref=packet.at[pl.ds(0, rows)],
            dst_ref=packet.at[pl.ds(0, rows)],
            send_sem=send_at,
            recv_sem=recv_at,
            device_id=(lat, other),
            device_id_type=MESH,
        )

    def arrived(last, far):
        blocks = (1 if last else groups - 1) * (near if far else near - 1)
        bulk(blocks * span, send_sem, recv_sem.at[last, far]).wait_recv()

    def hand(core, last, far):
        begin, count = (groups - 1, 1) if last else (0, groups - 1)
        block = spec.at[far, pl.ds(pl.multiple_of((core * groups + begin) * span, span), count * span)]
        return pltpu.make_async_remote_copy(
            src_ref=block,
            dst_ref=block,
            send_sem=pass_send.at[last, far],
            recv_sem=pass_recv.at[last, far],
            device_id=(lat, other),
            device_id_type=MESH,
        )

    def fold(f, carry):
        fetch(f).wait()
        total_f = ring[f, :, 0:128].astype(jnp.float32)
        for piece in range(1, ring.shape[2] // 128):
            total_f = total_f + ring[f, :, piece * 128 : (piece + 1) * 128].astype(jnp.float32)
        high = total_f.astype(jnp.bfloat16)
        low = (total_f - high.astype(jnp.float32)).astype(jnp.bfloat16)
        begin = pl.multiple_of(lax.rem(f, GROUP) * 128, 128)
        folded[pl.ds(begin, 128), 0:128] = high
        folded[pl.ds(begin, 128), 128:256] = low
        return carry

    for group in range(groups):
        lax.fori_loop(group * GROUP, (group + 1) * GROUP, fold, 0)
        value = lax.dot_general(table_ref[...], folded[...], NT, preferred_element_type=jnp.float32)
        for k in range(GROUP):
            staged[pl.ds(k, 4 * lats, stride=GROUP), :] = value[:, k * 128 : (k + 1) * 128]
        packet[group * lats * span : (group + 1) * lats * span, :] = staged[...].astype(jnp.bfloat16)
        if group == 0:
            pl.semaphore_wait(barrier, lats)

        def send_far(i, carry, group=group):
            send(group, (1 - side) * near + lax.rem(spot + i, near), 1).start()
            return carry

        def send_near(i, carry, group=group):
            send(group, side * near + lax.rem(spot + i, near), 0).start()
            return carry

        lax.fori_loop(0, near, send_far, 0)
        lax.fori_loop(1, near, send_near, 0)
        spec[
            0,
            pl.ds(pl.multiple_of((rep * groups + group) * span, span), span),
            pl.ds(pl.multiple_of(spot * 128, 128), 128),
        ] = packet[pl.ds(pl.multiple_of((group * lats + lat) * span, span), span), :]

    first_order = spacing * assign_ref[2 * lat]
    second_order = spacing * assign_ref[2 * lat + 1]
    border = LMAX - first_order
    loads[1].wait()
    loads[2].wait()
    out_rows = syn.shape[1]
    kinds = 4 * out_rows
    row_at = lax.broadcasted_iota(jnp.int32, (kinds, out_rows), 0)
    col_at = lax.broadcasted_iota(jnp.int32, (kinds, out_rows), 1)
    pick_v = ((row_at == col_at) | (row_at == col_at + out_rows)).astype(jnp.float32).astype(jnp.bfloat16)
    pick_w = (
        ((row_at == col_at + 2 * out_rows) | (row_at == col_at + 3 * out_rows)).astype(jnp.float32).astype(jnp.bfloat16)
    )
    spread = jnp.dot(pick_v, syn[0], preferred_element_type=jnp.float32)
    spread = spread + jnp.dot(pick_w, syn[1], preferred_element_type=jnp.float32)
    packed = rep * half_pack + lax.broadcasted_iota(jnp.int32, (1, half_pack), 1)
    degree = jnp.where(packed >= border, second_order + packed - border, first_order + packed)
    quarter = (degree + 1) & 3
    cosine = jnp.where(quarter == 0, 1.0, jnp.where(quarter == 2, -1.0, 0.0))
    sine = jnp.where(quarter == 1, -1.0, jnp.where(quarter == 3, 1.0, 0.0))
    kind = lax.broadcasted_iota(jnp.int32, (kinds, 1), 0) // out_rows
    factor = jnp.where((kind & 1) == 0, cosine, sine)
    mix[...] = (spread * factor).astype(jnp.bfloat16)

    own_rows = out_rows // lats
    shape = (out_rows, 128)
    row = lax.broadcasted_iota(jnp.int32, shape, 0)
    n = lax.broadcasted_iota(jnp.int32, shape, 1)
    for slot_at in range(2):
        order = orders_of((row // own_rows) * 2 + slot_at)
        weight = jnp.where(order == 0, 1.0, 2.0) * (1.0 / math.sqrt(2 * lats))
        for part_at in range(2):
            phase = lax.rem(order * n + part_at * (NLON_OUT // 4), NLON_OUT)
            wave = weight * jnp.cos(phase.astype(jnp.float32) * (2.0 * math.pi / NLON_OUT))
            begin = (part_at * 2 + slot_at) * out_rows
            for o in range(own_rows):
                inverse_ref[begin : begin + out_rows, o * 128 : (o + 1) * 128] = jnp.where(
                    lax.rem(row, own_rows) == o, wave, 0.0
                ).astype(jnp.bfloat16)

    columns = pl.ds(pl.multiple_of(side * width, 128), width)

    def start_project(k):
        total[k] = lax.dot_general(ana[k, :, columns], spec[0], NT, preferred_element_type=jnp.float32)

    loads[3].wait()
    loads[4].wait()
    arrived(0, 0)
    hand(rep, 0, 0).start()
    arrived(1, 0)
    hand(rep, 1, 0).start()
    arrived(0, 1)
    hand(rep, 0, 1).start()
    arrived(1, 1)
    hand(rep, 1, 1).start()
    hand(other, 0, 0).wait_recv()
    hand(other, 1, 0).wait_recv()
    start_project(0)
    start_project(1)
    hand(other, 0, 1).wait_recv()
    hand(other, 1, 1).wait_recv()

    columns = pl.ds(pl.multiple_of((1 - side) * width, 128), width)
    lane = lax.broadcasted_iota(jnp.int32, (1, 128), 1)
    lane_slot = (lane // GROUP) & 1
    at = rep * half_pack + lax.broadcasted_iota(jnp.int32, (half_pack, 1), 0)
    row_slot = jnp.where(at >= border, 1, 0)
    for k in range(2):
        value = total[k] + lax.dot_general(ana[k, :, columns], spec[1], NT, preferred_element_type=jnp.float32)
        coeffs[:, k * 128 : (k + 1) * 128] = jnp.where(row_slot == lane_slot, value, 0.0).astype(jnp.bfloat16)

    part = (lane // (2 * GROUP)) & 1
    comp = lane // 64

    def swap_part(x):
        return jnp.where(part == 0, pltpu.roll(x, 128 - 2 * GROUP, 1), pltpu.roll(x, 2 * GROUP, 1))

    def swap_comp(x):
        return pltpu.roll(x, 64, 1)

    part_sign = jnp.where(part == 0, -1.0, 1.0)
    comp_sign = jnp.where(comp == 0, 1.0, -1.0)
    synth = jnp.dot(mix[...], coeffs[...], preferred_element_type=jnp.float32)
    synth = synth[:, 0:128] - comp_sign * part_sign * swap_comp(swap_part(synth[:, 128:256]))
    cos_v, sin_v, cos_w, sin_w = (synth[k * out_rows : (k + 1) * out_rows] for k in range(4))
    rows = cos_v + part_sign * swap_part(sin_v)
    rows = rows + comp_sign * swap_comp(sin_w) - comp_sign * part_sign * swap_comp(swap_part(cos_w))
    for k in range(lats):
        rows_out[k] = rows[k * own_rows : (k + 1) * own_rows]

    def row_copy(target_lat, target_rep):
        return pltpu.make_async_remote_copy(
            src_ref=rows_out.at[target_lat],
            dst_ref=rows_in.at[rep * lats + lat],
            send_sem=row_send,
            recv_sem=row_recv,
            device_id=(target_lat, target_rep),
            device_id_type=MESH,
        )

    def send_rows(i, carry):
        peer = lax.rem(lat + i, lats)
        row_copy(peer, rep).start()
        row_copy(peer, other).start()
        return carry

    lax.fori_loop(1, lats, send_rows, 0)
    row_copy(lat, other).start()
    rows_in[rep * lats + lat] = rows_out[lat]

    bulk(groups * (lats - 1) * span, send_sem, recv_sem.at[0, 0]).wait_send()
    for last in range(2):
        for far in range(2):
            hand(rep, last, far).wait_send()

    all_rows = pltpu.make_async_remote_copy(
        src_ref=rows_in.at[pl.ds(0, 2 * lats - 1)],
        dst_ref=rows_in.at[pl.ds(0, 2 * lats - 1)],
        send_sem=row_send,
        recv_sem=row_recv,
        device_id=(lat, other),
        device_id_type=MESH,
    )
    all_rows.wait_recv()

    for k in range(lats):
        rows_sum[k * own_rows : (k + 1) * own_rows, :] = rows_in[k] + rows_in[lats + k]
    summed = rows_sum[...]
    gathered = [summed] + [pltpu.roll(summed, 128 - k * GROUP, 1) for k in range(1, 4)]
    gathered = jnp.concatenate(gathered, axis=0).astype(jnp.bfloat16)
    value = lax.dot_general(gathered, inverse_ref[...], TN, preferred_element_type=jnp.float32)
    for block in range(2 * groups):
        comp_at, group = block // groups, block % groups
        for o in range(own_rows):
            begin = (group * GROUP * 2 + comp_at) * own_rows + o
            out_ref[pl.ds(begin, GROUP, stride=2 * own_rows), :] = value[
                block * span : block * span + GROUP, o * 128 : (o + 1) * 128
            ]
    all_rows.wait_send()


def repeat_kernel(small_ref, out_hbm, wide, sem):
    value = small_ref[...]
    width = wide.shape[3]
    for k in range(width // 128):
        wide[:, :, :, k * 128 : (k + 1) * 128] = value
    copies = [
        pltpu.make_async_copy(wide, out_hbm.at[:, :, :, k * width : (k + 1) * width], sem.at[k])
        for k in range(out_hbm.shape[3] // width)
    ]
    for copy in copies:
        copy.start()
    for copy in copies:
        copy.wait()


def fast_body(near_field, assign, ana_v, ana_w, syn_v, syn_w):
    lats = lax.axis_size("lat")
    fields, comps, own_lat, length = near_field.shape
    order_count = assign.shape[0]
    half_pack = ana_v.shape[1]
    out_rows = syn_v.shape[2]
    own_rows = out_rows // lats
    hbm_spec = pl.BlockSpec(memory_space=pltpu.HBM)
    vmem_spec = pl.BlockSpec(memory_space=pltpu.VMEM)
    inputs = (assign, near_field, ana_v, ana_w, syn_v.swapaxes(1, 2), syn_w.swapaxes(1, 2))
    small = pl.pallas_call(
        functools.partial(kernel, lats, LMAX // order_count),
        out_shape=pltpu.VMEM((fields * 2 * own_rows, 128), jnp.float32),
        in_specs=[hbm_spec] * 6,
        out_specs=vmem_spec,
        scratch_shapes=[
            pltpu.SMEM((order_count,), jnp.int32),
            pltpu.VMEM((4 * lats, 256), jnp.bfloat16),
            pltpu.VMEM((4 * out_rows, own_rows * 128), jnp.bfloat16),
            pltpu.VMEM((fields, own_lat, length), jnp.bfloat16),
            pltpu.VMEM((2, half_pack, ana_v.shape[2]), jnp.bfloat16),
            pltpu.VMEM((2, out_rows, half_pack), jnp.bfloat16),
            pltpu.VMEM((4 * out_rows, half_pack), jnp.bfloat16),
            pltpu.VMEM((128 * GROUP, 256), jnp.bfloat16),
            pltpu.VMEM((4 * lats * GROUP, 128), jnp.float32),
            pltpu.VMEM((4 * lats * fields, 128), jnp.bfloat16),
            pltpu.VMEM((2, 8 * fields, lats // 2 * own_lat), jnp.bfloat16),
            pltpu.VMEM((2, half_pack, 128), jnp.float32),
            pltpu.VMEM((half_pack, 256), jnp.bfloat16),
            pltpu.VMEM((lats, own_rows, 128), jnp.float32),
            pltpu.VMEM((2 * lats, own_rows, 128), jnp.float32),
            pltpu.VMEM((lats * own_rows, 128), jnp.float32),
            pltpu.SemaphoreType.DMA((fields,)),
            pltpu.SemaphoreType.DMA((5,)),
            pltpu.SemaphoreType.DMA,
            pltpu.SemaphoreType.DMA((2, 2)),
            pltpu.SemaphoreType.DMA((2, 2)),
            pltpu.SemaphoreType.DMA((2, 2)),
            pltpu.SemaphoreType.DMA,
            pltpu.SemaphoreType.DMA,
        ],
        compiler_params=pltpu.CompilerParams(
            collective_id=0, has_side_effects=True, vmem_limit_bytes=40_000_000
        ),
    )(*(pltpu.with_memory_space_constraint(x, pltpu.HBM) for x in inputs))
    repeats = NLON_OUT // lax.axis_size("rep") // 128
    spread = 4
    return pl.pallas_call(
        repeat_kernel,
        out_shape=jax.ShapeDtypeStruct((fields, 2, own_rows, repeats * 128), jnp.float32),
        in_specs=[pl.BlockSpec(memory_space=pltpu.VMEM)],
        out_specs=hbm_spec,
        scratch_shapes=[
            pltpu.VMEM((fields, 2, own_rows, repeats // spread * 128), jnp.float32),
            pltpu.SemaphoreType.DMA((spread,)),
        ],
    )(pltpu.with_memory_space_constraint(small.reshape(fields, 2, own_rows, 128), pltpu.VMEM))


def fits(mesh, near_field, assign, ana_v, syn_v):
    lats = mesh.shape["lat"]
    fields, comps, rows, length = near_field.shape
    spacing = LMAX // assign.shape[0]
    return (
        mesh.shape["rep"] == 2
        and fields == 4 * GROUP
        and lats >= 4
        and comps == 2
        and lats & (lats - 1) == 0
        and rows == 128 * lats
        and assign.shape[0] == 2 * lats
        and 128 * spacing % length == 0
        and 128 * spacing % NLON_OUT == 0
        and syn_v.shape[2] == 32
        and ana_v.shape[1] % 64 == 0
    )


def solution(mesh):
    in_specs = (
        P(None, None, "lat", None),
        P(),
        P("lat", "rep", None),
        P("lat", "rep", None),
        P("lat", "rep", None),
        P("lat", "rep", None),
    )
    out_specs = P(None, None, "lat", "rep")

    def run(near_field, assign, ana_v, ana_w, syn_v, syn_w):
        chosen = fast_body if fits(mesh, near_field, assign, ana_v, syn_v) else plain_body
        mapped = jax.shard_map(chosen, mesh=mesh, in_specs=in_specs, out_specs=out_specs, check_vma=False)
        return mapped(near_field, assign, ana_v, ana_w, syn_v, syn_w)

    return run
```

```python
import functools
import math

import jax
import jax.numpy as jnp
from jax import lax
from jax.experimental import pallas as pl
from jax.experimental.pallas import tpu as pltpu
from jax.sharding import PartitionSpec as P

LMAX = 2048
NLON_OUT = 8192


def forward_table(orders, length):
    column = jnp.arange(length, dtype=jnp.int32)
    phase_index = orders[:, None] * column[None, :] % length
    angles = phase_index.astype(jnp.float32) * (2.0 * math.pi / length)
    factor = 1.0 / math.sqrt(length)
    stacked = jnp.stack([jnp.cos(angles) * factor, -jnp.sin(angles) * factor], axis=1)
    return stacked.reshape(2 * orders.shape[0], length).astype(jnp.bfloat16)


def inverse_table(orders, begin, count, length):
    column = begin + jnp.arange(count, dtype=jnp.int32)
    phase_index = orders[:, None] * column[None, :] % length
    angles = phase_index.astype(jnp.float32) * (2.0 * math.pi / length)
    weight = jnp.where(orders == 0, 1.0, 2.0).astype(jnp.float32)[:, None] / math.sqrt(
        orders.shape[0]
    )
    stacked = jnp.stack([weight * jnp.cos(angles), -weight * jnp.sin(angles)], axis=1)
    return stacked.reshape(2 * orders.shape[0], count).astype(jnp.bfloat16)


def pad_rows(matrix, tile_count, tile_rows):
    missing = tile_count * tile_rows - matrix.shape[0]
    return jnp.pad(matrix, ((0, missing), (0, 0))).reshape(tile_count, tile_rows, matrix.shape[1])


def legendre(spectra, mat_av, mat_aw, mat_sv, mat_sw, packed_start, first_order, second_order):
    count = spectra.shape[1]
    flat = spectra.reshape(2, 4 * count, spectra.shape[3])
    tile_rows = 128
    tile_count = -(-mat_av.shape[0] // tile_rows)
    out_rows = mat_sv.shape[1]
    border = LMAX - first_order

    def step(carry, inputs_now):
        total_v, total_w = carry
        number, tile_av, tile_aw, tile_sv, tile_sw = inputs_now
        first_row = packed_start + number * tile_rows
        packed = first_row + jnp.arange(tile_rows, dtype=jnp.int32)
        second = packed >= border
        branch_kind = jnp.where(
            first_row >= border, 1, jnp.where(first_row + tile_rows - 1 < border, 0, 2)
        )

        def single_slot(slot):

            def compute():
                slot_flat = flat[slot]
                part_v = jnp.dot(tile_av, slot_flat.T, preferred_element_type=jnp.float32).reshape(
                    tile_rows, 2, count, 2
                )
                part_w = jnp.dot(tile_aw, slot_flat.T, preferred_element_type=jnp.float32).reshape(
                    tile_rows, 2, count, 2
                )
                return (part_v, part_w)

            return compute

        def both_slots():
            first_v, first_w = single_slot(0)()
            second_v, second_w = single_slot(1)()
            choose_second = second[:, None, None, None]
            return (
                jnp.where(choose_second, second_v, first_v),
                jnp.where(choose_second, second_w, first_w),
            )

        chosen_v, chosen_w = lax.switch(branch_kind, [single_slot(0), single_slot(1), both_slots])
        degree = jnp.where(second, second_order + packed - border, first_order + packed)
        sph_re = chosen_v[:, 0, :, 0] + chosen_w[:, 1, :, 1]
        sph_im = chosen_v[:, 1, :, 0] - chosen_w[:, 0, :, 1]
        tor_re = chosen_w[:, 1, :, 0] - chosen_v[:, 0, :, 1]
        tor_im = -chosen_w[:, 0, :, 0] - chosen_v[:, 1, :, 1]
        quarter = (degree + 1) % 4
        cosine = jnp.where(quarter == 0, 1.0, jnp.where(quarter == 2, -1.0, 0.0)).astype(
            jnp.float32
        )[:, None]
        sine = jnp.where(quarter == 1, -1.0, jnp.where(quarter == 3, 1.0, 0.0)).astype(jnp.float32)[
            :, None
        ]
        coeffs = jnp.stack(
            [
                cosine * sph_re - sine * sph_im,
                cosine * sph_im + sine * sph_re,
                cosine * tor_re - sine * tor_im,
                cosine * tor_im + sine * tor_re,
            ],
            axis=1,
        ).astype(jnp.bfloat16)
        flat_coeffs = coeffs.reshape(tile_rows, 4 * count)
        second_mask = second.astype(jnp.bfloat16)[:, None]

        def mixed_rows():
            lower_c = flat_coeffs * (1 - second_mask)
            upper_c = flat_coeffs * second_mask
            add_v = jnp.stack(
                [
                    jnp.dot(lower_c.T, tile_sv, preferred_element_type=jnp.float32),
                    jnp.dot(upper_c.T, tile_sv, preferred_element_type=jnp.float32),
                ]
            )
            add_w = jnp.stack(
                [
                    jnp.dot(lower_c.T, tile_sw, preferred_element_type=jnp.float32),
                    jnp.dot(upper_c.T, tile_sw, preferred_element_type=jnp.float32),
                ]
            )
            return (add_v, add_w)

        def single_rows():
            part_v = jnp.dot(flat_coeffs.T, tile_sv, preferred_element_type=jnp.float32)
            part_w = jnp.dot(flat_coeffs.T, tile_sw, preferred_element_type=jnp.float32)
            upper_pick = (branch_kind == 1).astype(jnp.float32)
            return (
                jnp.stack([part_v * (1.0 - upper_pick), part_v * upper_pick]),
                jnp.stack([part_w * (1.0 - upper_pick), part_w * upper_pick]),
            )

        add_v, add_w = lax.cond(branch_kind == 2, mixed_rows, single_rows)
        return ((total_v + add_v, total_w + add_w), None)

    start_v = jnp.zeros((2, 4 * count, out_rows), jnp.float32)
    start_w = jnp.zeros((2, 4 * count, out_rows), jnp.float32)
    numbers = jnp.arange(tile_count, dtype=jnp.int32)
    (total_v, total_w), unused = lax.scan(
        step,
        (start_v, start_w),
        (
            numbers,
            pad_rows(mat_av, tile_count, tile_rows),
            pad_rows(mat_aw, tile_count, tile_rows),
            pad_rows(mat_sv, tile_count, tile_rows),
            pad_rows(mat_sw, tile_count, tile_rows),
        ),
    )
    synth_v = total_v.reshape(2, 4, count, -1)
    synth_w = total_w.reshape(2, 4, count, -1)
    theta_re = synth_v[:, 0] - synth_w[:, 3]
    theta_im = synth_v[:, 1] + synth_w[:, 2]
    phi_re = -synth_w[:, 1] - synth_v[:, 2]
    phi_im = synth_w[:, 0] - synth_v[:, 3]
    real_part = jnp.stack([theta_re, phi_re], axis=2)
    imag_part = jnp.stack([theta_im, phi_im], axis=2)
    return jnp.stack([real_part, imag_part], axis=1).reshape(4, count, 2, -1)


def plain_body(near_field, assign, ana_v, ana_w, syn_v, syn_w):
    order_count = assign.shape[0]
    spacing = LMAX // order_count
    orders = spacing * assign
    pair_orders = lax.dynamic_slice_in_dim(orders, 2 * lax.axis_index("lat"), 2, 0)
    half_pack = ana_v.shape[1]
    packed_start = lax.axis_index("rep") * half_pack
    table = forward_table(orders, near_field.shape[3])
    spectrum = jnp.einsum(
        "jk,fctk->jfct", table, near_field, preferred_element_type=jnp.float32
    ).astype(jnp.bfloat16)
    partial_value = legendre(
        lax.all_to_all(spectrum, "lat", split_axis=0, concat_axis=3, tiled=True),
        ana_v[0],
        ana_w[0],
        syn_v[0],
        syn_w[0],
        packed_start,
        pair_orders[0],
        pair_orders[1],
    )
    summed = lax.psum(partial_value, "rep").astype(jnp.bfloat16)
    regrouped = lax.all_to_all(summed, "lat", split_axis=3, concat_axis=0, tiled=True)
    longitudes = NLON_OUT // lax.axis_size("rep")
    inverse = inverse_table(orders, lax.axis_index("rep") * longitudes, longitudes, NLON_OUT)
    return jnp.einsum("jfcr,jp->fcrp", regrouped, inverse, preferred_element_type=jnp.float32)

MESH = pl.DeviceIdType.MESH
GROUP = 4
BATCHES = (2, 1, 1)
NT = (((1,), (1,)), ((), ()))
TN = (((0,), (0,)), ((), ()))


def kernel(
    lats,
    spacing,
    assign_hbm,
    field_hbm,
    av_hbm,
    aw_hbm,
    sv_hbm,
    sw_hbm,
    out_ref,
    assign_ref,
    table_ref,
    inverse_ref,
    ring,
    ana,
    syn,
    mix,
    folded,
    staged,
    packets,
    spec,
    total,
    joined,
    rows_out,
    rows_in,
    rows_sum,
    field_sem,
    load_sem,
    send_sem,
    recv_sem,
    pass_send,
    pass_recv,
    row_send,
    row_recv,
):
    lat = lax.axis_index("lat")
    rep = lax.axis_index("rep")
    other = 1 - rep
    fields = field_hbm.shape[0]
    groups = fields // GROUP
    half_pack = ana.shape[1]
    span = 4 * GROUP
    near = lats // 2
    side = lat // near
    spot = lax.rem(lat, near)
    width = near * 128

    def fetch(f):
        return pltpu.make_async_copy(field_hbm.at[f, rep], ring.at[f], field_sem.at[f])

    loads = [
        pltpu.make_async_copy(assign_hbm, assign_ref, load_sem.at[0]),
        pltpu.make_async_copy(sv_hbm.at[0], syn.at[0], load_sem.at[1]),
        pltpu.make_async_copy(sw_hbm.at[0], syn.at[1], load_sem.at[2]),
        pltpu.make_async_copy(av_hbm.at[0], ana.at[0], load_sem.at[3]),
        pltpu.make_async_copy(aw_hbm.at[0], ana.at[1], load_sem.at[4]),
    ]
    barrier = pltpu.get_barrier_semaphore()

    def greet(i, carry):
        peer = lax.rem(lat + i, lats)
        pl.semaphore_signal(barrier, inc=1, device_id=(peer, rep), device_id_type=MESH)
        return carry

    lax.fori_loop(1, lats, greet, 0)
    pl.semaphore_signal(barrier, inc=1, device_id=(lat, other), device_id_type=MESH)

    loads[0].start()
    for f in range(GROUP):
        fetch(f).start()

    for f in range(GROUP, fields):
        fetch(f).start()
    for load in loads[1:]:
        load.start()

    loads[0].wait()
    length = field_hbm.shape[3]

    def orders_of(index):
        order = jnp.zeros(index.shape, jnp.int32)
        for k in range(2 * lats):
            order = jnp.where(index == k, spacing * assign_ref[k], order)
        return order

    shape = (4 * lats, 128)
    row = lax.broadcasted_iota(jnp.int32, shape, 0)
    phase = orders_of((row // 4) * 2 + (row & 1)) * lax.broadcasted_iota(jnp.int32, shape, 1)
    phase = lax.rem(phase + ((row // 2) & 1) * (length // 4), length)
    wave = jnp.cos(phase.astype(jnp.float32) * (2.0 * math.pi / length)) * (1.0 / math.sqrt(length))
    wave = wave.astype(jnp.bfloat16)
    table_ref[:, 0:128] = wave
    table_ref[:, 128:256] = wave

    def send(batch, peer, far):
        first, count = sum(BATCHES[:batch]), BATCHES[batch]
        return pltpu.make_async_remote_copy(
            src_ref=packets[batch].at[peer],
            dst_ref=spec.at[
                far,
                pl.ds(pl.multiple_of((rep * groups + first) * span, span), count * span),
                pl.ds(pl.multiple_of(spot * 128, 128), 128),
            ],
            send_sem=send_sem,
            recv_sem=recv_sem.at[1 if batch == len(BATCHES) - 1 else 0, far],
            device_id=(peer, rep),
            device_id_type=MESH,
        )

    def bulk(blocks, send_at, recv_at):
        tall = 1
        while blocks % tall or blocks // tall * 128 > ring.shape[2]:
            tall += 1
        like = ring.at[0, pl.ds(0, tall * span), pl.ds(0, blocks // tall * 128)]
        return pltpu.make_async_remote_copy(
            src_ref=like,
            dst_ref=like,
            send_sem=send_at,
            recv_sem=recv_at,
            device_id=(lat, other),
            device_id_type=MESH,
        )

    def arrived(last, far):
        blocks = (BATCHES[-1] if last else groups - BATCHES[-1]) * (near if far else near - 1)
        bulk(blocks, send_sem, recv_sem.at[last, far]).wait_recv()

    def hand(core, last, far):
        tail = BATCHES[-1]
        begin, count = (groups - tail, tail) if last else (0, groups - tail)
        block = spec.at[far, pl.ds(pl.multiple_of((core * groups + begin) * span, span), count * span)]
        return pltpu.make_async_remote_copy(
            src_ref=block,
            dst_ref=block,
            send_sem=pass_send.at[last, far],
            recv_sem=pass_recv.at[last, far],
            device_id=(lat, other),
            device_id_type=MESH,
        )

    def fold(f, carry):
        fetch(f).wait()
        total_f = ring[f, :, 0:128].astype(jnp.float32)
        for piece in range(1, ring.shape[2] // 128):
            total_f = total_f + ring[f, :, piece * 128 : (piece + 1) * 128].astype(jnp.float32)
        high = total_f.astype(jnp.bfloat16)
        low = (total_f - high.astype(jnp.float32)).astype(jnp.bfloat16)
        begin = pl.multiple_of(lax.rem(f, GROUP) * 128, 128)
        folded[pl.ds(begin, 128), 0:128] = high
        folded[pl.ds(begin, 128), 128:256] = low
        return carry

    group = 0
    for batch, count in enumerate(BATCHES):
        for member in range(count):
            lax.fori_loop(group * GROUP, (group + 1) * GROUP, fold, 0)
            value = lax.dot_general(table_ref[...], folded[...], NT, preferred_element_type=jnp.float32)
            for k in range(GROUP):
                staged[pl.ds(k, 4 * lats, stride=GROUP), :] = value[:, k * 128 : (k + 1) * 128]
            packets[batch][:, member * span : (member + 1) * span, :] = (
                staged[...].astype(jnp.bfloat16).reshape(lats, span, 128)
            )
            spec[
                0,
                pl.ds(pl.multiple_of((rep * groups + group) * span, span), span),
                pl.ds(pl.multiple_of(spot * 128, 128), 128),
            ] = packets[batch][lat, member * span : (member + 1) * span, :]
            group += 1
        if batch == 0:
            pl.semaphore_wait(barrier, lats)

        def send_far(i, carry, batch=batch):
            send(batch, (1 - side) * near + lax.rem(spot + near - i, near), 1).start()
            return carry

        def send_near(i, carry, batch=batch):
            send(batch, side * near + lax.rem(spot + near - i, near), 0).start()
            return carry

        lax.fori_loop(0, near, send_far, 0)
        lax.fori_loop(1, near, send_near, 0)

    first_order = spacing * assign_ref[2 * lat]
    second_order = spacing * assign_ref[2 * lat + 1]
    border = LMAX - first_order
    loads[1].wait()
    loads[2].wait()
    out_rows = syn.shape[1]
    packed = rep * half_pack + lax.broadcasted_iota(jnp.int32, (1, half_pack), 1)
    degree = jnp.where(packed >= border, second_order + packed - border, first_order + packed)
    quarter = (degree + 1) & 3
    cosine = jnp.where(quarter == 0, 1.0, jnp.where(quarter == 2, -1.0, 0.0))
    sine = jnp.where(quarter == 1, -1.0, jnp.where(quarter == 3, 1.0, 0.0))
    held = jnp.where(packed >= border, 1, 0)
    for k in range(2):
        values = syn[k].astype(jnp.float32)
        for slot_at in range(2):
            for turn, factor in enumerate((cosine, sine)):
                piece = (values * jnp.where(held == slot_at, factor, 0.0)).astype(jnp.bfloat16)
                for target in range(2):
                    begin = (((target ^ k) * 2 + slot_at) * 2 + turn) * out_rows
                    mix[target, begin : begin + out_rows, :] = piece

    own_rows = out_rows // lats
    shape = (out_rows, 128)
    row = lax.broadcasted_iota(jnp.int32, shape, 0)
    n = lax.broadcasted_iota(jnp.int32, shape, 1)
    for slot_at in range(2):
        order = orders_of((row // own_rows) * 2 + slot_at)
        weight = jnp.where(order == 0, 1.0, 2.0) * (1.0 / math.sqrt(2 * lats))
        for part_at in range(2):
            phase = lax.rem(order * n + part_at * (NLON_OUT // 4), NLON_OUT)
            wave = weight * jnp.cos(phase.astype(jnp.float32) * (2.0 * math.pi / NLON_OUT))
            begin = (part_at * 2 + slot_at) * out_rows
            for o in range(own_rows):
                inverse_ref[begin : begin + out_rows, o * 128 : (o + 1) * 128] = jnp.where(
                    lax.rem(row, own_rows) == o, wave, 0.0
                ).astype(jnp.bfloat16)

    halves = [pl.ds(pl.multiple_of(half * width, 128), width) for half in (side, 1 - side)]
    loads[3].wait()
    for far in range(2):
        total[far] = jnp.dot(mix[0], ana[0, :, halves[far]], preferred_element_type=jnp.float32)
    loads[4].wait()
    for far in range(2):
        value = total[far] + jnp.dot(mix[1], ana[1, :, halves[far]], preferred_element_type=jnp.float32)
        joined[far] = value.astype(jnp.bfloat16)

    arrived(0, 0)
    hand(rep, 0, 0).start()
    arrived(1, 0)
    hand(rep, 1, 0).start()
    arrived(0, 1)
    hand(rep, 0, 1).start()
    arrived(1, 1)
    hand(rep, 1, 1).start()
    hand(other, 0, 0).wait_recv()
    hand(other, 1, 0).wait_recv()
    synth = lax.dot_general(joined[0], spec[0], NT, preferred_element_type=jnp.float32)
    hand(other, 0, 1).wait_recv()
    hand(other, 1, 1).wait_recv()
    synth = synth + lax.dot_general(joined[1], spec[1], NT, preferred_element_type=jnp.float32)

    lane = lax.broadcasted_iota(jnp.int32, (1, 128), 1)
    lane_slot = (lane // GROUP) & 1
    part = (lane // (2 * GROUP)) & 1
    comp = lane // 64

    def swap_part(x):
        return jnp.where(part == 0, pltpu.roll(x, 128 - 2 * GROUP, 1), pltpu.roll(x, 2 * GROUP, 1))

    def swap_comp(x):
        return pltpu.roll(x, 64, 1)

    part_sign = jnp.where(part == 0, -1.0, 1.0)
    comp_sign = jnp.where(comp == 0, 1.0, -1.0)

    def turned(kind):
        both = [synth[(kind * 2 + k) * 2 * out_rows : (kind * 2 + k + 1) * 2 * out_rows] for k in range(2)]
        value = jnp.where(lane_slot == 0, both[0], both[1])
        return value[:out_rows] + part_sign * swap_part(value[out_rows:])

    rows = turned(0) - comp_sign * part_sign * swap_comp(swap_part(turned(1)))
    for k in range(lats):
        rows_out[k] = rows[k * own_rows : (k + 1) * own_rows]

    def row_copy(target_lat, target_rep):
        return pltpu.make_async_remote_copy(
            src_ref=rows_out.at[target_lat],
            dst_ref=rows_in.at[rep * lats + lat],
            send_sem=row_send,
            recv_sem=row_recv,
            device_id=(target_lat, target_rep),
            device_id_type=MESH,
        )

    def send_rows(i, carry):
        peer = lax.rem(lat + i, lats)
        row_copy(peer, rep).start()
        row_copy(peer, other).start()
        return carry

    lax.fori_loop(1, lats, send_rows, 0)
    row_copy(lat, other).start()
    rows_in[rep * lats + lat] = rows_out[lat]

    bulk(groups * (lats - 1), send_sem, recv_sem.at[0, 0]).wait_send()
    for last in range(2):
        for far in range(2):
            hand(rep, last, far).wait_send()

    all_rows = pltpu.make_async_remote_copy(
        src_ref=rows_in.at[pl.ds(0, 2 * lats - 1)],
        dst_ref=rows_in.at[pl.ds(0, 2 * lats - 1)],
        send_sem=row_send,
        recv_sem=row_recv,
        device_id=(lat, other),
        device_id_type=MESH,
    )
    all_rows.wait_recv()

    for k in range(lats):
        rows_sum[k * own_rows : (k + 1) * own_rows, :] = rows_in[k] + rows_in[lats + k]
    summed = rows_sum[...]
    gathered = [summed] + [pltpu.roll(summed, 128 - k * GROUP, 1) for k in range(1, 4)]
    gathered = jnp.concatenate(gathered, axis=0).astype(jnp.bfloat16)
    value = lax.dot_general(gathered, inverse_ref[...], TN, preferred_element_type=jnp.float32)
    for block in range(2 * groups):
        comp_at, group = block // groups, block % groups
        for o in range(own_rows):
            begin = (group * GROUP * 2 + comp_at) * own_rows + o
            out_ref[pl.ds(begin, GROUP, stride=2 * own_rows), :] = value[
                block * span : block * span + GROUP, o * 128 : (o + 1) * 128
            ]
    all_rows.wait_send()


def repeat_kernel(small_ref, out_hbm, wide, sem):
    value = small_ref[...]
    width = wide.shape[3]
    for k in range(width // 128):
        wide[:, :, :, k * 128 : (k + 1) * 128] = value
    copies = [
        pltpu.make_async_copy(wide, out_hbm.at[:, :, :, k * width : (k + 1) * width], sem.at[k])
        for k in range(out_hbm.shape[3] // width)
    ]
    for copy in copies:
        copy.start()
    for copy in copies:
        copy.wait()


def fast_body(near_field, assign, ana_v, ana_w, syn_v, syn_w):
    lats = lax.axis_size("lat")
    fields, comps, own_lat, length = near_field.shape
    order_count = assign.shape[0]
    half_pack = ana_v.shape[1]
    out_rows = syn_v.shape[2]
    own_rows = out_rows // lats
    hbm_spec = pl.BlockSpec(memory_space=pltpu.HBM)
    vmem_spec = pl.BlockSpec(memory_space=pltpu.VMEM)
    inputs = (assign, near_field, ana_v, ana_w, syn_v.swapaxes(1, 2), syn_w.swapaxes(1, 2))
    small = pl.pallas_call(
        functools.partial(kernel, lats, LMAX // order_count),
        out_shape=pltpu.VMEM((fields * 2 * own_rows, 128), jnp.float32),
        in_specs=[hbm_spec] * 6,
        out_specs=vmem_spec,
        scratch_shapes=[
            pltpu.SMEM((order_count,), jnp.int32),
            pltpu.VMEM((4 * lats, 256), jnp.bfloat16),
            pltpu.VMEM((4 * out_rows, own_rows * 128), jnp.bfloat16),
            pltpu.VMEM((fields, own_lat, length), jnp.bfloat16),
            pltpu.VMEM((2, half_pack, ana_v.shape[2]), jnp.bfloat16),
            pltpu.VMEM((2, out_rows, half_pack), jnp.bfloat16),
            pltpu.VMEM((2, 8 * out_rows, half_pack), jnp.bfloat16),
            pltpu.VMEM((128 * GROUP, 256), jnp.bfloat16),
            pltpu.VMEM((4 * lats * GROUP, 128), jnp.float32),
            [pltpu.VMEM((lats, 4 * GROUP * count, 128), jnp.bfloat16) for count in BATCHES],
            pltpu.VMEM((2, 8 * fields, lats // 2 * own_lat), jnp.bfloat16),
            pltpu.VMEM((2, 8 * out_rows, lats // 2 * own_lat), jnp.float32),
            pltpu.VMEM((2, 8 * out_rows, lats // 2 * own_lat), jnp.bfloat16),
            pltpu.VMEM((lats, own_rows, 128), jnp.float32),
            pltpu.VMEM((2 * lats, own_rows, 128), jnp.float32),
            pltpu.VMEM((lats * own_rows, 128), jnp.float32),
            pltpu.SemaphoreType.DMA((fields,)),
            pltpu.SemaphoreType.DMA((5,)),
            pltpu.SemaphoreType.DMA,
            pltpu.SemaphoreType.DMA((2, 2)),
            pltpu.SemaphoreType.DMA((2, 2)),
            pltpu.SemaphoreType.DMA((2, 2)),
            pltpu.SemaphoreType.DMA,
            pltpu.SemaphoreType.DMA,
        ],
        compiler_params=pltpu.CompilerParams(
            collective_id=0, has_side_effects=True, vmem_limit_bytes=40_000_000
        ),
    )(*(pltpu.with_memory_space_constraint(x, pltpu.HBM) for x in inputs))
    repeats = NLON_OUT // lax.axis_size("rep") // 128
    spread = 4
    return pl.pallas_call(
        repeat_kernel,
        out_shape=jax.ShapeDtypeStruct((fields, 2, own_rows, repeats * 128), jnp.float32),
        in_specs=[pl.BlockSpec(memory_space=pltpu.VMEM)],
        out_specs=hbm_spec,
        scratch_shapes=[
            pltpu.VMEM((fields, 2, own_rows, repeats // spread * 128), jnp.float32),
            pltpu.SemaphoreType.DMA((spread,)),
        ],
    )(pltpu.with_memory_space_constraint(small.reshape(fields, 2, own_rows, 128), pltpu.VMEM))


def fits(mesh, near_field, assign, ana_v, syn_v):
    lats = mesh.shape["lat"]
    fields, comps, rows, length = near_field.shape
    spacing = LMAX // assign.shape[0]
    return (
        mesh.shape["rep"] == 2
        and fields == 4 * GROUP
        and lats >= 4
        and comps == 2
        and lats & (lats - 1) == 0
        and rows == 128 * lats
        and assign.shape[0] == 2 * lats
        and 128 * spacing % length == 0
        and 128 * spacing % NLON_OUT == 0
        and syn_v.shape[2] == 32
        and ana_v.shape[1] % 64 == 0
    )


def solution(mesh):
    in_specs = (
        P(None, None, "lat", None),
        P(),
        P("lat", "rep", None),
        P("lat", "rep", None),
        P("lat", "rep", None),
        P("lat", "rep", None),
    )
    out_specs = P(None, None, "lat", "rep")

    def run(near_field, assign, ana_v, ana_w, syn_v, syn_w):
        chosen = fast_body if fits(mesh, near_field, assign, ana_v, syn_v) else plain_body
        mapped = jax.shard_map(chosen, mesh=mesh, in_specs=in_specs, out_specs=out_specs, check_vma=False)
        return mapped(near_field, assign, ana_v, ana_w, syn_v, syn_w)

    return run
```

```python
import functools
import math

import jax
import jax.numpy as jnp
from jax import lax
from jax.experimental import pallas as pl
from jax.experimental.pallas import tpu as pltpu
from jax.sharding import PartitionSpec as P

LMAX = 2048
NLON_OUT = 8192


def forward_table(orders, length):
    column = jnp.arange(length, dtype=jnp.int32)
    phase_index = orders[:, None] * column[None, :] % length
    angles = phase_index.astype(jnp.float32) * (2.0 * math.pi / length)
    factor = 1.0 / math.sqrt(length)
    stacked = jnp.stack([jnp.cos(angles) * factor, -jnp.sin(angles) * factor], axis=1)
    return stacked.reshape(2 * orders.shape[0], length).astype(jnp.bfloat16)


def inverse_table(orders, begin, count, length):
    column = begin + jnp.arange(count, dtype=jnp.int32)
    phase_index = orders[:, None] * column[None, :] % length
    angles = phase_index.astype(jnp.float32) * (2.0 * math.pi / length)
    weight = jnp.where(orders == 0, 1.0, 2.0).astype(jnp.float32)[:, None] / math.sqrt(
        orders.shape[0]
    )
    stacked = jnp.stack([weight * jnp.cos(angles), -weight * jnp.sin(angles)], axis=1)
    return stacked.reshape(2 * orders.shape[0], count).astype(jnp.bfloat16)


def pad_rows(matrix, tile_count, tile_rows):
    missing = tile_count * tile_rows - matrix.shape[0]
    return jnp.pad(matrix, ((0, missing), (0, 0))).reshape(tile_count, tile_rows, matrix.shape[1])


def legendre(spectra, mat_av, mat_aw, mat_sv, mat_sw, packed_start, first_order, second_order):
    count = spectra.shape[1]
    flat = spectra.reshape(2, 4 * count, spectra.shape[3])
    tile_rows = 128
    tile_count = -(-mat_av.shape[0] // tile_rows)
    out_rows = mat_sv.shape[1]
    border = LMAX - first_order

    def step(carry, inputs_now):
        total_v, total_w = carry
        number, tile_av, tile_aw, tile_sv, tile_sw = inputs_now
        first_row = packed_start + number * tile_rows
        packed = first_row + jnp.arange(tile_rows, dtype=jnp.int32)
        second = packed >= border
        branch_kind = jnp.where(
            first_row >= border, 1, jnp.where(first_row + tile_rows - 1 < border, 0, 2)
        )

        def single_slot(slot):

            def compute():
                slot_flat = flat[slot]
                part_v = jnp.dot(tile_av, slot_flat.T, preferred_element_type=jnp.float32).reshape(
                    tile_rows, 2, count, 2
                )
                part_w = jnp.dot(tile_aw, slot_flat.T, preferred_element_type=jnp.float32).reshape(
                    tile_rows, 2, count, 2
                )
                return (part_v, part_w)

            return compute

        def both_slots():
            first_v, first_w = single_slot(0)()
            second_v, second_w = single_slot(1)()
            choose_second = second[:, None, None, None]
            return (
                jnp.where(choose_second, second_v, first_v),
                jnp.where(choose_second, second_w, first_w),
            )

        chosen_v, chosen_w = lax.switch(branch_kind, [single_slot(0), single_slot(1), both_slots])
        degree = jnp.where(second, second_order + packed - border, first_order + packed)
        sph_re = chosen_v[:, 0, :, 0] + chosen_w[:, 1, :, 1]
        sph_im = chosen_v[:, 1, :, 0] - chosen_w[:, 0, :, 1]
        tor_re = chosen_w[:, 1, :, 0] - chosen_v[:, 0, :, 1]
        tor_im = -chosen_w[:, 0, :, 0] - chosen_v[:, 1, :, 1]
        quarter = (degree + 1) % 4
        cosine = jnp.where(quarter == 0, 1.0, jnp.where(quarter == 2, -1.0, 0.0)).astype(
            jnp.float32
        )[:, None]
        sine = jnp.where(quarter == 1, -1.0, jnp.where(quarter == 3, 1.0, 0.0)).astype(jnp.float32)[
            :, None
        ]
        coeffs = jnp.stack(
            [
                cosine * sph_re - sine * sph_im,
                cosine * sph_im + sine * sph_re,
                cosine * tor_re - sine * tor_im,
                cosine * tor_im + sine * tor_re,
            ],
            axis=1,
        ).astype(jnp.bfloat16)
        flat_coeffs = coeffs.reshape(tile_rows, 4 * count)
        second_mask = second.astype(jnp.bfloat16)[:, None]

        def mixed_rows():
            lower_c = flat_coeffs * (1 - second_mask)
            upper_c = flat_coeffs * second_mask
            add_v = jnp.stack(
                [
                    jnp.dot(lower_c.T, tile_sv, preferred_element_type=jnp.float32),
                    jnp.dot(upper_c.T, tile_sv, preferred_element_type=jnp.float32),
                ]
            )
            add_w = jnp.stack(
                [
                    jnp.dot(lower_c.T, tile_sw, preferred_element_type=jnp.float32),
                    jnp.dot(upper_c.T, tile_sw, preferred_element_type=jnp.float32),
                ]
            )
            return (add_v, add_w)

        def single_rows():
            part_v = jnp.dot(flat_coeffs.T, tile_sv, preferred_element_type=jnp.float32)
            part_w = jnp.dot(flat_coeffs.T, tile_sw, preferred_element_type=jnp.float32)
            upper_pick = (branch_kind == 1).astype(jnp.float32)
            return (
                jnp.stack([part_v * (1.0 - upper_pick), part_v * upper_pick]),
                jnp.stack([part_w * (1.0 - upper_pick), part_w * upper_pick]),
            )

        add_v, add_w = lax.cond(branch_kind == 2, mixed_rows, single_rows)
        return ((total_v + add_v, total_w + add_w), None)

    start_v = jnp.zeros((2, 4 * count, out_rows), jnp.float32)
    start_w = jnp.zeros((2, 4 * count, out_rows), jnp.float32)
    numbers = jnp.arange(tile_count, dtype=jnp.int32)
    (total_v, total_w), unused = lax.scan(
        step,
        (start_v, start_w),
        (
            numbers,
            pad_rows(mat_av, tile_count, tile_rows),
            pad_rows(mat_aw, tile_count, tile_rows),
            pad_rows(mat_sv, tile_count, tile_rows),
            pad_rows(mat_sw, tile_count, tile_rows),
        ),
    )
    synth_v = total_v.reshape(2, 4, count, -1)
    synth_w = total_w.reshape(2, 4, count, -1)
    theta_re = synth_v[:, 0] - synth_w[:, 3]
    theta_im = synth_v[:, 1] + synth_w[:, 2]
    phi_re = -synth_w[:, 1] - synth_v[:, 2]
    phi_im = synth_w[:, 0] - synth_v[:, 3]
    real_part = jnp.stack([theta_re, phi_re], axis=2)
    imag_part = jnp.stack([theta_im, phi_im], axis=2)
    return jnp.stack([real_part, imag_part], axis=1).reshape(4, count, 2, -1)


def plain_body(near_field, assign, ana_v, ana_w, syn_v, syn_w):
    order_count = assign.shape[0]
    spacing = LMAX // order_count
    orders = spacing * assign
    pair_orders = lax.dynamic_slice_in_dim(orders, 2 * lax.axis_index("lat"), 2, 0)
    half_pack = ana_v.shape[1]
    packed_start = lax.axis_index("rep") * half_pack
    table = forward_table(orders, near_field.shape[3])
    spectrum = jnp.einsum(
        "jk,fctk->jfct", table, near_field, preferred_element_type=jnp.float32
    ).astype(jnp.bfloat16)
    partial_value = legendre(
        lax.all_to_all(spectrum, "lat", split_axis=0, concat_axis=3, tiled=True),
        ana_v[0],
        ana_w[0],
        syn_v[0],
        syn_w[0],
        packed_start,
        pair_orders[0],
        pair_orders[1],
    )
    summed = lax.psum(partial_value, "rep").astype(jnp.bfloat16)
    regrouped = lax.all_to_all(summed, "lat", split_axis=3, concat_axis=0, tiled=True)
    longitudes = NLON_OUT // lax.axis_size("rep")
    inverse = inverse_table(orders, lax.axis_index("rep") * longitudes, longitudes, NLON_OUT)
    return jnp.einsum("jfcr,jp->fcrp", regrouped, inverse, preferred_element_type=jnp.float32)

MESH = pl.DeviceIdType.MESH
GROUP = 4
BATCHES = (2, 1, 1)
NT = (((1,), (1,)), ((), ()))
TN = (((0,), (0,)), ((), ()))


def kernel(
    lats,
    spacing,
    assign_hbm,
    field_hbm,
    av_hbm,
    aw_hbm,
    sv_hbm,
    sw_hbm,
    out_ref,
    assign_ref,
    table_ref,
    inverse_ref,
    ring,
    ana,
    syn,
    mix,
    folded,
    staged,
    packets,
    spec,
    total,
    joined,
    theirs,
    rows_out,
    rows_in,
    rows_sum,
    field_sem,
    load_sem,
    send_sem,
    recv_sem,
    pass_send,
    pass_recv,
    row_send,
    row_recv,
):
    lat = lax.axis_index("lat")
    rep = lax.axis_index("rep")
    other = 1 - rep
    fields = field_hbm.shape[0]
    groups = fields // GROUP
    half_pack = ana.shape[1]
    span = 4 * GROUP
    near = lats // 2
    side = lat // near
    spot = lax.rem(lat, near)
    width = near * 128

    def fetch(f):
        return pltpu.make_async_copy(field_hbm.at[f, rep], ring.at[f], field_sem.at[f])

    loads = [
        pltpu.make_async_copy(assign_hbm, assign_ref, load_sem.at[0]),
        pltpu.make_async_copy(sv_hbm.at[0], syn.at[0], load_sem.at[1]),
        pltpu.make_async_copy(sw_hbm.at[0], syn.at[1], load_sem.at[2]),
        pltpu.make_async_copy(av_hbm.at[0], ana.at[0], load_sem.at[3]),
        pltpu.make_async_copy(aw_hbm.at[0], ana.at[1], load_sem.at[4]),
    ]
    barrier = pltpu.get_barrier_semaphore()

    def greet(i, carry):
        peer = lax.rem(lat + i, lats)
        pl.semaphore_signal(barrier, inc=1, device_id=(peer, rep), device_id_type=MESH)
        pl.semaphore_signal(barrier, inc=1, device_id=(peer, other), device_id_type=MESH)
        return carry

    pl.semaphore_signal(barrier, inc=1, device_id=(lat, other), device_id_type=MESH)
    lax.fori_loop(1, lats, greet, 0)

    loads[0].start()
    for f in range(GROUP):
        fetch(f).start()

    for f in range(GROUP, fields):
        fetch(f).start()
    for load in loads[1:]:
        load.start()

    loads[0].wait()
    length = field_hbm.shape[3]

    def orders_of(index):
        order = jnp.zeros(index.shape, jnp.int32)
        for k in range(2 * lats):
            order = jnp.where(index == k, spacing * assign_ref[k], order)
        return order

    shape = (4 * lats, 128)
    row = lax.broadcasted_iota(jnp.int32, shape, 0)
    phase = orders_of((row // 4) * 2 + (row & 1)) * lax.broadcasted_iota(jnp.int32, shape, 1)
    phase = lax.rem(phase + ((row // 2) & 1) * (length // 4), length)
    wave = jnp.cos(phase.astype(jnp.float32) * (2.0 * math.pi / length)) * (1.0 / math.sqrt(length))
    wave = wave.astype(jnp.bfloat16)
    table_ref[:, 0:128] = wave
    table_ref[:, 128:256] = wave

    def send(batch, peer):
        first, count = sum(BATCHES[:batch]), BATCHES[batch]
        return pltpu.make_async_remote_copy(
            src_ref=packets[batch].at[peer],
            dst_ref=spec.at[
                pl.ds(pl.multiple_of((rep * groups + first) * span, span), count * span),
                pl.ds(pl.multiple_of(spot * 128, 128), 128),
            ],
            send_sem=send_sem,
            recv_sem=recv_sem,
            device_id=(peer, side),
            device_id_type=MESH,
        )

    def bulk(blocks, send_at, recv_at):
        tall = 1
        while blocks % tall or blocks // tall * 128 > ring.shape[2]:
            tall += 1
        like = ring.at[0, pl.ds(0, tall * span), pl.ds(0, blocks // tall * 128)]
        return pltpu.make_async_remote_copy(
            src_ref=like,
            dst_ref=like,
            send_sem=send_at,
            recv_sem=recv_at,
            device_id=(lat, other),
            device_id_type=MESH,
        )

    share = pltpu.make_async_remote_copy(
        src_ref=joined,
        dst_ref=theirs,
        send_sem=pass_send,
        recv_sem=pass_recv,
        device_id=(lat, other),
        device_id_type=MESH,
    )

    def fold(f, carry):
        fetch(f).wait()
        total_f = ring[f, :, 0:128].astype(jnp.float32)
        for piece in range(1, ring.shape[2] // 128):
            total_f = total_f + ring[f, :, piece * 128 : (piece + 1) * 128].astype(jnp.float32)
        high = total_f.astype(jnp.bfloat16)
        low = (total_f - high.astype(jnp.float32)).astype(jnp.bfloat16)
        begin = pl.multiple_of(lax.rem(f, GROUP) * 128, 128)
        folded[pl.ds(begin, 128), 0:128] = high
        folded[pl.ds(begin, 128), 128:256] = low
        return carry

    group = 0
    for batch, count in enumerate(BATCHES):
        for member in range(count):
            lax.fori_loop(group * GROUP, (group + 1) * GROUP, fold, 0)
            value = lax.dot_general(table_ref[...], folded[...], NT, preferred_element_type=jnp.float32)
            for k in range(GROUP):
                staged[pl.ds(k, 4 * lats, stride=GROUP), :] = value[:, k * 128 : (k + 1) * 128]
            packets[batch][:, member * span : (member + 1) * span, :] = (
                staged[...].astype(jnp.bfloat16).reshape(lats, span, 128)
            )
            group += 1
        if batch == 0:
            pl.semaphore_wait(barrier, 2 * lats - 1)

        def send_far(i, carry, batch=batch):
            send(batch, (1 - side) * near + lax.rem(spot + near - i, near)).start()
            return carry

        def send_near(i, carry, batch=batch):
            send(batch, side * near + lax.rem(spot + near - i, near)).start()
            return carry

        lax.fori_loop(0, near, send_far, 0)
        lax.fori_loop(1, near, send_near, 0)

        @pl.when(side == rep)
        def _(batch=batch):
            first, count = sum(BATCHES[:batch]), BATCHES[batch]
            spec[
                pl.ds(pl.multiple_of((rep * groups + first) * span, span), count * span),
                pl.ds(pl.multiple_of(spot * 128, 128), 128),
            ] = packets[batch][lat]

        @pl.when(side != rep)
        def _(batch=batch):
            send(batch, lat).start()

    first_order = spacing * assign_ref[2 * lat]
    second_order = spacing * assign_ref[2 * lat + 1]
    border = LMAX - first_order
    loads[1].wait()
    loads[2].wait()
    out_rows = syn.shape[1]
    packed = rep * half_pack + lax.broadcasted_iota(jnp.int32, (1, half_pack), 1)
    degree = jnp.where(packed >= border, second_order + packed - border, first_order + packed)
    quarter = (degree + 1) & 3
    cosine = jnp.where(quarter == 0, 1.0, jnp.where(quarter == 2, -1.0, 0.0))
    sine = jnp.where(quarter == 1, -1.0, jnp.where(quarter == 3, 1.0, 0.0))
    held = jnp.where(packed >= border, 1, 0)
    for k in range(2):
        values = syn[k].astype(jnp.float32)
        for slot_at in range(2):
            for turn, factor in enumerate((cosine, sine)):
                piece = (values * jnp.where(held == slot_at, factor, 0.0)).astype(jnp.bfloat16)
                for target in range(2):
                    begin = (((target ^ k) * 2 + slot_at) * 2 + turn) * out_rows
                    mix[target, begin : begin + out_rows, :] = piece

    halves = [pl.ds(pl.multiple_of(half * width, 128), width) for half in (other, rep)]
    loads[3].wait()
    for k in range(2):
        total[k] = jnp.dot(mix[0], ana[0, :, halves[k]], preferred_element_type=jnp.float32)
    loads[4].wait()
    value = total[0] + jnp.dot(mix[1], ana[1, :, halves[0]], preferred_element_type=jnp.float32)
    joined[...] = value.astype(jnp.bfloat16)
    share.start()
    total[1] = total[1] + jnp.dot(mix[1], ana[1, :, halves[1]], preferred_element_type=jnp.float32)

    own_rows = out_rows // lats
    shape = (out_rows, 128)
    row = lax.broadcasted_iota(jnp.int32, shape, 0)
    n = lax.broadcasted_iota(jnp.int32, shape, 1)
    for slot_at in range(2):
        order = orders_of((row // own_rows) * 2 + slot_at)
        weight = jnp.where(order == 0, 1.0, 2.0) * (1.0 / math.sqrt(2 * lats))
        for part_at in range(2):
            phase = lax.rem(order * n + part_at * (NLON_OUT // 4), NLON_OUT)
            wave = weight * jnp.cos(phase.astype(jnp.float32) * (2.0 * math.pi / NLON_OUT))
            begin = (part_at * 2 + slot_at) * out_rows
            for o in range(own_rows):
                inverse_ref[begin : begin + out_rows, o * 128 : (o + 1) * 128] = jnp.where(
                    lax.rem(row, own_rows) == o, wave, 0.0
                ).astype(jnp.bfloat16)

    share.wait_recv()
    theirs[...] = (total[1] + theirs[...].astype(jnp.float32)).astype(jnp.bfloat16)

    @pl.when(side == rep)
    def _():
        bulk(groups * (2 * near - 1), send_sem, recv_sem).wait_recv()

    @pl.when(side != rep)
    def _():
        bulk(groups * 2 * near, send_sem, recv_sem).wait_recv()

    synth = lax.dot_general(theirs[...], spec[...], NT, preferred_element_type=jnp.float32)

    lane = lax.broadcasted_iota(jnp.int32, (1, 128), 1)
    lane_slot = (lane // GROUP) & 1
    part = (lane // (2 * GROUP)) & 1
    comp = lane // 64

    def swap_part(x):
        return jnp.where(part == 0, pltpu.roll(x, 128 - 2 * GROUP, 1), pltpu.roll(x, 2 * GROUP, 1))

    def swap_comp(x):
        return pltpu.roll(x, 64, 1)

    part_sign = jnp.where(part == 0, -1.0, 1.0)
    comp_sign = jnp.where(comp == 0, 1.0, -1.0)

    def turned(kind):
        both = [synth[(kind * 2 + k) * 2 * out_rows : (kind * 2 + k + 1) * 2 * out_rows] for k in range(2)]
        value = jnp.where(lane_slot == 0, both[0], both[1])
        return value[:out_rows] + part_sign * swap_part(value[out_rows:])

    rows = turned(0) - comp_sign * part_sign * swap_comp(swap_part(turned(1)))
    for k in range(lats):
        rows_out[k] = rows[k * own_rows : (k + 1) * own_rows]

    def row_copy(target_lat, target_rep):
        return pltpu.make_async_remote_copy(
            src_ref=rows_out.at[target_lat],
            dst_ref=rows_in.at[rep * lats + lat],
            send_sem=row_send,
            recv_sem=row_recv,
            device_id=(target_lat, target_rep),
            device_id_type=MESH,
        )

    def send_rows(i, carry):
        peer = lax.rem(lat + i, lats)
        row_copy(peer, rep).start()
        row_copy(peer, other).start()
        return carry

    lax.fori_loop(1, lats, send_rows, 0)
    row_copy(lat, other).start()
    rows_in[rep * lats + lat] = rows_out[lat]

    share.wait_send()

    @pl.when(side == rep)
    def _():
        bulk(groups * (lats - 1), send_sem, recv_sem).wait_send()

    @pl.when(side != rep)
    def _():
        bulk(groups * lats, send_sem, recv_sem).wait_send()

    all_rows = pltpu.make_async_remote_copy(
        src_ref=rows_in.at[pl.ds(0, 2 * lats - 1)],
        dst_ref=rows_in.at[pl.ds(0, 2 * lats - 1)],
        send_sem=row_send,
        recv_sem=row_recv,
        device_id=(lat, other),
        device_id_type=MESH,
    )
    all_rows.wait_recv()

    for k in range(lats):
        rows_sum[k * own_rows : (k + 1) * own_rows, :] = rows_in[k] + rows_in[lats + k]
    summed = rows_sum[...]
    gathered = [summed] + [pltpu.roll(summed, 128 - k * GROUP, 1) for k in range(1, 4)]
    gathered = jnp.concatenate(gathered, axis=0).astype(jnp.bfloat16)
    value = lax.dot_general(gathered, inverse_ref[...], TN, preferred_element_type=jnp.float32)
    for block in range(2 * groups):
        comp_at, group = block // groups, block % groups
        for o in range(own_rows):
            begin = (group * GROUP * 2 + comp_at) * own_rows + o
            out_ref[pl.ds(begin, GROUP, stride=2 * own_rows), :] = value[
                block * span : block * span + GROUP, o * 128 : (o + 1) * 128
            ]
    all_rows.wait_send()


def repeat_kernel(small_ref, out_hbm, wide, sem):
    value = small_ref[...]
    width = wide.shape[3]
    for k in range(width // 128):
        wide[:, :, :, k * 128 : (k + 1) * 128] = value
    copies = [
        pltpu.make_async_copy(wide, out_hbm.at[:, :, :, k * width : (k + 1) * width], sem.at[k])
        for k in range(out_hbm.shape[3] // width)
    ]
    for copy in copies:
        copy.start()
    for copy in copies:
        copy.wait()


def fast_body(near_field, assign, ana_v, ana_w, syn_v, syn_w):
    lats = lax.axis_size("lat")
    fields, comps, own_lat, length = near_field.shape
    order_count = assign.shape[0]
    half_pack = ana_v.shape[1]
    out_rows = syn_v.shape[2]
    own_rows = out_rows // lats
    hbm_spec = pl.BlockSpec(memory_space=pltpu.HBM)
    vmem_spec = pl.BlockSpec(memory_space=pltpu.VMEM)
    inputs = (assign, near_field, ana_v, ana_w, syn_v.swapaxes(1, 2), syn_w.swapaxes(1, 2))
    small = pl.pallas_call(
        functools.partial(kernel, lats, LMAX // order_count),
        out_shape=pltpu.VMEM((fields * 2 * own_rows, 128), jnp.float32),
        in_specs=[hbm_spec] * 6,
        out_specs=vmem_spec,
        scratch_shapes=[
            pltpu.SMEM((order_count,), jnp.int32),
            pltpu.VMEM((4 * lats, 256), jnp.bfloat16),
            pltpu.VMEM((4 * out_rows, own_rows * 128), jnp.bfloat16),
            pltpu.VMEM((fields, own_lat, length), jnp.bfloat16),
            pltpu.VMEM((2, half_pack, ana_v.shape[2]), jnp.bfloat16),
            pltpu.VMEM((2, out_rows, half_pack), jnp.bfloat16),
            pltpu.VMEM((2, 8 * out_rows, half_pack), jnp.bfloat16),
            pltpu.VMEM((128 * GROUP, 256), jnp.bfloat16),
            pltpu.VMEM((4 * lats * GROUP, 128), jnp.float32),
            [pltpu.VMEM((lats, 4 * GROUP * count, 128), jnp.bfloat16) for count in BATCHES],
            pltpu.VMEM((8 * fields, lats // 2 * own_lat), jnp.bfloat16),
            pltpu.VMEM((2, 8 * out_rows, lats // 2 * own_lat), jnp.float32),
            pltpu.VMEM((8 * out_rows, lats // 2 * own_lat), jnp.bfloat16),
            pltpu.VMEM((8 * out_rows, lats // 2 * own_lat), jnp.bfloat16),
            pltpu.VMEM((lats, own_rows, 128), jnp.float32),
            pltpu.VMEM((2 * lats, own_rows, 128), jnp.float32),
            pltpu.VMEM((lats * own_rows, 128), jnp.float32),
            pltpu.SemaphoreType.DMA((fields,)),
            pltpu.SemaphoreType.DMA((5,)),
            pltpu.SemaphoreType.DMA,
            pltpu.SemaphoreType.DMA,
            pltpu.SemaphoreType.DMA,
            pltpu.SemaphoreType.DMA,
            pltpu.SemaphoreType.DMA,
            pltpu.SemaphoreType.DMA,
        ],
        compiler_params=pltpu.CompilerParams(
            collective_id=0, has_side_effects=True, vmem_limit_bytes=40_000_000
        ),
    )(*(pltpu.with_memory_space_constraint(x, pltpu.HBM) for x in inputs))
    repeats = NLON_OUT // lax.axis_size("rep") // 128
    spread = 4
    return pl.pallas_call(
        repeat_kernel,
        out_shape=jax.ShapeDtypeStruct((fields, 2, own_rows, repeats * 128), jnp.float32),
        in_specs=[pl.BlockSpec(memory_space=pltpu.VMEM)],
        out_specs=hbm_spec,
        scratch_shapes=[
            pltpu.VMEM((fields, 2, own_rows, repeats // spread * 128), jnp.float32),
            pltpu.SemaphoreType.DMA((spread,)),
        ],
    )(pltpu.with_memory_space_constraint(small.reshape(fields, 2, own_rows, 128), pltpu.VMEM))


def fits(mesh, near_field, assign, ana_v, syn_v):
    lats = mesh.shape["lat"]
    fields, comps, rows, length = near_field.shape
    spacing = LMAX // assign.shape[0]
    return (
        mesh.shape["rep"] == 2
        and fields == 4 * GROUP
        and lats >= 4
        and comps == 2
        and lats & (lats - 1) == 0
        and rows == 128 * lats
        and assign.shape[0] == 2 * lats
        and 128 * spacing % length == 0
        and 128 * spacing % NLON_OUT == 0
        and syn_v.shape[2] == 32
        and ana_v.shape[1] % 64 == 0
    )


def solution(mesh):
    in_specs = (
        P(None, None, "lat", None),
        P(),
        P("lat", "rep", None),
        P("lat", "rep", None),
        P("lat", "rep", None),
        P("lat", "rep", None),
    )
    out_specs = P(None, None, "lat", "rep")

    def run(near_field, assign, ana_v, ana_w, syn_v, syn_w):
        chosen = fast_body if fits(mesh, near_field, assign, ana_v, syn_v) else plain_body
        mapped = jax.shard_map(chosen, mesh=mesh, in_specs=in_specs, out_specs=out_specs, check_vma=False)
        return mapped(near_field, assign, ana_v, ana_w, syn_v, syn_w)

    return run
```

```python
import functools
import math

import jax
import jax.numpy as jnp
from jax import lax
from jax.experimental import pallas as pl
from jax.experimental.pallas import tpu as pltpu
from jax.sharding import PartitionSpec as P

LMAX = 2048
NLON_OUT = 8192


def forward_table(orders, length):
    column = jnp.arange(length, dtype=jnp.int32)
    phase_index = orders[:, None] * column[None, :] % length
    angles = phase_index.astype(jnp.float32) * (2.0 * math.pi / length)
    factor = 1.0 / math.sqrt(length)
    stacked = jnp.stack([jnp.cos(angles) * factor, -jnp.sin(angles) * factor], axis=1)
    return stacked.reshape(2 * orders.shape[0], length).astype(jnp.bfloat16)


def inverse_table(orders, begin, count, length):
    column = begin + jnp.arange(count, dtype=jnp.int32)
    phase_index = orders[:, None] * column[None, :] % length
    angles = phase_index.astype(jnp.float32) * (2.0 * math.pi / length)
    weight = jnp.where(orders == 0, 1.0, 2.0).astype(jnp.float32)[:, None] / math.sqrt(
        orders.shape[0]
    )
    stacked = jnp.stack([weight * jnp.cos(angles), -weight * jnp.sin(angles)], axis=1)
    return stacked.reshape(2 * orders.shape[0], count).astype(jnp.bfloat16)


def pad_rows(matrix, tile_count, tile_rows):
    missing = tile_count * tile_rows - matrix.shape[0]
    return jnp.pad(matrix, ((0, missing), (0, 0))).reshape(tile_count, tile_rows, matrix.shape[1])


def legendre(spectra, mat_av, mat_aw, mat_sv, mat_sw, packed_start, first_order, second_order):
    count = spectra.shape[1]
    flat = spectra.reshape(2, 4 * count, spectra.shape[3])
    tile_rows = 128
    tile_count = -(-mat_av.shape[0] // tile_rows)
    out_rows = mat_sv.shape[1]
    border = LMAX - first_order

    def step(carry, inputs_now):
        total_v, total_w = carry
        number, tile_av, tile_aw, tile_sv, tile_sw = inputs_now
        first_row = packed_start + number * tile_rows
        packed = first_row + jnp.arange(tile_rows, dtype=jnp.int32)
        second = packed >= border
        branch_kind = jnp.where(
            first_row >= border, 1, jnp.where(first_row + tile_rows - 1 < border, 0, 2)
        )

        def single_slot(slot):

            def compute():
                slot_flat = flat[slot]
                part_v = jnp.dot(tile_av, slot_flat.T, preferred_element_type=jnp.float32).reshape(
                    tile_rows, 2, count, 2
                )
                part_w = jnp.dot(tile_aw, slot_flat.T, preferred_element_type=jnp.float32).reshape(
                    tile_rows, 2, count, 2
                )
                return (part_v, part_w)

            return compute

        def both_slots():
            first_v, first_w = single_slot(0)()
            second_v, second_w = single_slot(1)()
            choose_second = second[:, None, None, None]
            return (
                jnp.where(choose_second, second_v, first_v),
                jnp.where(choose_second, second_w, first_w),
            )

        chosen_v, chosen_w = lax.switch(branch_kind, [single_slot(0), single_slot(1), both_slots])
        degree = jnp.where(second, second_order + packed - border, first_order + packed)
        sph_re = chosen_v[:, 0, :, 0] + chosen_w[:, 1, :, 1]
        sph_im = chosen_v[:, 1, :, 0] - chosen_w[:, 0, :, 1]
        tor_re = chosen_w[:, 1, :, 0] - chosen_v[:, 0, :, 1]
        tor_im = -chosen_w[:, 0, :, 0] - chosen_v[:, 1, :, 1]
        quarter = (degree + 1) % 4
        cosine = jnp.where(quarter == 0, 1.0, jnp.where(quarter == 2, -1.0, 0.0)).astype(
            jnp.float32
        )[:, None]
        sine = jnp.where(quarter == 1, -1.0, jnp.where(quarter == 3, 1.0, 0.0)).astype(jnp.float32)[
            :, None
        ]
        coeffs = jnp.stack(
            [
                cosine * sph_re - sine * sph_im,
                cosine * sph_im + sine * sph_re,
                cosine * tor_re - sine * tor_im,
                cosine * tor_im + sine * tor_re,
            ],
            axis=1,
        ).astype(jnp.bfloat16)
        flat_coeffs = coeffs.reshape(tile_rows, 4 * count)
        second_mask = second.astype(jnp.bfloat16)[:, None]

        def mixed_rows():
            lower_c = flat_coeffs * (1 - second_mask)
            upper_c = flat_coeffs * second_mask
            add_v = jnp.stack(
                [
                    jnp.dot(lower_c.T, tile_sv, preferred_element_type=jnp.float32),
                    jnp.dot(upper_c.T, tile_sv, preferred_element_type=jnp.float32),
                ]
            )
            add_w = jnp.stack(
                [
                    jnp.dot(lower_c.T, tile_sw, preferred_element_type=jnp.float32),
                    jnp.dot(upper_c.T, tile_sw, preferred_element_type=jnp.float32),
                ]
            )
            return (add_v, add_w)

        def single_rows():
            part_v = jnp.dot(flat_coeffs.T, tile_sv, preferred_element_type=jnp.float32)
            part_w = jnp.dot(flat_coeffs.T, tile_sw, preferred_element_type=jnp.float32)
            upper_pick = (branch_kind == 1).astype(jnp.float32)
            return (
                jnp.stack([part_v * (1.0 - upper_pick), part_v * upper_pick]),
                jnp.stack([part_w * (1.0 - upper_pick), part_w * upper_pick]),
            )

        add_v, add_w = lax.cond(branch_kind == 2, mixed_rows, single_rows)
        return ((total_v + add_v, total_w + add_w), None)

    start_v = jnp.zeros((2, 4 * count, out_rows), jnp.float32)
    start_w = jnp.zeros((2, 4 * count, out_rows), jnp.float32)
    numbers = jnp.arange(tile_count, dtype=jnp.int32)
    (total_v, total_w), unused = lax.scan(
        step,
        (start_v, start_w),
        (
            numbers,
            pad_rows(mat_av, tile_count, tile_rows),
            pad_rows(mat_aw, tile_count, tile_rows),
            pad_rows(mat_sv, tile_count, tile_rows),
            pad_rows(mat_sw, tile_count, tile_rows),
        ),
    )
    synth_v = total_v.reshape(2, 4, count, -1)
    synth_w = total_w.reshape(2, 4, count, -1)
    theta_re = synth_v[:, 0] - synth_w[:, 3]
    theta_im = synth_v[:, 1] + synth_w[:, 2]
    phi_re = -synth_w[:, 1] - synth_v[:, 2]
    phi_im = synth_w[:, 0] - synth_v[:, 3]
    real_part = jnp.stack([theta_re, phi_re], axis=2)
    imag_part = jnp.stack([theta_im, phi_im], axis=2)
    return jnp.stack([real_part, imag_part], axis=1).reshape(4, count, 2, -1)


def plain_body(near_field, assign, ana_v, ana_w, syn_v, syn_w):
    order_count = assign.shape[0]
    spacing = LMAX // order_count
    orders = spacing * assign
    pair_orders = lax.dynamic_slice_in_dim(orders, 2 * lax.axis_index("lat"), 2, 0)
    half_pack = ana_v.shape[1]
    packed_start = lax.axis_index("rep") * half_pack
    table = forward_table(orders, near_field.shape[3])
    spectrum = jnp.einsum(
        "jk,fctk->jfct", table, near_field, preferred_element_type=jnp.float32
    ).astype(jnp.bfloat16)
    partial_value = legendre(
        lax.all_to_all(spectrum, "lat", split_axis=0, concat_axis=3, tiled=True),
        ana_v[0],
        ana_w[0],
        syn_v[0],
        syn_w[0],
        packed_start,
        pair_orders[0],
        pair_orders[1],
    )
    summed = lax.psum(partial_value, "rep").astype(jnp.bfloat16)
    regrouped = lax.all_to_all(summed, "lat", split_axis=3, concat_axis=0, tiled=True)
    longitudes = NLON_OUT // lax.axis_size("rep")
    inverse = inverse_table(orders, lax.axis_index("rep") * longitudes, longitudes, NLON_OUT)
    return jnp.einsum("jfcr,jp->fcrp", regrouped, inverse, preferred_element_type=jnp.float32)

MESH = pl.DeviceIdType.MESH
GROUP = 4
BATCHES = (2, 1, 1)
NT = (((1,), (1,)), ((), ()))
TN = (((0,), (0,)), ((), ()))


def kernel(
    lats,
    spacing,
    assign_hbm,
    field_hbm,
    av_hbm,
    aw_hbm,
    sv_hbm,
    sw_hbm,
    out_ref,
    assign_ref,
    table_ref,
    inverse_ref,
    ring,
    ana,
    syn,
    mix,
    folded,
    staged,
    packets,
    spec,
    total,
    joined,
    theirs,
    rows_out,
    rows_in,
    rows_sum,
    field_sem,
    load_sem,
    send_sem,
    recv_sem,
    pass_send,
    pass_recv,
    row_send,
    row_recv,
):
    lat = lax.axis_index("lat")
    rep = lax.axis_index("rep")
    other = 1 - rep
    fields = field_hbm.shape[0]
    groups = fields // GROUP
    half_pack = ana.shape[1]
    span = 4 * GROUP
    near = lats // 2
    side = lat // near
    spot = lax.rem(lat, near)
    width = near * 128

    def fetch(f):
        return pltpu.make_async_copy(field_hbm.at[f, rep], ring.at[f], field_sem.at[f])

    loads = [
        pltpu.make_async_copy(assign_hbm, assign_ref, load_sem.at[0]),
        pltpu.make_async_copy(sv_hbm.at[0], syn.at[0], load_sem.at[1]),
        pltpu.make_async_copy(sw_hbm.at[0], syn.at[1], load_sem.at[2]),
        pltpu.make_async_copy(av_hbm.at[0], ana.at[0], load_sem.at[3]),
        pltpu.make_async_copy(aw_hbm.at[0], ana.at[1], load_sem.at[4]),
    ]
    barrier = pltpu.get_barrier_semaphore()

    def greet(i, carry):
        peer = lax.rem(lat + i, lats)
        pl.semaphore_signal(barrier, inc=1, device_id=(peer, rep), device_id_type=MESH)
        pl.semaphore_signal(barrier, inc=1, device_id=(peer, other), device_id_type=MESH)
        return carry

    pl.semaphore_signal(barrier, inc=1, device_id=(lat, other), device_id_type=MESH)
    lax.fori_loop(1, lats, greet, 0)

    loads[0].start()
    for f in range(GROUP):
        fetch(f).start()

    for f in range(GROUP, fields):
        fetch(f).start()
    for load in loads[1:3]:
        load.start()

    loads[0].wait()
    length = field_hbm.shape[3]

    def orders_of(index):
        order = jnp.zeros(index.shape, jnp.int32)
        for k in range(2 * lats):
            order = jnp.where(index == k, spacing * assign_ref[k], order)
        return order

    shape = (4 * lats, 128)
    row = lax.broadcasted_iota(jnp.int32, shape, 0)
    phase = orders_of((row // 4) * 2 + (row & 1)) * lax.broadcasted_iota(jnp.int32, shape, 1)
    phase = lax.rem(phase + ((row // 2) & 1) * (length // 4), length)
    wave = jnp.cos(phase.astype(jnp.float32) * (2.0 * math.pi / length)) * (1.0 / math.sqrt(length))
    wave = wave.astype(jnp.bfloat16)
    table_ref[:, 0:128] = wave
    table_ref[:, 128:256] = wave

    def send(batch, peer):
        first, count = sum(BATCHES[:batch]), BATCHES[batch]
        return pltpu.make_async_remote_copy(
            src_ref=packets[batch].at[peer],
            dst_ref=spec.at[
                pl.ds(pl.multiple_of((rep * groups + first) * span, span), count * span),
                pl.ds(pl.multiple_of(spot * 128, 128), 128),
            ],
            send_sem=send_sem,
            recv_sem=recv_sem,
            device_id=(peer, side),
            device_id_type=MESH,
        )

    def bulk(blocks, send_at, recv_at):
        tall = 1
        while blocks % tall or blocks // tall * 128 > ring.shape[2]:
            tall += 1
        like = ring.at[0, pl.ds(0, tall * span), pl.ds(0, blocks // tall * 128)]
        return pltpu.make_async_remote_copy(
            src_ref=like,
            dst_ref=like,
            send_sem=send_at,
            recv_sem=recv_at,
            device_id=(lat, other),
            device_id_type=MESH,
        )

    share = pltpu.make_async_remote_copy(
        src_ref=joined,
        dst_ref=theirs,
        send_sem=pass_send,
        recv_sem=pass_recv,
        device_id=(lat, other),
        device_id_type=MESH,
    )

    def fold(f, carry):
        fetch(f).wait()
        total_f = ring[f, :, 0:128].astype(jnp.float32)
        for piece in range(1, ring.shape[2] // 128):
            total_f = total_f + ring[f, :, piece * 128 : (piece + 1) * 128].astype(jnp.float32)
        high = total_f.astype(jnp.bfloat16)
        low = (total_f - high.astype(jnp.float32)).astype(jnp.bfloat16)
        begin = pl.multiple_of(lax.rem(f, GROUP) * 128, 128)
        folded[pl.ds(begin, 128), 0:128] = high
        folded[pl.ds(begin, 128), 128:256] = low
        return carry

    group = 0
    for batch, count in enumerate(BATCHES):
        for member in range(count):
            lax.fori_loop(group * GROUP, (group + 1) * GROUP, fold, 0)
            value = lax.dot_general(table_ref[...], folded[...], NT, preferred_element_type=jnp.float32)
            for k in range(GROUP):
                staged[pl.ds(k, 4 * lats, stride=GROUP), :] = value[:, k * 128 : (k + 1) * 128]
            packets[batch][:, member * span : (member + 1) * span, :] = (
                staged[...].astype(jnp.bfloat16).reshape(lats, span, 128)
            )
            group += 1
            if group == 3:
                loads[3].start()
                loads[4].start()
        if batch == 0:
            pl.semaphore_wait(barrier, 2 * lats - 1)

        def send_far(i, carry, batch=batch):
            send(batch, (1 - side) * near + lax.rem(spot + near - i, near)).start()
            return carry

        def send_near(i, carry, batch=batch):
            send(batch, side * near + lax.rem(spot + near - i, near)).start()
            return carry

        lax.fori_loop(0, near, send_far, 0)
        lax.fori_loop(1, near, send_near, 0)

        @pl.when(side == rep)
        def _(batch=batch):
            first, count = sum(BATCHES[:batch]), BATCHES[batch]
            spec[
                pl.ds(pl.multiple_of((rep * groups + first) * span, span), count * span),
                pl.ds(pl.multiple_of(spot * 128, 128), 128),
            ] = packets[batch][lat]

        @pl.when(side != rep)
        def _(batch=batch):
            send(batch, lat).start()

    first_order = spacing * assign_ref[2 * lat]
    second_order = spacing * assign_ref[2 * lat + 1]
    border = LMAX - first_order
    loads[1].wait()
    loads[2].wait()
    out_rows = syn.shape[1]
    packed = rep * half_pack + lax.broadcasted_iota(jnp.int32, (1, half_pack), 1)
    degree = jnp.where(packed >= border, second_order + packed - border, first_order + packed)
    quarter = (degree + 1) & 3
    cosine = jnp.where(quarter == 0, 1.0, jnp.where(quarter == 2, -1.0, 0.0))
    sine = jnp.where(quarter == 1, -1.0, jnp.where(quarter == 3, 1.0, 0.0))
    held = jnp.where(packed >= border, 1, 0)
    for k in range(2):
        values = syn[k].astype(jnp.float32)
        for slot_at in range(2):
            for turn, factor in enumerate((cosine, sine)):
                piece = (values * jnp.where(held == slot_at, factor, 0.0)).astype(jnp.bfloat16)
                for target in range(2):
                    begin = (((target ^ k) * 2 + slot_at) * 2 + turn) * out_rows
                    mix[target, begin : begin + out_rows, :] = piece

    halves = [pl.ds(pl.multiple_of(half * width, 128), width) for half in (other, rep)]
    loads[3].wait()
    for k in range(2):
        total[k] = jnp.dot(mix[0], ana[0, :, halves[k]], preferred_element_type=jnp.float32)
    loads[4].wait()
    value = total[0] + jnp.dot(mix[1], ana[1, :, halves[0]], preferred_element_type=jnp.float32)
    joined[...] = value.astype(jnp.bfloat16)
    share.start()
    total[1] = total[1] + jnp.dot(mix[1], ana[1, :, halves[1]], preferred_element_type=jnp.float32)

    own_rows = out_rows // lats
    shape = (out_rows, 128)
    row = lax.broadcasted_iota(jnp.int32, shape, 0)
    n = lax.broadcasted_iota(jnp.int32, shape, 1)
    for slot_at in range(2):
        order = orders_of((row // own_rows) * 2 + slot_at)
        weight = jnp.where(order == 0, 1.0, 2.0) * (1.0 / math.sqrt(2 * lats))
        for part_at in range(2):
            phase = lax.rem(order * n + part_at * (NLON_OUT // 4), NLON_OUT)
            wave = weight * jnp.cos(phase.astype(jnp.float32) * (2.0 * math.pi / NLON_OUT))
            begin = (part_at * 2 + slot_at) * out_rows
            for o in range(own_rows):
                inverse_ref[begin : begin + out_rows, o * 128 : (o + 1) * 128] = jnp.where(
                    lax.rem(row, own_rows) == o, wave, 0.0
                ).astype(jnp.bfloat16)

    share.wait_recv()
    theirs[...] = (total[1] + theirs[...].astype(jnp.float32)).astype(jnp.bfloat16)

    @pl.when(side == rep)
    def _():
        bulk(groups * (2 * near - 1), send_sem, recv_sem).wait_recv()

    @pl.when(side != rep)
    def _():
        bulk(groups * 2 * near, send_sem, recv_sem).wait_recv()

    synth = lax.dot_general(theirs[...], spec[...], NT, preferred_element_type=jnp.float32)

    lane = lax.broadcasted_iota(jnp.int32, (1, 128), 1)
    lane_slot = (lane // GROUP) & 1
    part = (lane // (2 * GROUP)) & 1
    comp = lane // 64

    def swap_part(x):
        return jnp.where(part == 0, pltpu.roll(x, 128 - 2 * GROUP, 1), pltpu.roll(x, 2 * GROUP, 1))

    def swap_comp(x):
        return pltpu.roll(x, 64, 1)

    part_sign = jnp.where(part == 0, -1.0, 1.0)
    comp_sign = jnp.where(comp == 0, 1.0, -1.0)

    def turned(kind):
        both = [synth[(kind * 2 + k) * 2 * out_rows : (kind * 2 + k + 1) * 2 * out_rows] for k in range(2)]
        value = jnp.where(lane_slot == 0, both[0], both[1])
        return value[:out_rows] + part_sign * swap_part(value[out_rows:])

    rows = turned(0) - comp_sign * part_sign * swap_comp(swap_part(turned(1)))
    rows_out[...] = rows.reshape(lats, own_rows, 128)

    def row_copy(target_lat, target_rep):
        return pltpu.make_async_remote_copy(
            src_ref=rows_out.at[target_lat],
            dst_ref=rows_in.at[rep * lats + lat],
            send_sem=row_send,
            recv_sem=row_recv,
            device_id=(target_lat, target_rep),
            device_id_type=MESH,
        )

    def send_rows(i, carry):
        peer = lax.rem(lat + i, lats)
        row_copy(peer, rep).start()
        row_copy(peer, other).start()
        return carry

    lax.fori_loop(1, lats, send_rows, 0)
    row_copy(lat, other).start()
    rows_in[rep * lats + lat] = rows_out[lat]

    share.wait_send()

    @pl.when(side == rep)
    def _():
        bulk(groups * (lats - 1), send_sem, recv_sem).wait_send()

    @pl.when(side != rep)
    def _():
        bulk(groups * lats, send_sem, recv_sem).wait_send()

    all_rows = pltpu.make_async_remote_copy(
        src_ref=rows_in.at[pl.ds(0, 2 * lats - 1)],
        dst_ref=rows_in.at[pl.ds(0, 2 * lats - 1)],
        send_sem=row_send,
        recv_sem=row_recv,
        device_id=(lat, other),
        device_id_type=MESH,
    )
    all_rows.wait_recv()

    for k in range(lats):
        rows_sum[k * own_rows : (k + 1) * own_rows, :] = rows_in[k] + rows_in[lats + k]
    summed = rows_sum[...]
    gathered = [summed] + [pltpu.roll(summed, 128 - k * GROUP, 1) for k in range(1, 4)]
    gathered = jnp.concatenate(gathered, axis=0).astype(jnp.bfloat16)
    value = lax.dot_general(gathered, inverse_ref[...], TN, preferred_element_type=jnp.float32)
    for block in range(2 * groups):
        comp_at, group = block // groups, block % groups
        for o in range(own_rows):
            begin = (group * GROUP * 2 + comp_at) * own_rows + o
            out_ref[pl.ds(begin, GROUP, stride=2 * own_rows), :] = value[
                block * span : block * span + GROUP, o * 128 : (o + 1) * 128
            ]
    all_rows.wait_send()


def repeat_kernel(small_ref, out_hbm, wide, sem):
    value = small_ref[...]
    width = wide.shape[3]
    for k in range(width // 128):
        wide[:, :, :, k * 128 : (k + 1) * 128] = value
    copies = [
        pltpu.make_async_copy(wide, out_hbm.at[:, :, :, k * width : (k + 1) * width], sem.at[k])
        for k in range(out_hbm.shape[3] // width)
    ]
    for copy in copies:
        copy.start()
    for copy in copies:
        copy.wait()


def fast_body(near_field, assign, ana_v, ana_w, syn_v, syn_w):
    lats = lax.axis_size("lat")
    fields, comps, own_lat, length = near_field.shape
    order_count = assign.shape[0]
    half_pack = ana_v.shape[1]
    out_rows = syn_v.shape[2]
    own_rows = out_rows // lats
    hbm_spec = pl.BlockSpec(memory_space=pltpu.HBM)
    vmem_spec = pl.BlockSpec(memory_space=pltpu.VMEM)
    inputs = (assign, near_field, ana_v, ana_w, syn_v.swapaxes(1, 2), syn_w.swapaxes(1, 2))
    small = pl.pallas_call(
        functools.partial(kernel, lats, LMAX // order_count),
        out_shape=pltpu.VMEM((fields * 2 * own_rows, 128), jnp.float32),
        in_specs=[hbm_spec] * 6,
        out_specs=vmem_spec,
        scratch_shapes=[
            pltpu.SMEM((order_count,), jnp.int32),
            pltpu.VMEM((4 * lats, 256), jnp.bfloat16),
            pltpu.VMEM((4 * out_rows, own_rows * 128), jnp.bfloat16),
            pltpu.VMEM((fields, own_lat, length), jnp.bfloat16),
            pltpu.VMEM((2, half_pack, ana_v.shape[2]), jnp.bfloat16),
            pltpu.VMEM((2, out_rows, half_pack), jnp.bfloat16),
            pltpu.VMEM((2, 8 * out_rows, half_pack), jnp.bfloat16),
            pltpu.VMEM((128 * GROUP, 256), jnp.bfloat16),
            pltpu.VMEM((4 * lats * GROUP, 128), jnp.float32),
            [pltpu.VMEM((lats, 4 * GROUP * count, 128), jnp.bfloat16) for count in BATCHES],
            pltpu.VMEM((8 * fields, lats // 2 * own_lat), jnp.bfloat16),
            pltpu.VMEM((2, 8 * out_rows, lats // 2 * own_lat), jnp.float32),
            pltpu.VMEM((8 * out_rows, lats // 2 * own_lat), jnp.bfloat16),
            pltpu.VMEM((8 * out_rows, lats // 2 * own_lat), jnp.bfloat16),
            pltpu.VMEM((lats, own_rows, 128), jnp.float32),
            pltpu.VMEM((2 * lats, own_rows, 128), jnp.float32),
            pltpu.VMEM((lats * own_rows, 128), jnp.float32),
            pltpu.SemaphoreType.DMA((fields,)),
            pltpu.SemaphoreType.DMA((5,)),
            pltpu.SemaphoreType.DMA,
            pltpu.SemaphoreType.DMA,
            pltpu.SemaphoreType.DMA,
            pltpu.SemaphoreType.DMA,
            pltpu.SemaphoreType.DMA,
            pltpu.SemaphoreType.DMA,
        ],
        compiler_params=pltpu.CompilerParams(
            collective_id=0, has_side_effects=True, vmem_limit_bytes=40_000_000
        ),
    )(*(pltpu.with_memory_space_constraint(x, pltpu.HBM) for x in inputs))
    repeats = NLON_OUT // lax.axis_size("rep") // 128
    spread = 4
    return pl.pallas_call(
        repeat_kernel,
        out_shape=jax.ShapeDtypeStruct((fields, 2, own_rows, repeats * 128), jnp.float32),
        in_specs=[pl.BlockSpec(memory_space=pltpu.VMEM)],
        out_specs=hbm_spec,
        scratch_shapes=[
            pltpu.VMEM((fields, 2, own_rows, repeats // spread * 128), jnp.float32),
            pltpu.SemaphoreType.DMA((spread,)),
        ],
    )(pltpu.with_memory_space_constraint(small.reshape(fields, 2, own_rows, 128), pltpu.VMEM))


def fits(mesh, near_field, assign, ana_v, syn_v):
    lats = mesh.shape["lat"]
    fields, comps, rows, length = near_field.shape
    spacing = LMAX // assign.shape[0]
    return (
        mesh.shape["rep"] == 2
        and fields == 4 * GROUP
        and lats >= 4
        and comps == 2
        and lats & (lats - 1) == 0
        and rows == 128 * lats
        and assign.shape[0] == 2 * lats
        and 128 * spacing % length == 0
        and 128 * spacing % NLON_OUT == 0
        and syn_v.shape[2] == 32
        and ana_v.shape[1] % 64 == 0
    )


def solution(mesh):
    in_specs = (
        P(None, None, "lat", None),
        P(),
        P("lat", "rep", None),
        P("lat", "rep", None),
        P("lat", "rep", None),
        P("lat", "rep", None),
    )
    out_specs = P(None, None, "lat", "rep")

    def run(near_field, assign, ana_v, ana_w, syn_v, syn_w):
        chosen = fast_body if fits(mesh, near_field, assign, ana_v, syn_v) else plain_body
        mapped = jax.shard_map(chosen, mesh=mesh, in_specs=in_specs, out_specs=out_specs, check_vma=False)
        return mapped(near_field, assign, ana_v, ana_w, syn_v, syn_w)

    return run
```

```python
import functools
import math

import jax
import jax.numpy as jnp
from jax import lax
from jax.experimental import pallas as pl
from jax.experimental.pallas import tpu as pltpu
from jax.sharding import PartitionSpec as P

LMAX = 2048
NLON_OUT = 8192


def forward_table(orders, length):
    column = jnp.arange(length, dtype=jnp.int32)
    phase_index = orders[:, None] * column[None, :] % length
    angles = phase_index.astype(jnp.float32) * (2.0 * math.pi / length)
    factor = 1.0 / math.sqrt(length)
    stacked = jnp.stack([jnp.cos(angles) * factor, -jnp.sin(angles) * factor], axis=1)
    return stacked.reshape(2 * orders.shape[0], length).astype(jnp.bfloat16)


def inverse_table(orders, begin, count, length):
    column = begin + jnp.arange(count, dtype=jnp.int32)
    phase_index = orders[:, None] * column[None, :] % length
    angles = phase_index.astype(jnp.float32) * (2.0 * math.pi / length)
    weight = jnp.where(orders == 0, 1.0, 2.0).astype(jnp.float32)[:, None] / math.sqrt(
        orders.shape[0]
    )
    stacked = jnp.stack([weight * jnp.cos(angles), -weight * jnp.sin(angles)], axis=1)
    return stacked.reshape(2 * orders.shape[0], count).astype(jnp.bfloat16)


def pad_rows(matrix, tile_count, tile_rows):
    missing = tile_count * tile_rows - matrix.shape[0]
    return jnp.pad(matrix, ((0, missing), (0, 0))).reshape(tile_count, tile_rows, matrix.shape[1])


def legendre(spectra, mat_av, mat_aw, mat_sv, mat_sw, packed_start, first_order, second_order):
    count = spectra.shape[1]
    flat = spectra.reshape(2, 4 * count, spectra.shape[3])
    tile_rows = 128
    tile_count = -(-mat_av.shape[0] // tile_rows)
    out_rows = mat_sv.shape[1]
    border = LMAX - first_order

    def step(carry, inputs_now):
        total_v, total_w = carry
        number, tile_av, tile_aw, tile_sv, tile_sw = inputs_now
        first_row = packed_start + number * tile_rows
        packed = first_row + jnp.arange(tile_rows, dtype=jnp.int32)
        second = packed >= border
        branch_kind = jnp.where(
            first_row >= border, 1, jnp.where(first_row + tile_rows - 1 < border, 0, 2)
        )

        def single_slot(slot):

            def compute():
                slot_flat = flat[slot]
                part_v = jnp.dot(tile_av, slot_flat.T, preferred_element_type=jnp.float32).reshape(
                    tile_rows, 2, count, 2
                )
                part_w = jnp.dot(tile_aw, slot_flat.T, preferred_element_type=jnp.float32).reshape(
                    tile_rows, 2, count, 2
                )
                return (part_v, part_w)

            return compute

        def both_slots():
            first_v, first_w = single_slot(0)()
            second_v, second_w = single_slot(1)()
            choose_second = second[:, None, None, None]
            return (
                jnp.where(choose_second, second_v, first_v),
                jnp.where(choose_second, second_w, first_w),
            )

        chosen_v, chosen_w = lax.switch(branch_kind, [single_slot(0), single_slot(1), both_slots])
        degree = jnp.where(second, second_order + packed - border, first_order + packed)
        sph_re = chosen_v[:, 0, :, 0] + chosen_w[:, 1, :, 1]
        sph_im = chosen_v[:, 1, :, 0] - chosen_w[:, 0, :, 1]
        tor_re = chosen_w[:, 1, :, 0] - chosen_v[:, 0, :, 1]
        tor_im = -chosen_w[:, 0, :, 0] - chosen_v[:, 1, :, 1]
        quarter = (degree + 1) % 4
        cosine = jnp.where(quarter == 0, 1.0, jnp.where(quarter == 2, -1.0, 0.0)).astype(
            jnp.float32
        )[:, None]
        sine = jnp.where(quarter == 1, -1.0, jnp.where(quarter == 3, 1.0, 0.0)).astype(jnp.float32)[
            :, None
        ]
        coeffs = jnp.stack(
            [
                cosine * sph_re - sine * sph_im,
                cosine * sph_im + sine * sph_re,
                cosine * tor_re - sine * tor_im,
                cosine * tor_im + sine * tor_re,
            ],
            axis=1,
        ).astype(jnp.bfloat16)
        flat_coeffs = coeffs.reshape(tile_rows, 4 * count)
        second_mask = second.astype(jnp.bfloat16)[:, None]

        def mixed_rows():
            lower_c = flat_coeffs * (1 - second_mask)
            upper_c = flat_coeffs * second_mask
            add_v = jnp.stack(
                [
                    jnp.dot(lower_c.T, tile_sv, preferred_element_type=jnp.float32),
                    jnp.dot(upper_c.T, tile_sv, preferred_element_type=jnp.float32),
                ]
            )
            add_w = jnp.stack(
                [
                    jnp.dot(lower_c.T, tile_sw, preferred_element_type=jnp.float32),
                    jnp.dot(upper_c.T, tile_sw, preferred_element_type=jnp.float32),
                ]
            )
            return (add_v, add_w)

        def single_rows():
            part_v = jnp.dot(flat_coeffs.T, tile_sv, preferred_element_type=jnp.float32)
            part_w = jnp.dot(flat_coeffs.T, tile_sw, preferred_element_type=jnp.float32)
            upper_pick = (branch_kind == 1).astype(jnp.float32)
            return (
                jnp.stack([part_v * (1.0 - upper_pick), part_v * upper_pick]),
                jnp.stack([part_w * (1.0 - upper_pick), part_w * upper_pick]),
            )

        add_v, add_w = lax.cond(branch_kind == 2, mixed_rows, single_rows)
        return ((total_v + add_v, total_w + add_w), None)

    start_v = jnp.zeros((2, 4 * count, out_rows), jnp.float32)
    start_w = jnp.zeros((2, 4 * count, out_rows), jnp.float32)
    numbers = jnp.arange(tile_count, dtype=jnp.int32)
    (total_v, total_w), unused = lax.scan(
        step,
        (start_v, start_w),
        (
            numbers,
            pad_rows(mat_av, tile_count, tile_rows),
            pad_rows(mat_aw, tile_count, tile_rows),
            pad_rows(mat_sv, tile_count, tile_rows),
            pad_rows(mat_sw, tile_count, tile_rows),
        ),
    )
    synth_v = total_v.reshape(2, 4, count, -1)
    synth_w = total_w.reshape(2, 4, count, -1)
    theta_re = synth_v[:, 0] - synth_w[:, 3]
    theta_im = synth_v[:, 1] + synth_w[:, 2]
    phi_re = -synth_w[:, 1] - synth_v[:, 2]
    phi_im = synth_w[:, 0] - synth_v[:, 3]
    real_part = jnp.stack([theta_re, phi_re], axis=2)
    imag_part = jnp.stack([theta_im, phi_im], axis=2)
    return jnp.stack([real_part, imag_part], axis=1).reshape(4, count, 2, -1)


def plain_body(near_field, assign, ana_v, ana_w, syn_v, syn_w):
    order_count = assign.shape[0]
    spacing = LMAX // order_count
    orders = spacing * assign
    pair_orders = lax.dynamic_slice_in_dim(orders, 2 * lax.axis_index("lat"), 2, 0)
    half_pack = ana_v.shape[1]
    packed_start = lax.axis_index("rep") * half_pack
    table = forward_table(orders, near_field.shape[3])
    spectrum = jnp.einsum(
        "jk,fctk->jfct", table, near_field, preferred_element_type=jnp.float32
    ).astype(jnp.bfloat16)
    partial_value = legendre(
        lax.all_to_all(spectrum, "lat", split_axis=0, concat_axis=3, tiled=True),
        ana_v[0],
        ana_w[0],
        syn_v[0],
        syn_w[0],
        packed_start,
        pair_orders[0],
        pair_orders[1],
    )
    summed = lax.psum(partial_value, "rep").astype(jnp.bfloat16)
    regrouped = lax.all_to_all(summed, "lat", split_axis=3, concat_axis=0, tiled=True)
    longitudes = NLON_OUT // lax.axis_size("rep")
    inverse = inverse_table(orders, lax.axis_index("rep") * longitudes, longitudes, NLON_OUT)
    return jnp.einsum("jfcr,jp->fcrp", regrouped, inverse, preferred_element_type=jnp.float32)

MESH = pl.DeviceIdType.MESH
GROUP = 4
BATCHES = (2, 1, 1)
NT = (((1,), (1,)), ((), ()))
TN = (((0,), (0,)), ((), ()))


def kernel(
    lats,
    spacing,
    assign_hbm,
    field_hbm,
    av_hbm,
    aw_hbm,
    sv_hbm,
    sw_hbm,
    out_ref,
    assign_ref,
    table_ref,
    inverse_ref,
    ring,
    ana,
    syn,
    mix,
    folded,
    staged,
    packets,
    spec,
    total,
    joined,
    theirs,
    rows_out,
    rows_in,
    rows_sum,
    field_sem,
    load_sem,
    send_sem,
    recv_sem,
    pass_send,
    pass_recv,
    row_send,
    row_recv,
):
    lat = lax.axis_index("lat")
    rep = lax.axis_index("rep")
    other = 1 - rep
    fields = field_hbm.shape[0]
    groups = fields // GROUP
    half_pack = ana.shape[1]
    span = 4 * GROUP
    near = lats // 2
    side = lat // near
    spot = lax.rem(lat, near)
    width = near * 128

    def fetch(f):
        return pltpu.make_async_copy(field_hbm.at[f, rep], ring.at[f], field_sem.at[f])

    loads = [
        pltpu.make_async_copy(assign_hbm, assign_ref, load_sem.at[0]),
        pltpu.make_async_copy(sv_hbm.at[0], syn.at[0], load_sem.at[1]),
        pltpu.make_async_copy(sw_hbm.at[0], syn.at[1], load_sem.at[2]),
    ]
    halves = [pl.ds(pl.multiple_of(half * width, 128), width) for half in (other, rep)]
    for half in halves:
        for k, source in enumerate((av_hbm, aw_hbm)):
            loads.append(
                pltpu.make_async_copy(source.at[0, :, half], ana.at[k, :, half], load_sem.at[len(loads)])
            )
    barrier = pltpu.get_barrier_semaphore()

    def greet(i, carry):
        peer = lax.rem(lat + i, lats)
        pl.semaphore_signal(barrier, inc=1, device_id=(peer, rep), device_id_type=MESH)
        pl.semaphore_signal(barrier, inc=1, device_id=(peer, other), device_id_type=MESH)
        return carry

    pl.semaphore_signal(barrier, inc=1, device_id=(lat, other), device_id_type=MESH)
    lax.fori_loop(1, lats, greet, 0)

    loads[0].start()
    for f in range(GROUP):
        fetch(f).start()

    for f in range(GROUP, fields):
        fetch(f).start()
    for load in loads[1:3]:
        load.start()

    loads[0].wait()
    length = field_hbm.shape[3]

    def orders_of(index):
        order = jnp.zeros(index.shape, jnp.int32)
        for k in range(2 * lats):
            order = jnp.where(index == k, spacing * assign_ref[k], order)
        return order

    shape = (4 * lats, 128)
    row = lax.broadcasted_iota(jnp.int32, shape, 0)
    phase = orders_of((row // 4) * 2 + (row & 1)) * lax.broadcasted_iota(jnp.int32, shape, 1)
    phase = lax.rem(phase + ((row // 2) & 1) * (length // 4), length)
    wave = jnp.cos(phase.astype(jnp.float32) * (2.0 * math.pi / length)) * (1.0 / math.sqrt(length))
    wave = wave.astype(jnp.bfloat16)
    table_ref[:, 0:128] = wave
    table_ref[:, 128:256] = wave

    def send(batch, peer):
        first, count = sum(BATCHES[:batch]), BATCHES[batch]
        return pltpu.make_async_remote_copy(
            src_ref=packets[batch].at[peer],
            dst_ref=spec.at[
                pl.ds(pl.multiple_of((rep * groups + first) * span, span), count * span),
                pl.ds(pl.multiple_of(spot * 128, 128), 128),
            ],
            send_sem=send_sem,
            recv_sem=recv_sem,
            device_id=(peer, side),
            device_id_type=MESH,
        )

    def bulk(blocks, send_at, recv_at):
        tall = 1
        while blocks % tall or blocks // tall * 128 > ring.shape[2]:
            tall += 1
        like = ring.at[0, pl.ds(0, tall * span), pl.ds(0, blocks // tall * 128)]
        return pltpu.make_async_remote_copy(
            src_ref=like,
            dst_ref=like,
            send_sem=send_at,
            recv_sem=recv_at,
            device_id=(lat, other),
            device_id_type=MESH,
        )

    share = pltpu.make_async_remote_copy(
        src_ref=joined,
        dst_ref=theirs,
        send_sem=pass_send,
        recv_sem=pass_recv,
        device_id=(lat, other),
        device_id_type=MESH,
    )

    def fold(f, carry):
        fetch(f).wait()
        total_f = ring[f, :, 0:128].astype(jnp.float32)
        for piece in range(1, ring.shape[2] // 128):
            total_f = total_f + ring[f, :, piece * 128 : (piece + 1) * 128].astype(jnp.float32)
        high = total_f.astype(jnp.bfloat16)
        low = (total_f - high.astype(jnp.float32)).astype(jnp.bfloat16)
        begin = pl.multiple_of(lax.rem(f, GROUP) * 128, 128)
        folded[pl.ds(begin, 128), 0:128] = high
        folded[pl.ds(begin, 128), 128:256] = low
        return carry

    group = 0
    for batch, count in enumerate(BATCHES):
        for member in range(count):
            lax.fori_loop(group * GROUP, (group + 1) * GROUP, fold, 0)
            value = lax.dot_general(table_ref[...], folded[...], NT, preferred_element_type=jnp.float32)
            for k in range(GROUP):
                staged[pl.ds(k, 4 * lats, stride=GROUP), :] = value[:, k * 128 : (k + 1) * 128]
            packets[batch][:, member * span : (member + 1) * span, :] = (
                staged[...].astype(jnp.bfloat16).reshape(lats, span, 128)
            )
            group += 1
            if group == 3:
                loads[3].start()
                loads[4].start()
            if group == groups:
                loads[5].start()
                loads[6].start()
        if batch == 0:
            pl.semaphore_wait(barrier, 2 * lats - 1)

        def send_far(i, carry, batch=batch):
            send(batch, (1 - side) * near + lax.rem(spot + near - i, near)).start()
            return carry

        def send_near(i, carry, batch=batch):
            send(batch, side * near + lax.rem(spot + near - i, near)).start()
            return carry

        lax.fori_loop(0, near, send_far, 0)
        lax.fori_loop(1, near, send_near, 0)

        @pl.when(side == rep)
        def _(batch=batch):
            first, count = sum(BATCHES[:batch]), BATCHES[batch]
            spec[
                pl.ds(pl.multiple_of((rep * groups + first) * span, span), count * span),
                pl.ds(pl.multiple_of(spot * 128, 128), 128),
            ] = packets[batch][lat]

        @pl.when(side != rep)
        def _(batch=batch):
            send(batch, lat).start()

    first_order = spacing * assign_ref[2 * lat]
    second_order = spacing * assign_ref[2 * lat + 1]
    border = LMAX - first_order
    loads[1].wait()
    loads[2].wait()
    out_rows = syn.shape[1]
    packed = rep * half_pack + lax.broadcasted_iota(jnp.int32, (1, half_pack), 1)
    degree = jnp.where(packed >= border, second_order + packed - border, first_order + packed)
    quarter = (degree + 1) & 3
    cosine = jnp.where(quarter == 0, 1.0, jnp.where(quarter == 2, -1.0, 0.0))
    sine = jnp.where(quarter == 1, -1.0, jnp.where(quarter == 3, 1.0, 0.0))
    held = jnp.where(packed >= border, 1, 0)
    for k in range(2):
        values = syn[k].astype(jnp.float32)
        for slot_at in range(2):
            for turn, factor in enumerate((cosine, sine)):
                piece = (values * jnp.where(held == slot_at, factor, 0.0)).astype(jnp.bfloat16)
                for target in range(2):
                    begin = (((target ^ k) * 2 + slot_at) * 2 + turn) * out_rows
                    mix[target, begin : begin + out_rows, :] = piece

    loads[3].wait()
    value = jnp.dot(mix[0], ana[0, :, halves[0]], preferred_element_type=jnp.float32)
    loads[4].wait()
    value = value + jnp.dot(mix[1], ana[1, :, halves[0]], preferred_element_type=jnp.float32)
    joined[...] = value.astype(jnp.bfloat16)
    share.start()
    loads[5].wait()
    total[...] = jnp.dot(mix[0], ana[0, :, halves[1]], preferred_element_type=jnp.float32)
    loads[6].wait()
    total[...] = total[...] + jnp.dot(mix[1], ana[1, :, halves[1]], preferred_element_type=jnp.float32)

    own_rows = out_rows // lats
    shape = (out_rows, 128)
    row = lax.broadcasted_iota(jnp.int32, shape, 0)
    n = lax.broadcasted_iota(jnp.int32, shape, 1)
    for slot_at in range(2):
        order = orders_of((row // own_rows) * 2 + slot_at)
        weight = jnp.where(order == 0, 1.0, 2.0) * (1.0 / math.sqrt(2 * lats))
        for part_at in range(2):
            phase = lax.rem(order * n + part_at * (NLON_OUT // 4), NLON_OUT)
            wave = weight * jnp.cos(phase.astype(jnp.float32) * (2.0 * math.pi / NLON_OUT))
            begin = (part_at * 2 + slot_at) * out_rows
            for o in range(own_rows):
                inverse_ref[begin : begin + out_rows, o * 128 : (o + 1) * 128] = jnp.where(
                    lax.rem(row, own_rows) == o, wave, 0.0
                ).astype(jnp.bfloat16)

    share.wait_recv()
    theirs[...] = (total[...] + theirs[...].astype(jnp.float32)).astype(jnp.bfloat16)

    @pl.when(side == rep)
    def _():
        bulk(groups * (2 * near - 1), send_sem, recv_sem).wait_recv()

    @pl.when(side != rep)
    def _():
        bulk(groups * 2 * near, send_sem, recv_sem).wait_recv()

    synth = lax.dot_general(theirs[...], spec[...], NT, preferred_element_type=jnp.float32)

    lane = lax.broadcasted_iota(jnp.int32, (1, 128), 1)
    lane_slot = (lane // GROUP) & 1
    part = (lane // (2 * GROUP)) & 1
    comp = lane // 64

    def swap_part(x):
        return jnp.where(part == 0, pltpu.roll(x, 128 - 2 * GROUP, 1), pltpu.roll(x, 2 * GROUP, 1))

    def swap_comp(x):
        return pltpu.roll(x, 64, 1)

    part_sign = jnp.where(part == 0, -1.0, 1.0)
    comp_sign = jnp.where(comp == 0, 1.0, -1.0)

    def turned(kind):
        both = [synth[(kind * 2 + k) * 2 * out_rows : (kind * 2 + k + 1) * 2 * out_rows] for k in range(2)]
        value = jnp.where(lane_slot == 0, both[0], both[1])
        return value[:out_rows] + part_sign * swap_part(value[out_rows:])

    rows = turned(0) - comp_sign * part_sign * swap_comp(swap_part(turned(1)))
    rows_out[...] = rows.reshape(lats, own_rows, 128)

    quarter_lats = lats // 4

    def ranked(t):
        plane = t // quarter_lats
        plane = side * plane + (1 - side) * (3 - plane)
        return plane * quarter_lats + lax.rem(lat + t, quarter_lats)

    def row_copy(target_lat, target_rep):
        return pltpu.make_async_remote_copy(
            src_ref=rows_out.at[target_lat],
            dst_ref=rows_in.at[rep * lats + lat],
            send_sem=row_send,
            recv_sem=row_recv,
            device_id=(target_lat, target_rep),
            device_id_type=MESH,
        )

    def send_rows(i, carry):
        peer = ranked(i)
        row_copy(peer, other).start()

        @pl.when(peer != lat)
        def _():
            row_copy(peer, rep).start()

        return carry

    lax.fori_loop(0, lats, send_rows, 0)
    rows_in[rep * lats + lat] = rows_out[lat]

    share.wait_send()

    @pl.when(side == rep)
    def _():
        bulk(groups * (lats - 1), send_sem, recv_sem).wait_send()

    @pl.when(side != rep)
    def _():
        bulk(groups * lats, send_sem, recv_sem).wait_send()

    all_rows = pltpu.make_async_remote_copy(
        src_ref=rows_in.at[pl.ds(0, 2 * lats - 1)],
        dst_ref=rows_in.at[pl.ds(0, 2 * lats - 1)],
        send_sem=row_send,
        recv_sem=row_recv,
        device_id=(lat, other),
        device_id_type=MESH,
    )
    all_rows.wait_recv()

    summed = (rows_in[0:lats] + rows_in[lats : 2 * lats]).reshape(out_rows, 128)
    gathered = [summed] + [pltpu.roll(summed, 128 - k * GROUP, 1) for k in range(1, 4)]
    gathered = jnp.concatenate(gathered, axis=0).astype(jnp.bfloat16)
    value = lax.dot_general(gathered, inverse_ref[...], TN, preferred_element_type=jnp.float32)
    for block in range(2 * groups):
        comp_at, group = block // groups, block % groups
        for o in range(own_rows):
            begin = (group * GROUP * 2 + comp_at) * own_rows + o
            out_ref[pl.ds(begin, GROUP, stride=2 * own_rows), :] = value[
                block * span : block * span + GROUP, o * 128 : (o + 1) * 128
            ]
    all_rows.wait_send()


def repeat_kernel(small_ref, out_hbm, wide, sem):
    value = small_ref[...]
    width = wide.shape[3]
    for k in range(width // 128):
        wide[:, :, :, k * 128 : (k + 1) * 128] = value
    copies = [
        pltpu.make_async_copy(wide, out_hbm.at[:, :, :, k * width : (k + 1) * width], sem.at[k])
        for k in range(out_hbm.shape[3] // width)
    ]
    for copy in copies:
        copy.start()
    for copy in copies:
        copy.wait()


def fast_body(near_field, assign, ana_v, ana_w, syn_v, syn_w):
    lats = lax.axis_size("lat")
    fields, comps, own_lat, length = near_field.shape
    order_count = assign.shape[0]
    half_pack = ana_v.shape[1]
    out_rows = syn_v.shape[2]
    own_rows = out_rows // lats
    hbm_spec = pl.BlockSpec(memory_space=pltpu.HBM)
    vmem_spec = pl.BlockSpec(memory_space=pltpu.VMEM)
    inputs = (assign, near_field, ana_v, ana_w, syn_v.swapaxes(1, 2), syn_w.swapaxes(1, 2))
    small = pl.pallas_call(
        functools.partial(kernel, lats, LMAX // order_count),
        out_shape=pltpu.VMEM((fields * 2 * own_rows, 128), jnp.float32),
        in_specs=[hbm_spec] * 6,
        out_specs=vmem_spec,
        scratch_shapes=[
            pltpu.SMEM((order_count,), jnp.int32),
            pltpu.VMEM((4 * lats, 256), jnp.bfloat16),
            pltpu.VMEM((4 * out_rows, own_rows * 128), jnp.bfloat16),
            pltpu.VMEM((fields, own_lat, length), jnp.bfloat16),
            pltpu.VMEM((2, half_pack, ana_v.shape[2]), jnp.bfloat16),
            pltpu.VMEM((2, out_rows, half_pack), jnp.bfloat16),
            pltpu.VMEM((2, 8 * out_rows, half_pack), jnp.bfloat16),
            pltpu.VMEM((128 * GROUP, 256), jnp.bfloat16),
            pltpu.VMEM((4 * lats * GROUP, 128), jnp.float32),
            [pltpu.VMEM((lats, 4 * GROUP * count, 128), jnp.bfloat16) for count in BATCHES],
            pltpu.VMEM((8 * fields, lats // 2 * own_lat), jnp.bfloat16),
            pltpu.VMEM((8 * out_rows, lats // 2 * own_lat), jnp.float32),
            pltpu.VMEM((8 * out_rows, lats // 2 * own_lat), jnp.bfloat16),
            pltpu.VMEM((8 * out_rows, lats // 2 * own_lat), jnp.bfloat16),
            pltpu.VMEM((lats, own_rows, 128), jnp.float32),
            pltpu.VMEM((2 * lats, own_rows, 128), jnp.float32),
            pltpu.VMEM((lats * own_rows, 128), jnp.float32),
            pltpu.SemaphoreType.DMA((fields,)),
            pltpu.SemaphoreType.DMA((7,)),
            pltpu.SemaphoreType.DMA,
            pltpu.SemaphoreType.DMA,
            pltpu.SemaphoreType.DMA,
            pltpu.SemaphoreType.DMA,
            pltpu.SemaphoreType.DMA,
            pltpu.SemaphoreType.DMA,
        ],
        compiler_params=pltpu.CompilerParams(
            collective_id=0, has_side_effects=True, vmem_limit_bytes=40_000_000
        ),
    )(*(pltpu.with_memory_space_constraint(x, pltpu.HBM) for x in inputs))
    repeats = NLON_OUT // lax.axis_size("rep") // 128
    spread = 4
    return pl.pallas_call(
        repeat_kernel,
        out_shape=jax.ShapeDtypeStruct((fields, 2, own_rows, repeats * 128), jnp.float32),
        in_specs=[pl.BlockSpec(memory_space=pltpu.VMEM)],
        out_specs=hbm_spec,
        scratch_shapes=[
            pltpu.VMEM((fields, 2, own_rows, repeats // spread * 128), jnp.float32),
            pltpu.SemaphoreType.DMA((spread,)),
        ],
    )(pltpu.with_memory_space_constraint(small.reshape(fields, 2, own_rows, 128), pltpu.VMEM))


def fits(mesh, near_field, assign, ana_v, syn_v):
    lats = mesh.shape["lat"]
    fields, comps, rows, length = near_field.shape
    spacing = LMAX // assign.shape[0]
    return (
        mesh.shape["rep"] == 2
        and fields == 4 * GROUP
        and lats >= 4
        and comps == 2
        and lats & (lats - 1) == 0
        and rows == 128 * lats
        and assign.shape[0] == 2 * lats
        and 128 * spacing % length == 0
        and 128 * spacing % NLON_OUT == 0
        and syn_v.shape[2] == 32
        and ana_v.shape[1] % 64 == 0
    )


def solution(mesh):
    in_specs = (
        P(None, None, "lat", None),
        P(),
        P("lat", "rep", None),
        P("lat", "rep", None),
        P("lat", "rep", None),
        P("lat", "rep", None),
    )
    out_specs = P(None, None, "lat", "rep")

    def run(near_field, assign, ana_v, ana_w, syn_v, syn_w):
        chosen = fast_body if fits(mesh, near_field, assign, ana_v, syn_v) else plain_body
        mapped = jax.shard_map(chosen, mesh=mesh, in_specs=in_specs, out_specs=out_specs, check_vma=False)
        return mapped(near_field, assign, ana_v, ana_w, syn_v, syn_w)

    return run
```

```python
import functools
import math

import jax
import jax.numpy as jnp
from jax import lax
from jax.experimental import pallas as pl
from jax.experimental.pallas import tpu as pltpu
from jax.sharding import PartitionSpec as P

LMAX = 2048
NLON_OUT = 8192


def forward_table(orders, length):
    column = jnp.arange(length, dtype=jnp.int32)
    phase_index = orders[:, None] * column[None, :] % length
    angles = phase_index.astype(jnp.float32) * (2.0 * math.pi / length)
    factor = 1.0 / math.sqrt(length)
    stacked = jnp.stack([jnp.cos(angles) * factor, -jnp.sin(angles) * factor], axis=1)
    return stacked.reshape(2 * orders.shape[0], length).astype(jnp.bfloat16)


def inverse_table(orders, begin, count, length):
    column = begin + jnp.arange(count, dtype=jnp.int32)
    phase_index = orders[:, None] * column[None, :] % length
    angles = phase_index.astype(jnp.float32) * (2.0 * math.pi / length)
    weight = jnp.where(orders == 0, 1.0, 2.0).astype(jnp.float32)[:, None] / math.sqrt(
        orders.shape[0]
    )
    stacked = jnp.stack([weight * jnp.cos(angles), -weight * jnp.sin(angles)], axis=1)
    return stacked.reshape(2 * orders.shape[0], count).astype(jnp.bfloat16)


def pad_rows(matrix, tile_count, tile_rows):
    missing = tile_count * tile_rows - matrix.shape[0]
    return jnp.pad(matrix, ((0, missing), (0, 0))).reshape(tile_count, tile_rows, matrix.shape[1])


def legendre(spectra, mat_av, mat_aw, mat_sv, mat_sw, packed_start, first_order, second_order):
    count = spectra.shape[1]
    flat = spectra.reshape(2, 4 * count, spectra.shape[3])
    tile_rows = 128
    tile_count = -(-mat_av.shape[0] // tile_rows)
    out_rows = mat_sv.shape[1]
    border = LMAX - first_order

    def step(carry, inputs_now):
        total_v, total_w = carry
        number, tile_av, tile_aw, tile_sv, tile_sw = inputs_now
        first_row = packed_start + number * tile_rows
        packed = first_row + jnp.arange(tile_rows, dtype=jnp.int32)
        second = packed >= border
        branch_kind = jnp.where(
            first_row >= border, 1, jnp.where(first_row + tile_rows - 1 < border, 0, 2)
        )

        def single_slot(slot):

            def compute():
                slot_flat = flat[slot]
                part_v = jnp.dot(tile_av, slot_flat.T, preferred_element_type=jnp.float32).reshape(
                    tile_rows, 2, count, 2
                )
                part_w = jnp.dot(tile_aw, slot_flat.T, preferred_element_type=jnp.float32).reshape(
                    tile_rows, 2, count, 2
                )
                return (part_v, part_w)

            return compute

        def both_slots():
            first_v, first_w = single_slot(0)()
            second_v, second_w = single_slot(1)()
            choose_second = second[:, None, None, None]
            return (
                jnp.where(choose_second, second_v, first_v),
                jnp.where(choose_second, second_w, first_w),
            )

        chosen_v, chosen_w = lax.switch(branch_kind, [single_slot(0), single_slot(1), both_slots])
        degree = jnp.where(second, second_order + packed - border, first_order + packed)
        sph_re = chosen_v[:, 0, :, 0] + chosen_w[:, 1, :, 1]
        sph_im = chosen_v[:, 1, :, 0] - chosen_w[:, 0, :, 1]
        tor_re = chosen_w[:, 1, :, 0] - chosen_v[:, 0, :, 1]
        tor_im = -chosen_w[:, 0, :, 0] - chosen_v[:, 1, :, 1]
        quarter = (degree + 1) % 4
        cosine = jnp.where(quarter == 0, 1.0, jnp.where(quarter == 2, -1.0, 0.0)).astype(
            jnp.float32
        )[:, None]
        sine = jnp.where(quarter == 1, -1.0, jnp.where(quarter == 3, 1.0, 0.0)).astype(jnp.float32)[
            :, None
        ]
        coeffs = jnp.stack(
            [
                cosine * sph_re - sine * sph_im,
                cosine * sph_im + sine * sph_re,
                cosine * tor_re - sine * tor_im,
                cosine * tor_im + sine * tor_re,
            ],
            axis=1,
        ).astype(jnp.bfloat16)
        flat_coeffs = coeffs.reshape(tile_rows, 4 * count)
        second_mask = second.astype(jnp.bfloat16)[:, None]

        def mixed_rows():
            lower_c = flat_coeffs * (1 - second_mask)
            upper_c = flat_coeffs * second_mask
            add_v = jnp.stack(
                [
                    jnp.dot(lower_c.T, tile_sv, preferred_element_type=jnp.float32),
                    jnp.dot(upper_c.T, tile_sv, preferred_element_type=jnp.float32),
                ]
            )
            add_w = jnp.stack(
                [
                    jnp.dot(lower_c.T, tile_sw, preferred_element_type=jnp.float32),
                    jnp.dot(upper_c.T, tile_sw, preferred_element_type=jnp.float32),
                ]
            )
            return (add_v, add_w)

        def single_rows():
            part_v = jnp.dot(flat_coeffs.T, tile_sv, preferred_element_type=jnp.float32)
            part_w = jnp.dot(flat_coeffs.T, tile_sw, preferred_element_type=jnp.float32)
            upper_pick = (branch_kind == 1).astype(jnp.float32)
            return (
                jnp.stack([part_v * (1.0 - upper_pick), part_v * upper_pick]),
                jnp.stack([part_w * (1.0 - upper_pick), part_w * upper_pick]),
            )

        add_v, add_w = lax.cond(branch_kind == 2, mixed_rows, single_rows)
        return ((total_v + add_v, total_w + add_w), None)

    start_v = jnp.zeros((2, 4 * count, out_rows), jnp.float32)
    start_w = jnp.zeros((2, 4 * count, out_rows), jnp.float32)
    numbers = jnp.arange(tile_count, dtype=jnp.int32)
    (total_v, total_w), unused = lax.scan(
        step,
        (start_v, start_w),
        (
            numbers,
            pad_rows(mat_av, tile_count, tile_rows),
            pad_rows(mat_aw, tile_count, tile_rows),
            pad_rows(mat_sv, tile_count, tile_rows),
            pad_rows(mat_sw, tile_count, tile_rows),
        ),
    )
    synth_v = total_v.reshape(2, 4, count, -1)
    synth_w = total_w.reshape(2, 4, count, -1)
    theta_re = synth_v[:, 0] - synth_w[:, 3]
    theta_im = synth_v[:, 1] + synth_w[:, 2]
    phi_re = -synth_w[:, 1] - synth_v[:, 2]
    phi_im = synth_w[:, 0] - synth_v[:, 3]
    real_part = jnp.stack([theta_re, phi_re], axis=2)
    imag_part = jnp.stack([theta_im, phi_im], axis=2)
    return jnp.stack([real_part, imag_part], axis=1).reshape(4, count, 2, -1)


def plain_body(near_field, assign, ana_v, ana_w, syn_v, syn_w):
    order_count = assign.shape[0]
    spacing = LMAX // order_count
    orders = spacing * assign
    pair_orders = lax.dynamic_slice_in_dim(orders, 2 * lax.axis_index("lat"), 2, 0)
    half_pack = ana_v.shape[1]
    packed_start = lax.axis_index("rep") * half_pack
    table = forward_table(orders, near_field.shape[3])
    spectrum = jnp.einsum(
        "jk,fctk->jfct", table, near_field, preferred_element_type=jnp.float32
    ).astype(jnp.bfloat16)
    partial_value = legendre(
        lax.all_to_all(spectrum, "lat", split_axis=0, concat_axis=3, tiled=True),
        ana_v[0],
        ana_w[0],
        syn_v[0],
        syn_w[0],
        packed_start,
        pair_orders[0],
        pair_orders[1],
    )
    summed = lax.psum(partial_value, "rep").astype(jnp.bfloat16)
    regrouped = lax.all_to_all(summed, "lat", split_axis=3, concat_axis=0, tiled=True)
    longitudes = NLON_OUT // lax.axis_size("rep")
    inverse = inverse_table(orders, lax.axis_index("rep") * longitudes, longitudes, NLON_OUT)
    return jnp.einsum("jfcr,jp->fcrp", regrouped, inverse, preferred_element_type=jnp.float32)

MESH = pl.DeviceIdType.MESH
GROUP = 4
BATCHES = (2, 1, 1)
NT = (((1,), (1,)), ((), ()))
TN = (((0,), (0,)), ((), ()))


def kernel(
    lats,
    spacing,
    assign_hbm,
    field_hbm,
    av_hbm,
    aw_hbm,
    sv_hbm,
    sw_hbm,
    out_ref,
    assign_ref,
    table_ref,
    inverse_ref,
    ring,
    ana,
    syn,
    mix,
    folded,
    staged,
    packets,
    spec,
    total,
    joined,
    theirs,
    rows_out,
    rows_in,
    rows_sum,
    field_sem,
    load_sem,
    send_sem,
    recv_sem,
    pass_send,
    pass_recv,
    row_send,
    row_recv,
):
    lat = lax.axis_index("lat")
    rep = lax.axis_index("rep")
    other = 1 - rep
    fields = field_hbm.shape[0]
    groups = fields // GROUP
    half_pack = ana.shape[1]
    span = 4 * GROUP
    near = lats // 2
    side = lat // near
    spot = lax.rem(lat, near)
    width = near * 128

    def fetch(f):
        pair = pl.ds(2 * f, 2)
        return pltpu.make_async_copy(field_hbm.at[pair, rep], ring.at[pair], field_sem.at[f])

    loads = [
        pltpu.make_async_copy(assign_hbm, assign_ref, load_sem.at[0]),
        pltpu.make_async_copy(sv_hbm.at[0], syn.at[0], load_sem.at[1]),
        pltpu.make_async_copy(sw_hbm.at[0], syn.at[1], load_sem.at[2]),
    ]
    halves = [pl.ds(pl.multiple_of(half * width, 128), width) for half in (other, rep)]
    for half in halves:
        for k, source in enumerate((av_hbm, aw_hbm)):
            loads.append(
                pltpu.make_async_copy(source.at[0, :, half], ana.at[k, :, half], load_sem.at[len(loads)])
            )
    barrier = pltpu.get_barrier_semaphore()

    def greet(i, carry):
        peer = lax.rem(lat + i, lats)
        pl.semaphore_signal(barrier, inc=1, device_id=(peer, rep), device_id_type=MESH)
        pl.semaphore_signal(barrier, inc=1, device_id=(peer, other), device_id_type=MESH)
        return carry

    pl.semaphore_signal(barrier, inc=1, device_id=(lat, other), device_id_type=MESH)
    lax.fori_loop(1, lats, greet, 0)

    loads[0].start()
    for f in range(GROUP // 2):
        fetch(f).start()

    for f in range(GROUP // 2, fields // 2):
        fetch(f).start()
    for load in loads[1:3]:
        load.start()

    loads[0].wait()
    length = field_hbm.shape[3]

    def orders_of(index):
        order = jnp.zeros(index.shape, jnp.int32)
        for k in range(2 * lats):
            order = jnp.where(index == k, spacing * assign_ref[k], order)
        return order

    shape = (4 * lats, 128)
    row = lax.broadcasted_iota(jnp.int32, shape, 0)
    phase = orders_of((row // 4) * 2 + (row & 1)) * lax.broadcasted_iota(jnp.int32, shape, 1)
    phase = lax.rem(phase + ((row // 2) & 1) * (length // 4), length)
    wave = jnp.cos(phase.astype(jnp.float32) * (2.0 * math.pi / length)) * (1.0 / math.sqrt(length))
    wave = wave.astype(jnp.bfloat16)
    table_ref[:, 0:128] = wave
    table_ref[:, 128:256] = wave

    def send(batch, peer):
        first, count = sum(BATCHES[:batch]), BATCHES[batch]
        return pltpu.make_async_remote_copy(
            src_ref=packets[batch].at[peer],
            dst_ref=spec.at[
                pl.ds(pl.multiple_of((rep * groups + first) * span, span), count * span),
                pl.ds(pl.multiple_of(spot * 128, 128), 128),
            ],
            send_sem=send_sem,
            recv_sem=recv_sem,
            device_id=(peer, side),
            device_id_type=MESH,
        )

    def bulk(blocks, send_at, recv_at):
        tall = 1
        while blocks % tall or blocks // tall * 128 > ring.shape[2]:
            tall += 1
        like = ring.at[0, pl.ds(0, tall * span), pl.ds(0, blocks // tall * 128)]
        return pltpu.make_async_remote_copy(
            src_ref=like,
            dst_ref=like,
            send_sem=send_at,
            recv_sem=recv_at,
            device_id=(lat, other),
            device_id_type=MESH,
        )

    share = pltpu.make_async_remote_copy(
        src_ref=joined,
        dst_ref=theirs,
        send_sem=pass_send,
        recv_sem=pass_recv,
        device_id=(lat, other),
        device_id_type=MESH,
    )

    def fold(pair, carry):
        fetch(pair).wait()
        for f in range(2):
            at = 2 * pair + f
            total_f = ring[at, :, 0:128].astype(jnp.float32)
            for piece in range(1, ring.shape[2] // 128):
                total_f = total_f + ring[at, :, piece * 128 : (piece + 1) * 128].astype(jnp.float32)
            high = total_f.astype(jnp.bfloat16)
            low = (total_f - high.astype(jnp.float32)).astype(jnp.bfloat16)
            begin = pl.multiple_of(lax.rem(at, GROUP) * 128, 128)
            folded[pl.ds(begin, 128), 0:128] = high
            folded[pl.ds(begin, 128), 128:256] = low
        return carry

    group = 0
    for batch, count in enumerate(BATCHES):
        for member in range(count):
            lax.fori_loop(group * GROUP // 2, (group + 1) * GROUP // 2, fold, 0)
            value = lax.dot_general(table_ref[...], folded[...], NT, preferred_element_type=jnp.float32)
            for k in range(GROUP):
                staged[pl.ds(k, 4 * lats, stride=GROUP), :] = value[:, k * 128 : (k + 1) * 128]
            packets[batch][:, member * span : (member + 1) * span, :] = (
                staged[...].astype(jnp.bfloat16).reshape(lats, span, 128)
            )
            group += 1
            if group == 3:
                loads[3].start()
                loads[4].start()
            if group == groups:
                loads[5].start()
                loads[6].start()
        if batch == 0:
            pl.semaphore_wait(barrier, 2 * lats - 1)

        def send_far(i, carry, batch=batch):
            send(batch, (1 - side) * near + lax.rem(spot + near - i, near)).start()
            return carry

        def send_near(i, carry, batch=batch):
            send(batch, side * near + lax.rem(spot + near - i, near)).start()
            return carry

        lax.fori_loop(0, near, send_far, 0)
        lax.fori_loop(1, near, send_near, 0)

        @pl.when(side == rep)
        def _(batch=batch):
            first, count = sum(BATCHES[:batch]), BATCHES[batch]
            spec[
                pl.ds(pl.multiple_of((rep * groups + first) * span, span), count * span),
                pl.ds(pl.multiple_of(spot * 128, 128), 128),
            ] = packets[batch][lat]

        @pl.when(side != rep)
        def _(batch=batch):
            send(batch, lat).start()

    first_order = spacing * assign_ref[2 * lat]
    second_order = spacing * assign_ref[2 * lat + 1]
    border = LMAX - first_order
    loads[1].wait()
    loads[2].wait()
    out_rows = syn.shape[1]
    packed = rep * half_pack + lax.broadcasted_iota(jnp.int32, (1, half_pack), 1)
    degree = jnp.where(packed >= border, second_order + packed - border, first_order + packed)
    quarter = (degree + 1) & 3
    cosine = jnp.where(quarter == 0, 1.0, jnp.where(quarter == 2, -1.0, 0.0))
    sine = jnp.where(quarter == 1, -1.0, jnp.where(quarter == 3, 1.0, 0.0))
    held = jnp.where(packed >= border, 1, 0)
    for k in range(2):
        values = syn[k].astype(jnp.float32)
        for slot_at in range(2):
            for turn, factor in enumerate((cosine, sine)):
                piece = (values * jnp.where(held == slot_at, factor, 0.0)).astype(jnp.bfloat16)
                for target in range(2):
                    begin = (((target ^ k) * 2 + slot_at) * 2 + turn) * out_rows
                    mix[target, begin : begin + out_rows, :] = piece

    loads[3].wait()
    value = jnp.dot(mix[0], ana[0, :, halves[0]], preferred_element_type=jnp.float32)
    loads[4].wait()
    value = value + jnp.dot(mix[1], ana[1, :, halves[0]], preferred_element_type=jnp.float32)
    joined[...] = value.astype(jnp.bfloat16)
    share.start()
    loads[5].wait()
    total[...] = jnp.dot(mix[0], ana[0, :, halves[1]], preferred_element_type=jnp.float32)
    loads[6].wait()
    total[...] = total[...] + jnp.dot(mix[1], ana[1, :, halves[1]], preferred_element_type=jnp.float32)

    own_rows = out_rows // lats
    shape = (out_rows, 128)
    row = lax.broadcasted_iota(jnp.int32, shape, 0)
    n = lax.broadcasted_iota(jnp.int32, shape, 1)
    for slot_at in range(2):
        order = orders_of((row // own_rows) * 2 + slot_at)
        weight = jnp.where(order == 0, 1.0, 2.0) * (1.0 / math.sqrt(2 * lats))
        for part_at in range(2):
            phase = lax.rem(order * n + part_at * (NLON_OUT // 4), NLON_OUT)
            wave = weight * jnp.cos(phase.astype(jnp.float32) * (2.0 * math.pi / NLON_OUT))
            begin = (part_at * 2 + slot_at) * out_rows
            for o in range(own_rows):
                inverse_ref[begin : begin + out_rows, o * 128 : (o + 1) * 128] = jnp.where(
                    lax.rem(row, own_rows) == o, wave, 0.0
                ).astype(jnp.bfloat16)

    share.wait_recv()
    theirs[...] = (total[...] + theirs[...].astype(jnp.float32)).astype(jnp.bfloat16)

    @pl.when(side == rep)
    def _():
        bulk(groups * (2 * near - 1), send_sem, recv_sem).wait_recv()

    @pl.when(side != rep)
    def _():
        bulk(groups * 2 * near, send_sem, recv_sem).wait_recv()

    synth = lax.dot_general(theirs[...], spec[...], NT, preferred_element_type=jnp.float32)

    lane = lax.broadcasted_iota(jnp.int32, (1, 128), 1)
    lane_slot = (lane // GROUP) & 1
    part = (lane // (2 * GROUP)) & 1
    comp = lane // 64

    def swap_part(x):
        return jnp.where(part == 0, pltpu.roll(x, 128 - 2 * GROUP, 1), pltpu.roll(x, 2 * GROUP, 1))

    def swap_comp(x):
        return pltpu.roll(x, 64, 1)

    part_sign = jnp.where(part == 0, -1.0, 1.0)
    comp_sign = jnp.where(comp == 0, 1.0, -1.0)

    def turned(kind):
        both = [synth[(kind * 2 + k) * 2 * out_rows : (kind * 2 + k + 1) * 2 * out_rows] for k in range(2)]
        value = jnp.where(lane_slot == 0, both[0], both[1])
        return value[:out_rows] + part_sign * swap_part(value[out_rows:])

    rows = turned(0) - comp_sign * part_sign * swap_comp(swap_part(turned(1)))
    rows_out[...] = rows.reshape(lats, own_rows, 128)

    quarter_lats = lats // 4

    def ranked(t):
        plane = t // quarter_lats
        plane = side * plane + (1 - side) * (3 - plane)
        return plane * quarter_lats + lax.rem(lat + t, quarter_lats)

    def row_copy(target_lat, target_rep):
        return pltpu.make_async_remote_copy(
            src_ref=rows_out.at[target_lat],
            dst_ref=rows_in.at[rep * lats + lat],
            send_sem=row_send,
            recv_sem=row_recv,
            device_id=(target_lat, target_rep),
            device_id_type=MESH,
        )

    def send_rows(i, carry):
        peer = ranked(i)
        row_copy(peer, other).start()

        @pl.when(peer != lat)
        def _():
            row_copy(peer, rep).start()

        return carry

    lax.fori_loop(0, lats, send_rows, 0)
    rows_in[rep * lats + lat] = rows_out[lat]

    share.wait_send()

    @pl.when(side == rep)
    def _():
        bulk(groups * (lats - 1), send_sem, recv_sem).wait_send()

    @pl.when(side != rep)
    def _():
        bulk(groups * lats, send_sem, recv_sem).wait_send()

    all_rows = pltpu.make_async_remote_copy(
        src_ref=rows_in.at[pl.ds(0, 2 * lats - 1)],
        dst_ref=rows_in.at[pl.ds(0, 2 * lats - 1)],
        send_sem=row_send,
        recv_sem=row_recv,
        device_id=(lat, other),
        device_id_type=MESH,
    )
    all_rows.wait_recv()

    summed = (rows_in[0:lats] + rows_in[lats : 2 * lats]).reshape(out_rows, 128)
    gathered = [summed] + [pltpu.roll(summed, 128 - k * GROUP, 1) for k in range(1, 4)]
    gathered = jnp.concatenate(gathered, axis=0).astype(jnp.bfloat16)
    value = lax.dot_general(gathered, inverse_ref[...], TN, preferred_element_type=jnp.float32)
    for block in range(2 * groups):
        comp_at, group = block // groups, block % groups
        for o in range(own_rows):
            begin = (group * GROUP * 2 + comp_at) * own_rows + o
            out_ref[pl.ds(begin, GROUP, stride=2 * own_rows), :] = value[
                block * span : block * span + GROUP, o * 128 : (o + 1) * 128
            ]
    all_rows.wait_send()


def repeat_kernel(small_ref, out_hbm, wide, sem):
    value = small_ref[...]
    width = wide.shape[3]
    for k in range(width // 128):
        wide[:, :, :, k * 128 : (k + 1) * 128] = value
    copies = [
        pltpu.make_async_copy(wide, out_hbm.at[:, :, :, k * width : (k + 1) * width], sem.at[k])
        for k in range(out_hbm.shape[3] // width)
    ]
    for copy in copies:
        copy.start()
    for copy in copies:
        copy.wait()


def fast_body(near_field, assign, ana_v, ana_w, syn_v, syn_w):
    lats = lax.axis_size("lat")
    fields, comps, own_lat, length = near_field.shape
    order_count = assign.shape[0]
    half_pack = ana_v.shape[1]
    out_rows = syn_v.shape[2]
    own_rows = out_rows // lats
    hbm_spec = pl.BlockSpec(memory_space=pltpu.HBM)
    vmem_spec = pl.BlockSpec(memory_space=pltpu.VMEM)
    inputs = (assign, near_field, ana_v, ana_w, syn_v.swapaxes(1, 2), syn_w.swapaxes(1, 2))
    small = pl.pallas_call(
        functools.partial(kernel, lats, LMAX // order_count),
        out_shape=pltpu.VMEM((fields * 2 * own_rows, 128), jnp.float32),
        in_specs=[hbm_spec] * 6,
        out_specs=vmem_spec,
        scratch_shapes=[
            pltpu.SMEM((order_count,), jnp.int32),
            pltpu.VMEM((4 * lats, 256), jnp.bfloat16),
            pltpu.VMEM((4 * out_rows, own_rows * 128), jnp.bfloat16),
            pltpu.VMEM((fields, own_lat, length), jnp.bfloat16),
            pltpu.VMEM((2, half_pack, ana_v.shape[2]), jnp.bfloat16),
            pltpu.VMEM((2, out_rows, half_pack), jnp.bfloat16),
            pltpu.VMEM((2, 8 * out_rows, half_pack), jnp.bfloat16),
            pltpu.VMEM((128 * GROUP, 256), jnp.bfloat16),
            pltpu.VMEM((4 * lats * GROUP, 128), jnp.float32),
            [pltpu.VMEM((lats, 4 * GROUP * count, 128), jnp.bfloat16) for count in BATCHES],
            pltpu.VMEM((8 * fields, lats // 2 * own_lat), jnp.bfloat16),
            pltpu.VMEM((8 * out_rows, lats // 2 * own_lat), jnp.float32),
            pltpu.VMEM((8 * out_rows, lats // 2 * own_lat), jnp.bfloat16),
            pltpu.VMEM((8 * out_rows, lats // 2 * own_lat), jnp.bfloat16),
            pltpu.VMEM((lats, own_rows, 128), jnp.float32),
            pltpu.VMEM((2 * lats, own_rows, 128), jnp.float32),
            pltpu.VMEM((lats * own_rows, 128), jnp.float32),
            pltpu.SemaphoreType.DMA((fields // 2,)),
            pltpu.SemaphoreType.DMA((7,)),
            pltpu.SemaphoreType.DMA,
            pltpu.SemaphoreType.DMA,
            pltpu.SemaphoreType.DMA,
            pltpu.SemaphoreType.DMA,
            pltpu.SemaphoreType.DMA,
            pltpu.SemaphoreType.DMA,
        ],
        compiler_params=pltpu.CompilerParams(
            collective_id=0, has_side_effects=True, vmem_limit_bytes=40_000_000
        ),
    )(*(pltpu.with_memory_space_constraint(x, pltpu.HBM) for x in inputs))
    repeats = NLON_OUT // lax.axis_size("rep") // 128
    spread = 8
    return pl.pallas_call(
        repeat_kernel,
        out_shape=jax.ShapeDtypeStruct((fields, 2, own_rows, repeats * 128), jnp.float32),
        in_specs=[pl.BlockSpec(memory_space=pltpu.VMEM)],
        out_specs=hbm_spec,
        scratch_shapes=[
            pltpu.VMEM((fields, 2, own_rows, repeats // spread * 128), jnp.float32),
            pltpu.SemaphoreType.DMA((spread,)),
        ],
    )(pltpu.with_memory_space_constraint(small.reshape(fields, 2, own_rows, 128), pltpu.VMEM))


def fits(mesh, near_field, assign, ana_v, syn_v):
    lats = mesh.shape["lat"]
    fields, comps, rows, length = near_field.shape
    spacing = LMAX // assign.shape[0]
    return (
        mesh.shape["rep"] == 2
        and fields == 4 * GROUP
        and lats >= 4
        and comps == 2
        and lats & (lats - 1) == 0
        and rows == 128 * lats
        and assign.shape[0] == 2 * lats
        and 128 * spacing % length == 0
        and 128 * spacing % NLON_OUT == 0
        and syn_v.shape[2] == 32
        and ana_v.shape[1] % 64 == 0
    )


def solution(mesh):
    in_specs = (
        P(None, None, "lat", None),
        P(),
        P("lat", "rep", None),
        P("lat", "rep", None),
        P("lat", "rep", None),
        P("lat", "rep", None),
    )
    out_specs = P(None, None, "lat", "rep")

    def run(near_field, assign, ana_v, ana_w, syn_v, syn_w):
        chosen = fast_body if fits(mesh, near_field, assign, ana_v, syn_v) else plain_body
        mapped = jax.shard_map(chosen, mesh=mesh, in_specs=in_specs, out_specs=out_specs, check_vma=False)
        return mapped(near_field, assign, ana_v, ana_w, syn_v, syn_w)

    return run
```
